32 devices in a mesh: dp: 8 (over z, x), blk: 4 (over y, core).
Axes of the slice: x: 2, y: 2, z: 4, core: 2. Of those that a mesh axis runs over, the one named last changes fastest.
Arguments:
- tokens: bfloat16 [1024, 8, 1024], P('blk', 'dp'), may hold values from -6 to 6
- cotangent: bfloat16 [1024, 8, 1024], P('blk', 'dp'), may hold values from -6 to 6
- group_ids: int32 [8], P('dp'), may hold values from 0 to 7
- group_weight: float32 [8], replicated, may hold values from 0.25 to 4
- block_order: int32 [8, 4], P('dp'), may hold values from 0 to 3, each once within a row
- w_qkv: bfloat16 [1024, 3072], P(('dp', 'blk')), may hold values from -0.1875 to 0.1875
- w_out: bfloat16 [1024, 1024], P(('dp', 'blk')), may hold values from -1.5 to 1.5
- w_up: bfloat16 [1024, 4096], P(('dp', 'blk')), may hold values from -0.1875 to 0.1875
- w_down: bfloat16 [4096, 1024], P(('dp', 'blk')), may hold values from -0.09375 to 0.09375
- norm_gain: bfloat16 [4, 1024], P(None, ('dp', 'blk')), may hold values from 0.099609375 to 1.8984375
- norm_bias: bfloat16 [4, 1024], P(None, ('dp', 'blk')), may hold values from -1.5 to 1.5
Outputs:
- out_tokens: bfloat16 [1024, 8, 1024], P('blk', 'dp')
- grad_tokens: bfloat16 [1024, 8, 1024], P('blk', 'dp')
- grad_qkv: float32 [1024, 3072], P(('dp', 'blk'))
- grad_out: float32 [1024, 1024], P(('dp', 'blk'))
- grad_up: float32 [1024, 4096], P(('dp', 'blk'))
- grad_down: float32 [4096, 1024], P(('dp', 'blk'))
- grad_gain: float32 [4, 1024], P(None, ('dp', 'blk'))
- grad_bias: float32 [4, 1024], P(None, ('dp', 'blk'))
The draws below stay inside these ranges and needn't reach their ends.
Inputs may be any that keep to these rules, and one draw needn't show every extreme that they name: For each sequence r, index b of blk holds the block of positions block_order[r, b]; each block number appears once in each row.
All inputs are finite; a program needn't handle non-finite values.
Results may differ from the reference program's by a relative error of at most 0.017.
Values may be sent and summed in bfloat16 or wider, within the bound.
No kernel may reach another device: no remote copies, remote signals or barrier semaphores. Data moves between devices by JAX's collectives and lax.ppermute only.
A program may use at most 256 MiB of HBM per device.

```python
import math
import jax
import jax.numpy as jnp
from jax import lax

D = 1024
H = 16
HD = 64
FF = 4096
BLOCK = 256
GROUPS = 8
ROWS = 8
SEQ = 1024
N_BLK = 4


def place_ends(values, own_key, least, top_value):
    place = [jax.random.randint(jax.random.fold_in(own_key, axis), (), 0, length) for axis, length in enumerate(values.shape)]
    widest = values.shape.index(max(values.shape))
    next_to = place[:widest] + [(place[widest] + 1) % values.shape[widest]] + place[widest + 1:]
    return values.at[tuple(place)].set(least).at[tuple(next_to)].set(top_value)


def block_scale(rng, shape, shards, least, largest):
    factor_of = 1.0
    for axis_at, shards_of in shards:
        heights = jax.random.uniform(jax.random.fold_in(jax.random.fold_in(rng, 6), axis_at), (shards_of,), jnp.float32, least / len(shards), largest / len(shards))
        factor_of = factor_of * jnp.repeat(jnp.exp(heights), shape[axis_at] // shards_of).reshape((-1,) + (1,) * (len(shape) - 1 - axis_at))
    return factor_of


def noise(own_key, shape, spread, most, pieces=(), held_as=jnp.bfloat16):
    level = block_scale(own_key, shape, pieces, -0.22, 0.18) if pieces else 1.0
    entries = jax.random.normal(own_key, shape, jnp.float32) * spread * level
    return jnp.minimum(jnp.maximum(entries, -most), most).astype(held_as)


def setup_inputs(seed: int = 0) -> dict:
    streams_of = jax.random.split(jax.random.key(seed), 12)
    return {
        "tokens": noise(streams_of[0], (SEQ, ROWS, D), 1.0, 6.0, ((0, 4), (1, 8))),
        "cotangent": noise(streams_of[1], (SEQ, ROWS, D), 1.0, 6.0, ((0, 4), (1, 8))),
        "group_ids": place_ends(jax.random.randint(streams_of[2], (ROWS,), 0, GROUPS), jax.random.fold_in(streams_of[2], 1), 0, GROUPS - 1).astype(jnp.int32),
        "group_weight": jnp.clip(jnp.exp(jax.random.uniform(streams_of[3], (GROUPS,), jnp.float32, math.log(0.25), math.log(4.0))), 0.25, 4.0),
        "block_order": jax.vmap(lambda own: jax.random.permutation(own, N_BLK))(jax.random.split(streams_of[4], ROWS)).reshape((ROWS, N_BLK)).astype(jnp.int32),
        "w_qkv": noise(streams_of[5], (D, 3 * D), D ** -0.5, 0.1875, ((0, 32),)),
        "w_out": noise(streams_of[6], (D, D), (D // 64) ** -0.5, 1.5, ((0, 32),)),
        "w_up": noise(streams_of[7], (D, FF), D ** -0.5, 0.1875, ((0, 32),)),
        "w_down": noise(streams_of[8], (FF, D), FF ** -0.5, 0.09375, ((0, 32),)),
        "norm_gain": jnp.clip(1.0 + 0.18 * jax.random.normal(streams_of[9], (4, D), jnp.float32), 0.099609375, 1.8984375).astype(jnp.bfloat16),
        "norm_bias": noise(streams_of[10], (4, D), 0.3, 1.5, ((1, 32),)),
    }


@jax.custom_vjp
def low(v):
    return lax.optimization_barrier(v.astype(jnp.bfloat16)).astype(jnp.float32)

@jax.custom_vjp
def low_back(v):
    return v

def low_keep(v):
    return (low(v), None)

def low_pass(kept, grad):
    return (grad,)

def back_keep(v):
    return (v, None)

def back_low(kept, grad):
    return (low(grad),)
low.defvjp(low_keep, low_pass)
low_back.defvjp(back_keep, back_low)

def layer_norm(values, gain, bias):
    average = lax.optimization_barrier(jnp.mean(values, -1, keepdims=True))
    centred = values - average
    variance = lax.optimization_barrier(jnp.mean(centred * centred, -1, keepdims=True))
    return centred * lax.rsqrt(variance + 1e-05) * gain + bias

def rotate(values, cos_table, sine_table):
    half_dim = values.shape[-1] // 2
    first_half = values[..., :half_dim]
    second_half = values[..., half_dim:]
    return jnp.concatenate([first_half * cos_table - second_half * sine_table, second_half * cos_table + first_half * sine_table], -1)

def attend(queries, key_rows, value_rows, positions):

    def one_block(block_args):
        query_block, pos_block = block_args
        raw_scores = low_back(jnp.einsum('qhd,khd->hqk', query_block, key_rows, precision=lax.Precision.HIGHEST))
        visible = positions[None, :] <= pos_block[:, None]
        scores = jnp.where(visible[None], raw_scores * 0.125, -1e+30)
        probability = low(jax.nn.softmax(scores, -1))
        return jnp.einsum('hqk,khd->qhd', probability, value_rows, precision=lax.Precision.HIGHEST)
    length = queries.shape[0]
    block_rows = min(512, length)
    num_blocks = length // block_rows
    result = lax.map(jax.checkpoint(one_block), (queries.reshape((num_blocks, block_rows) + queries.shape[1:]), positions.reshape(num_blocks, block_rows)))
    return result.reshape(queries.shape)

def forward(tokens_row, w_qkv, w_out, w_up, w_down, gains, biases, cos_table, sine_table, positions):
    length = tokens_row.shape[0]
    model_width = w_out.shape[0]
    normed = low(layer_norm(tokens_row, gains[0], biases[0]))
    project = low_back(jnp.dot(normed, w_qkv, precision=lax.Precision.HIGHEST))
    shaped = project.reshape(length, 3, H, HD)
    queries = low(rotate(shaped[:, 0], cos_table, sine_table))
    key_rows = low(rotate(shaped[:, 1], cos_table, sine_table))
    value_rows = low(shaped[:, 2])
    attended = attend(queries, key_rows, value_rows, positions).reshape(length, model_width)
    attended = low_back(low(attended))
    branch = low_back(jnp.dot(attended, w_out, precision=lax.Precision.HIGHEST))
    hidden_state = tokens_row + layer_norm(branch, gains[1], biases[1])
    second = low(layer_norm(hidden_state, gains[2], biases[2]))
    pre_act = low_back(jnp.dot(second, w_up, precision=lax.Precision.HIGHEST))
    activated = low(jax.nn.gelu(pre_act))
    mlp_out = low_back(jnp.dot(activated, w_down, precision=lax.Precision.HIGHEST))
    return hidden_state + layer_norm(mlp_out, gains[3], biases[3])

def reference(tokens, cotangent, group_ids, group_weight, block_order, w_qkv, w_out, w_up, w_down, norm_gain, norm_bias):
    weights = tuple((weight.astype(jnp.float32) for weight in (w_qkv, w_out, w_up, w_down, norm_gain, norm_bias)))
    frequency = jnp.exp(jnp.arange(HD // 2, dtype=jnp.float32) * (-2.0 * math.log(10000.0) / HD))
    group_range = jnp.arange(GROUPS, dtype=jnp.int32)

    def one_row(totals, row_inputs):
        tokens_row, cot_row, group_id, order_row = row_inputs
        positions = (order_row[:, None] * BLOCK + jnp.arange(BLOCK, dtype=jnp.int32)[None, :]).reshape(-1).astype(jnp.int32)
        angles = positions.astype(jnp.float32)[:, None] * frequency[None, :]
        cos_table = jnp.cos(angles)[:, None, :]
        sine_table = jnp.sin(angles)[:, None, :]
        row_scale = jnp.sum(jnp.where(group_range == group_id, group_weight, 0.0))

        def apply_layer(tokens_in, *params):
            return forward(tokens_in, *params, cos_table, sine_table, positions)
        result, pullback = jax.vjp(apply_layer, tokens_row.astype(jnp.float32), *weights)
        gradients = pullback(cot_row.astype(jnp.float32) * row_scale)
        totals = tuple((total + update for total, update in zip(totals, gradients[1:])))
        return (totals, (result.astype(jnp.bfloat16), gradients[0].astype(jnp.bfloat16)))
    zero_sums = tuple((jnp.zeros(weight.shape, jnp.float32) for weight in weights))
    totals, (outputs, token_grads) = lax.scan(one_row, zero_sums, (jnp.swapaxes(tokens, 0, 1), jnp.swapaxes(cotangent, 0, 1), group_ids, block_order))
    return (jnp.swapaxes(outputs, 0, 1), jnp.swapaxes(token_grads, 0, 1), totals[0], totals[1], totals[2], totals[3], totals[4], totals[5])
```

```python
import math

import jax
import jax.numpy as jnp
from jax import lax
from jax.sharding import Mesh
from jax.sharding import PartitionSpec as P

HD = 64
F32 = jnp.float32
BF16 = jnp.bfloat16


def layer_norm(values, gain, bias):
    average = jnp.mean(values, -1, keepdims=True)
    centred = values - average
    variance = jnp.mean(centred * centred, -1, keepdims=True)
    return centred * lax.rsqrt(variance + 1e-05) * gain + bias


def rotate(values, cos_table, sine_table, direction):
    half_dim = values.shape[-1] // 2
    first_half = values[..., :half_dim]
    second_half = values[..., half_dim:]
    turned = direction * sine_table
    return jnp.concatenate(
        [
            first_half * cos_table - second_half * turned,
            second_half * cos_table + first_half * turned,
        ],
        -1,
    )


def rope_tables(positions):
    frequency = jnp.exp(jnp.arange(HD // 2, dtype=F32) * (-2.0 * math.log(10000.0) / HD))
    angles = positions.astype(F32)[:, None] * frequency[None, :]
    return jnp.cos(angles), jnp.sin(angles)


def dot(a, b):
    return jnp.dot(a, b, preferred_element_type=F32)


def dot_nt(a, b):
    return lax.dot_general(a, b, (((1,), (1,)), ((), ())), preferred_element_type=F32)


def dot_tn(a, b):
    return lax.dot_general(a, b, (((0,), (0,)), ((), ())), preferred_element_type=F32)


def shift(value, axis, step=1):
    size = lax.axis_size(axis)
    return lax.ppermute(value, axis, [(i, (i + step) % size) for i in range(size)])


def source(axis, step):
    size = lax.axis_size(axis)
    return lax.rem(lax.axis_index(axis) + size - step, size)


def put(buffer, piece, at):
    return lax.dynamic_update_slice(buffer, piece[None], (at,) + (0,) * piece.ndim)


def take(array, at):
    return lax.dynamic_index_in_dim(array, at, 0, keepdims=False)


def ring_gather(piece, axis):
    pieces = [piece]
    for _ in range(lax.axis_size(axis) - 1):
        pieces.append(shift(pieces[-1], axis))
    return pieces


def direct_gather(piece, axis):
    size = lax.axis_size(axis)
    return [piece] + [shift(piece, axis, step) for step in range(1, size)]


def in_order(pieces, axis):
    buffer = jnp.zeros((len(pieces),) + pieces[0].shape, pieces[0].dtype)
    for step, piece in enumerate(pieces):
        buffer = put(buffer, piece, source(axis, step))
    return buffer


def scatter_sum(parts, axis):
    size = lax.axis_size(axis)
    total = take(parts, source(axis, 1)).astype(BF16)
    for step in range(1, size):
        arrived = shift(total, axis).astype(F32)
        total = arrived + take(parts, source(axis, step + 1)).astype(F32)
        if step < size - 1:
            total = total.astype(BF16)
    return total


def all_sum(value, axis):
    pieces = direct_gather(value, axis)
    total = pieces[0]
    for piece in pieces[1:]:
        total = total + piece
    return total


def pair(own, other, core):
    first = jnp.where(core == 0, own, other)
    second = jnp.where(core == 0, other, own)
    return jnp.stack([first, second])


def on_device(
    tokens,
    cotangent,
    group_ids,
    group_weight,
    block_order,
    w_qkv,
    w_out,
    w_up,
    w_down,
    norm_gain,
    norm_bias,
):
    nz, nx, ny, nc = (lax.axis_size(a) for a in "zxyc")
    iz, ix, iy, ic = (lax.axis_index(a) for a in "zxyc")
    rows_here, _, width = tokens.shape
    heads = width // HD
    spans = ny * nc
    mine = heads // spans
    head_width = mine * HD
    chips = nz * nx * ny
    wrows = w_qkv.shape[0]
    ffrows = w_down.shape[0]
    ff = w_up.shape[1]
    ffh = ff // nc
    owh = width // nc
    span = iy * nc + ic

    small = jnp.concatenate([norm_gain, norm_bias], 0)
    for axis in "cyxz":
        small = in_order(direct_gather(small, axis), axis)
    small = small.reshape(chips * nc, 8, wrows).transpose(1, 0, 2).reshape(8, width).astype(F32)
    gains, biases = small[:4], small[4:]

    cut = w_qkv.reshape(wrows, 3, ny, nc, head_width).transpose(3, 2, 0, 1, 4)
    other = shift(take(cut, 1 - ic), "c")
    cut = pair(take(cut, ic), other, ic)
    cut = cut.transpose(1, 0, 2, 3, 4)
    pieces = [take(cut, iy)]
    for step in range(1, ny):
        pieces.append(shift(take(cut, lax.rem(iy + step, ny)), "y", step))
    qkv_part = in_order(pieces, "y").reshape(spans * wrows, 3 * head_width)
    qkv_part = in_order(ring_gather(qkv_part, "x"), "x")
    qkv_w = in_order(ring_gather(qkv_part, "z"), "z").reshape(width, 3 * head_width)

    up_cut = w_up.reshape(wrows, chips, nc, ffrows).transpose(2, 0, 1, 3).reshape(nc, wrows, ffh)
    out_cut = w_out.reshape(wrows, nc, owh).transpose(1, 0, 2)
    wide_cut = jnp.concatenate([up_cut, out_cut], -1)
    wide = pair(take(wide_cut, ic), shift(take(wide_cut, 1 - ic), "c"), ic)
    wide = wide.reshape(nc * wrows, ffh + owh)
    wide = in_order(ring_gather(wide, "y"), "y").reshape(spans * wrows, ffh + owh)
    ring = ring_gather(wide, "z")
    buffer = jnp.zeros((nz * nx,) + wide.shape, BF16)
    for step, piece in enumerate(ring):
        for far, item in enumerate(ring_gather(piece, "x")):
            buffer = put(buffer, item, source("z", step) * nx + source("x", far))
    wide_w = buffer.reshape(width, ffh + owh)
    up_w, out_w = wide_w[:, :ffh], wide_w[:, ffh:]

    ring = ring_gather(w_down, "z")
    buffer = jnp.zeros((nz * nx * ny,) + w_down.shape, BF16)
    for step, piece in enumerate(ring):
        both = in_order(ring_gather(piece, "x"), "x")
        for far, item in enumerate(ring_gather(both, "y")):
            for ox in range(nx):
                at = (source("z", step) * nx + ox) * ny + source("y", far)
                buffer = put(buffer, item[ox], at)
    down_w = buffer.reshape(ffh, width)

    x = tokens.astype(F32).reshape(rows_here, width)
    a1_f32, pull_zero = jax.vjp(layer_norm, x, gains[0], biases[0])
    a1_own = a1_f32.astype(BF16)
    a1 = in_order(ring_gather(pair(a1_own, shift(a1_own, "c"), ic), "y"), "y")
    length = spans * rows_here
    a1 = a1.reshape(length, width)
    order = block_order[0]
    offsets = jnp.arange(rows_here, dtype=jnp.int32)
    positions = (order[:, None] * rows_here + offsets[None, :]).reshape(length)
    cos_table, sine_table = rope_tables(positions)
    cos_table, sine_table = cos_table[:, None, :], sine_table[:, None, :]

    project = dot(a1, qkv_w).reshape(length, 3, mine, HD)
    q = rotate(project[:, 0], cos_table, sine_table, 1.0).astype(BF16)
    k = rotate(project[:, 1], cos_table, sine_table, 1.0).astype(BF16)
    v = project[:, 2].astype(BF16)
    visible = (positions[None, :] <= positions[:, None])[None]
    scores = jnp.einsum("qhd,khd->hqk", q, k, preferred_element_type=F32) * 0.125
    scores = jnp.where(visible, scores, -1e30)
    row_max = jnp.max(scores, -1, keepdims=True)
    weights = jnp.exp(scores - row_max)
    row_sum = jnp.sum(weights, -1, keepdims=True)
    log_total = row_max + jnp.log(row_sum)
    p_low = (weights / row_sum).astype(BF16)
    attn = jnp.einsum("hqk,khd->qhd", p_low, v, preferred_element_type=F32)

    sent = attn.astype(BF16).reshape(ny, nc * rows_here, head_width)
    pieces = [take(sent, iy)]
    for step in range(1, ny):
        pieces.append(shift(take(sent, lax.rem(iy + step, ny)), "y", step))
    o_half = in_order(pieces, "y")
    o_chip = pair(o_half, shift(o_half, "c"), ic)
    o_chip = o_chip.transpose(2, 1, 0, 3).reshape(nc * rows_here, width)
    r_half = dot(o_chip, out_w).reshape(nc, rows_here, owh)
    r = pair(take(r_half, ic), shift(take(r_half, 1 - ic), "c"), ic)
    r = r.transpose(1, 0, 2).reshape(rows_here, width)
    r_normed, pull_one = jax.vjp(layer_norm, r, gains[1], biases[1])
    h = x + r_normed
    a2_f32, pull_two = jax.vjp(layer_norm, h, gains[2], biases[2])
    a2_own = a2_f32.astype(BF16)
    a2 = pair(a2_own, shift(a2_own, "c"), ic).reshape(nc * rows_here, width)
    z = dot(a2, up_w)
    u_f32, gelu_pull = jax.vjp(jax.nn.gelu, z)
    u = u_f32.astype(BF16)
    m_part = dot(u, down_w).reshape(nc, rows_here, width)
    m = take(m_part, ic) + shift(take(m_part, 1 - ic).astype(BF16), "c").astype(F32)
    m_normed, pull_three = jax.vjp(layer_norm, m, gains[3], biases[3])
    out_tokens = (h + m_normed).astype(BF16).reshape(tokens.shape)

    match = group_ids[:, None] == jnp.arange(group_weight.shape[0], dtype=jnp.int32)[None, :]
    scale = jnp.sum(jnp.where(match, group_weight[None, :], 0.0))
    g = cotangent.astype(F32).reshape(rows_here, width) * scale
    dm_own, gain_three, bias_three = pull_three(g)
    dm_own = dm_own.astype(BF16)
    dm = pair(dm_own, shift(dm_own, "c"), ic).reshape(nc * rows_here, width)
    grad_down = dot_tn(u, dm).astype(BF16).reshape(nz, nx, ny, ffrows, width)
    du = dot_nt(dm, down_w)
    dz = gelu_pull(du)[0].astype(BF16)
    grad_up = dot_tn(a2, dz).astype(BF16).reshape(nz, nx, ny * nc * wrows, ffh)
    da_part = dot_nt(dz, up_w).reshape(nc, rows_here, width)
    da = take(da_part, ic) + shift(take(da_part, 1 - ic).astype(BF16), "c").astype(F32)
    dh, gain_two, bias_two = pull_two(da)
    dh = dh + g
    dr_own, gain_one, bias_one = pull_one(dh)
    dr_own = dr_own.astype(BF16).reshape(rows_here, nc, owh).transpose(1, 0, 2)
    dr = pair(take(dr_own, ic), shift(take(dr_own, 1 - ic), "c"), ic)
    dr = dr.reshape(nc * rows_here, owh)
    grad_out = dot_tn(o_chip, dr).astype(BF16).reshape(nz, nx, ny * nc * wrows, owh)
    do_part = dot_nt(dr, out_w).reshape(nc * rows_here, ny, nc, head_width).transpose(2, 1, 0, 3)
    do = take(do_part, ic) + shift(take(do_part, 1 - ic).astype(BF16), "c").astype(F32)
    do = do.astype(BF16)
    pieces = [take(do, iy)]
    for step in range(1, ny):
        pieces.append(shift(take(do, lax.rem(iy + step, ny)), "y", step))
    do = in_order(pieces, "y").reshape(length, mine, HD)

    delta = jnp.sum(do.astype(F32) * attn, -1).T[:, :, None]
    prob = jnp.where(visible, jnp.exp(scores - log_total), 0.0)
    dprob = jnp.einsum("qhd,khd->hqk", do, v, preferred_element_type=F32)
    ds = (prob * (dprob - delta) * 0.125).astype(BF16)
    dv = jnp.einsum("hqk,qhd->khd", prob.astype(BF16), do, preferred_element_type=F32)
    dq = jnp.einsum("hqk,khd->qhd", ds, k, preferred_element_type=F32)
    dk = jnp.einsum("hqk,qhd->khd", ds, q, preferred_element_type=F32)
    dqkv = jnp.stack(
        [
            rotate(dq, cos_table, sine_table, -1.0),
            rotate(dk, cos_table, sine_table, -1.0),
            dv,
        ],
        1,
    )
    dqkv = dqkv.astype(BF16).reshape(length, 3 * head_width)
    da1 = dot_nt(dqkv, qkv_w).reshape(ny, nc, rows_here, width).transpose(1, 0, 2, 3)
    da1 = take(da1, ic) + shift(take(da1, 1 - ic).astype(BF16), "c").astype(F32)
    da1 = scatter_sum(da1, "y")
    grad_qkv = dot_tn(a1, dqkv).astype(BF16).reshape(nz, nx, spans * wrows, 3 * head_width)
    dx, gain_zero, bias_zero = pull_zero(da1)
    grad_tokens = (dh + dx).astype(BF16).reshape(tokens.shape)

    down = scatter_sum(grad_down.transpose(2, 0, 1, 3, 4), "y").astype(BF16)
    down = scatter_sum(down.transpose(1, 0, 2, 3), "x").astype(BF16)
    down = scatter_sum(down, "z")

    wide_grad = jnp.concatenate([grad_up, grad_out], -1)
    wide_grad = scatter_sum(wide_grad.transpose(1, 0, 2, 3), "x").astype(BF16)
    wide_grad = scatter_sum(wide_grad, "z").astype(BF16)
    wide_grad = scatter_sum(wide_grad.reshape(ny, nc * wrows, ffh + owh), "y")
    wide_grad = wide_grad.reshape(nc, wrows, ffh + owh)
    wide_grad = pair(take(wide_grad, ic), shift(take(wide_grad, 1 - ic), "c"), ic)
    up = wide_grad[..., :ffh].reshape(nc, wrows, chips, ffrows).transpose(1, 2, 0, 3)
    up = up.reshape(wrows, ff)
    out = wide_grad[..., ffh:].transpose(1, 0, 2).reshape(wrows, width)

    qkv = scatter_sum(grad_qkv, "z").astype(BF16)
    qkv = scatter_sum(qkv, "x").reshape(ny, nc * wrows, 3 * head_width)
    pieces = [take(qkv, iy)]
    for step in range(1, ny):
        pieces.append(shift(take(qkv, lax.rem(iy + step, ny)), "y", step))
    qkv = in_order(pieces, "y").reshape(ny, nc, wrows, 3 * head_width).transpose(1, 0, 2, 3)
    qkv = pair(take(qkv, ic), shift(take(qkv, 1 - ic), "c"), ic)
    qkv = qkv.reshape(nc, ny, wrows, 3, head_width).transpose(2, 3, 1, 0, 4)
    qkv = qkv.reshape(wrows, 3 * width)

    norms = jnp.stack(
        [
            gain_zero,
            gain_one,
            gain_two,
            gain_three,
            bias_zero,
            bias_one,
            bias_two,
            bias_three,
        ]
    )
    for axis in "cyxz":
        norms = all_sum(norms, axis)
    place = ((iz * nx + ix) * ny + iy) * nc + ic
    norms = lax.dynamic_slice(norms, (0, place * wrows), (8, wrows))
    return (out_tokens, grad_tokens, qkv, out, up, down, norms[:4], norms[4:])


def solution(mesh):
    fine = Mesh(
        mesh.devices.reshape(mesh.shape["dp"] // 2, 2, mesh.shape["blk"] // 2, 2),
        ("z", "x", "y", "c"),
    )
    dp, blk, every = ("z", "x"), ("y", "c"), ("z", "x", "y", "c")
    return jax.shard_map(
        on_device,
        mesh=fine,
        in_specs=(
            P(blk, dp, None),
            P(blk, dp, None),
            P(dp),
            P(),
            P(dp, None),
            P(every, None),
            P(every, None),
            P(every, None),
            P(every, None),
            P(None, every),
            P(None, every),
        ),
        out_specs=(
            P(blk, dp, None),
            P(blk, dp, None),
            P(every, None),
            P(every, None),
            P(every, None),
            P(every, None),
            P(None, every),
            P(None, every),
        ),
        check_vma=False,
    )
```

```python
import functools
import math

import jax
import jax.numpy as jnp
from jax import lax
from jax.experimental import pallas as pl
from jax.experimental.pallas import tpu as pltpu
from jax.sharding import Mesh
from jax.sharding import PartitionSpec as P

HD = 64
F32 = jnp.float32
BF16 = jnp.bfloat16


def layer_norm(values, gain, bias):
    average = jnp.mean(values, -1, keepdims=True)
    centred = values - average
    variance = jnp.mean(centred * centred, -1, keepdims=True)
    return centred * lax.rsqrt(variance + 1e-05) * gain + bias


def rotate(values, cos_table, sine_table, direction):
    half_dim = values.shape[-1] // 2
    first_half = values[..., :half_dim]
    second_half = values[..., half_dim:]
    turned = direction * sine_table
    return jnp.concatenate(
        [
            first_half * cos_table - second_half * turned,
            second_half * cos_table + first_half * turned,
        ],
        -1,
    )


def rope_tables(positions):
    frequency = jnp.exp(jnp.arange(HD // 2, dtype=F32) * (-2.0 * math.log(10000.0) / HD))
    angles = positions.astype(F32)[:, None] * frequency[None, :]
    return jnp.cos(angles), jnp.sin(angles)


def dot(a, b):
    return jnp.dot(a, b, preferred_element_type=F32)


def dot_nt(a, b):
    return lax.dot_general(a, b, (((1,), (1,)), ((), ())), preferred_element_type=F32)


def dot_tn(a, b):
    return lax.dot_general(a, b, (((0,), (0,)), ((), ())), preferred_element_type=F32)


def shift(value, axis, step=1):
    size = lax.axis_size(axis)
    return lax.ppermute(value, axis, [(i, (i + step) % size) for i in range(size)])


def after(value, *others):
    return lax.optimization_barrier((value,) + others)[0]


def back(axis, step):
    size = lax.axis_size(axis)
    return lax.rem(lax.axis_index(axis) + size - step, size)


def take(array, at, axis=0):
    return lax.dynamic_index_in_dim(array, at, axis, keepdims=False)


def direct_gather(piece, axis):
    size = lax.axis_size(axis)
    return [piece] + [shift(piece, axis, step) for step in range(1, size)]


def ring_gather(piece, axis):
    pieces = [piece]
    for _ in range(lax.axis_size(axis) - 1):
        pieces.append(shift(pieces[-1], axis))
    return pieces


def in_order(pieces, axis):
    if len(pieces) == 2:
        return pair(pieces[0], pieces[1], lax.axis_index(axis))
    buffer = jnp.zeros((len(pieces),) + pieces[0].shape, pieces[0].dtype)
    for step, piece in enumerate(pieces):
        at = (back(axis, step),) + (0,) * piece.ndim
        buffer = lax.dynamic_update_slice(buffer, piece[None], at)
    return buffer


def pair(own, other, index):
    first = jnp.where(index == 0, own, other)
    second = jnp.where(index == 0, other, own)
    return jnp.stack([first, second])


def ring_scatter(parts, axis):
    size = len(parts)
    total = parts[1].astype(BF16)
    for step in range(1, size):
        arrived = shift(total, axis).astype(F32)
        total = arrived + parts[(step + 1) % size].astype(F32)
        if step < size - 1:
            total = total.astype(BF16)
    return total


def scatter_sum(parts, axis):
    size = parts.shape[0]
    return ring_scatter([take(parts, back(axis, step)) for step in range(size)], axis)


def exchange(parts, axis):
    size = parts.shape[0]
    index = lax.axis_index(axis)
    pieces = [take(parts, index)]
    for step in range(1, size):
        pieces.append(shift(take(parts, lax.rem(index + step, size)), axis, step))
    return in_order(pieces, axis)


def all_sum(value, axis):
    pieces = direct_gather(value, axis)
    total = pieces[0]
    for piece in pieces[1:]:
        total = total + piece
    return total


IN_VMEM = pl.BlockSpec(memory_space=pltpu.VMEM)
IN_SMEM = pl.BlockSpec(memory_space=pltpu.SMEM)
ANYWHERE = pl.BlockSpec(memory_space=pl.ANY)


def call(kernel, out_shape, in_specs, scratch, flops, nbytes):
    several = isinstance(out_shape, (tuple, list))
    return pl.pallas_call(
        kernel,
        out_shape=out_shape,
        in_specs=in_specs,
        out_specs=[IN_VMEM] * len(out_shape) if several else IN_VMEM,
        scratch_shapes=scratch,
        compiler_params=pltpu.CompilerParams(vmem_limit_bytes=56 * 1024 * 1024),
        cost_estimate=pl.CostEstimate(flops=flops, bytes_accessed=nbytes, transcendentals=0),
    )


def fetch(pieces, at_ref, target, sems, first, offset=0, columns=None):
    copies = []
    for number, piece in enumerate(pieces):
        rows = piece.shape[0]
        source = piece if columns is None else piece.at[:, pl.ds(offset, columns)]
        place = pl.ds(pl.multiple_of(at_ref[number] * rows, rows), rows)
        copies.append(pltpu.make_async_copy(source, target.at[place], sems.at[first + number]))
    for copy in copies:
        copy.start()
    return copies


def wait_all(copies):
    for copy in copies:
        copy.wait()


def partner(values):
    half = HD // 2
    if values.shape[-1] == HD:
        return jnp.concatenate([values[:, half:], values[:, :half]], -1)
    lanes = values.shape[-1]
    lane = lax.broadcasted_iota(jnp.int32, values.shape, 1)
    low = lax.rem(lane, HD) < half
    return jnp.where(low, pltpu.roll(values, lanes - half, 1), pltpu.roll(values, half, 1))


def qkv_kernel(count, lanes, offset, at_ref, a_ref, cos_ref, sin_ref, *refs):
    pieces, out_ref, weight, sems = refs[:count], refs[count], refs[count + 1], refs[count + 2]
    wide = out_ref.shape[1]
    wait_all(fetch(pieces, at_ref, weight, sems, 0, offset, wide))
    third = wide // 3
    block = 256
    for start in range(0, out_ref.shape[0], block):
        rows = pl.ds(start, block)
        acc = jnp.dot(a_ref[rows, :], weight[...], preferred_element_type=F32)
        cos, sin = cos_ref[rows, :], sin_ref[rows, :]
        for part in range(3):
            for left in range(0, third, lanes):
                at = part * third + left
                values = acc[:, at : at + lanes]
                if part < 2:
                    values = values * cos + partner(values) * sin
                if part == 0:
                    values = values * 0.125
                out_ref[rows, at : at + lanes] = values.astype(BF16)


def attend_kernel(blocks, lanes, order_ref, qkv_ref, o_ref, lse_ref):
    length, third = o_ref.shape
    size = length // blocks
    per = lanes // HD
    lane = lax.broadcasted_iota(jnp.int32, (1, lanes), 1) // HD
    row = lax.broadcasted_iota(jnp.int32, (size, size), 0)
    col = lax.broadcasted_iota(jnp.int32, (size, size), 1)
    for group in range(third // lanes):
        left = group * lanes

        def one_row(i):
            at = pl.multiple_of(order_ref[i] * size, size)
            q = qkv_ref[pl.ds(at, size), left : left + lanes]
            outs, totals = [], []
            for head in range(per):
                qh = q * (lane == head).astype(BF16)

                def scores(start):
                    k = qkv_ref[pl.ds(start, size), third + left : third + left + lanes]
                    return lax.dot_general(qh, k, (((1,), (1,)), ((), ())), preferred_element_type=F32)

                def values(p, start):
                    v = qkv_ref[pl.ds(start, size), 2 * third + left : 2 * third + left + lanes]
                    return jnp.dot(p.astype(BF16), v, preferred_element_type=F32)

                s = jnp.where(col <= row, scores(at), -1e30)
                top = jnp.max(s, -1, keepdims=True)
                p = jnp.exp(s - top)
                state = (top, jnp.sum(p, -1, keepdims=True), values(p, at))

                def step(j, state):
                    top, total, acc = state
                    start = pl.multiple_of(order_ref[j] * size, size)
                    s = scores(start)
                    new = jnp.maximum(top, jnp.max(s, -1, keepdims=True))
                    factor = jnp.exp(top - new)
                    p = jnp.exp(s - new)
                    total = total * factor + jnp.sum(p, -1, keepdims=True)
                    return new, total, acc * factor + values(p, start)

                if blocks <= 4:
                    for j in range(i):
                        state = step(j, state)
                else:
                    state = lax.fori_loop(0, i, step, state)
                top, total, acc = state
                outs.append(acc / total)
                lse = jnp.broadcast_to(top + jnp.log(total), (size, 128))
                lse_ref[group * per + head, pl.ds(at, size), :] = lse
            out = outs[0]
            for head in range(1, per):
                out = jnp.where(lane == head, outs[head], out)
            o_ref[pl.ds(at, size), left : left + lanes] = out.astype(BF16)

        if blocks <= 4:
            for i in range(blocks):
                one_row(i)
        else:
            pl.loop(0, blocks)(one_row)


def attend_back_kernel(
    blocks, lanes, order_ref, qkv_ref, o_ref, do_ref, lse_ref, cos_ref, sin_ref, out_ref, dk_ref, dv_ref
):
    length, third = o_ref.shape
    size = length // blocks
    per = lanes // HD
    lane = lax.broadcasted_iota(jnp.int32, (1, lanes), 1) // HD
    row = lax.broadcasted_iota(jnp.int32, (size, size), 0)
    col = lax.broadcasted_iota(jnp.int32, (size, size), 1)
    nt = (((1,), (1,)), ((), ()))
    tn = (((0,), (0,)), ((), ()))

    def unturn(values, rows):
        return values * cos_ref[rows, :] - partner(values) * sin_ref[rows, :]

    for group in range(third // lanes):
        left = group * lanes
        dk_ref[...] = jnp.zeros_like(dk_ref)
        dv_ref[...] = jnp.zeros_like(dv_ref)

        def one_row(i):
            at = pl.multiple_of(order_ref[i] * size, size)
            rows = pl.ds(at, size)
            q = qkv_ref[rows, left : left + lanes]
            do = do_ref[rows, left : left + lanes]
            prod = do.astype(F32) * o_ref[rows, left : left + lanes].astype(F32)
            grads = []
            for head in range(per):
                own = (lane == head).astype(BF16)
                qh, doh = q * own, do * own
                delta = jnp.sum(jnp.where(lane == head, prod, 0.0), -1, keepdims=True)
                lse = lse_ref[group * per + head, rows, 0:1]

                def step(start, diagonal):
                    where = pl.ds(start, size)
                    k = qkv_ref[where, third + left : third + left + lanes]
                    v = qkv_ref[where, 2 * third + left : 2 * third + left + lanes]
                    s = lax.dot_general(qh, k, nt, preferred_element_type=F32)
                    p = jnp.exp(s - lse)
                    if diagonal:
                        p = jnp.where(col <= row, p, 0.0)
                    dp = lax.dot_general(doh, v, nt, preferred_element_type=F32)
                    ds = (p * (dp - delta)).astype(BF16)
                    dv_ref[where, :] += lax.dot_general(p.astype(BF16), doh, tn, preferred_element_type=F32)
                    dk_ref[where, :] += lax.dot_general(ds, qh, tn, preferred_element_type=F32)
                    return jnp.dot(ds, k, preferred_element_type=F32)

                dq = step(at, True)
                if blocks <= 4:
                    for j in range(i):
                        dq = dq + step(pl.multiple_of(order_ref[j] * size, size), False)
                else:
                    dq = lax.fori_loop(
                        0, i, lambda j, c: c + step(pl.multiple_of(order_ref[j] * size, size), False), dq
                    )
                grads.append(dq)
            dq = grads[0]
            for head in range(1, per):
                dq = jnp.where(lane == head, grads[head], dq)
            out_ref[rows, left : left + lanes] = unturn(dq * 0.125, rows).astype(BF16)

        if blocks <= 4:
            for i in range(blocks):
                one_row(i)
        else:
            pl.loop(0, blocks)(one_row)
        for start in range(0, length, size):
            rows = pl.ds(start, size)
            out_ref[rows, third + left : third + left + lanes] = unturn(dk_ref[rows, :], rows).astype(BF16)
            out_ref[rows, 2 * third + left : 2 * third + left + lanes] = dv_ref[rows, :].astype(BF16)


def weight_kernel(count, offset, transposed, at_ref, a_ref, *refs):
    pieces, out_ref, weight, sems = refs[:count], refs[count], refs[count + 1], refs[count + 2]
    wait_all(fetch(pieces, at_ref, weight, sems, 0, offset, weight.shape[1]))
    dims = (((1,), (1 if transposed else 0,)), ((), ()))
    block = 256
    for start in range(0, out_ref.shape[0], block):
        rows = pl.ds(start, block)
        out_ref[rows, :] = lax.dot_general(a_ref[rows, :], weight[...], dims, preferred_element_type=F32)


GELU_A = math.sqrt(2.0 / math.pi)
GELU_B = 0.044715


def mlp_kernel(ups, downs, up_at, down_at, a_ref, *refs):
    up_pieces, down_pieces = refs[:ups], refs[ups : ups + downs]
    m_ref, u_ref, slope_ref, up, down, sems = refs[ups + downs :]
    copies = fetch(up_pieces, up_at, up, sems, 0)
    later = fetch(down_pieces, down_at, down, sems, ups)
    wait_all(copies)
    rows_all, wide = u_ref.shape
    block, step = 256, min(512, wide)
    for start in range(0, rows_all, block):
        rows = pl.ds(start, block)
        for left in range(0, wide, step):
            z = jnp.dot(a_ref[rows, :], up[:, left : left + step], preferred_element_type=F32)
            square = z * z
            t = jnp.tanh(GELU_A * z * (1.0 + GELU_B * square))
            half = 0.5 * (1.0 + t)
            u_ref[rows, left : left + step] = (z * half).astype(BF16)
            slope = half + 0.5 * z * (1.0 - t * t) * (GELU_A * (1.0 + 3.0 * GELU_B * square))
            slope_ref[rows, left : left + step] = slope.astype(BF16)
    wait_all(later)
    for start in range(0, rows_all, block):
        rows = pl.ds(start, block)
        m_ref[rows, :] = jnp.dot(u_ref[rows, :], down[...], preferred_element_type=F32)


def mlp_back_kernel(ups, downs, up_at, down_at, dm_ref, slope_ref, *refs):
    up_pieces, down_pieces = refs[:ups], refs[ups : ups + downs]
    da_ref, dz_ref, up, down, sems = refs[ups + downs :]
    copies = fetch(down_pieces, down_at, down, sems, ups)
    later = fetch(up_pieces, up_at, up, sems, 0)
    wait_all(copies)
    rows_all, wide = dz_ref.shape
    block, step = 256, min(512, wide)
    nt = (((1,), (1,)), ((), ()))
    for start in range(0, rows_all, block):
        rows = pl.ds(start, block)
        for left in range(0, wide, step):
            du = lax.dot_general(dm_ref[rows, :], down[left : left + step, :], nt, preferred_element_type=F32)
            slope = slope_ref[rows, left : left + step].astype(F32)
            dz_ref[rows, left : left + step] = (du * slope).astype(BF16)
    wait_all(later)
    for start in range(0, rows_all, block):
        rows = pl.ds(start, block)
        da_ref[rows, :] = lax.dot_general(dz_ref[rows, :], up[...], nt, preferred_element_type=F32)


def on_device(
    tokens,
    cotangent,
    group_ids,
    group_weight,
    block_order,
    w_qkv,
    w_out,
    w_up,
    w_down,
    norm_gain,
    norm_bias,
):
    nz, nx, ny, nc = (lax.axis_size(a) for a in "zxyc")
    iz, ix, iy, ic = (lax.axis_index(a) for a in "zxyc")
    rows_here, _, width = tokens.shape
    heads = width // HD
    spans = ny * nc
    mine = heads // spans
    hw = mine * HD
    lanes = min(128, hw)
    chips = nz * nx * ny
    wrows = w_qkv.shape[0]
    ffrows = w_down.shape[0]
    ff = w_up.shape[1]
    ffh = ff // nc
    owh = width // nc
    dprows = spans * wrows
    length = spans * rows_here
    crow = nc * rows_here
    shaped = jax.ShapeDtypeStruct

    tok = tokens.reshape(rows_here, width)
    tok_y = ring_gather(tok, "y")
    down_x = in_order(ring_gather(w_down, "x"), "x").reshape(nx * ffrows, width)

    cut = jnp.concatenate(
        [
            w_qkv.reshape(wrows, 3, ny, nc, hw).transpose(3, 0, 2, 1, 4).reshape(nc, wrows, ny * 3 * hw),
            w_out.reshape(wrows, nc, owh).transpose(1, 0, 2),
            w_up.reshape(wrows, nz, nx, ny, nc, ffrows).transpose(4, 0, 1, 3, 2, 5).reshape(nc, wrows, ffh),
        ],
        -1,
    )
    cut = pair(take(cut, ic), shift(take(cut, 1 - ic), "c"), ic).reshape(nc * wrows, -1)
    q_cut = cut[:, : ny * 3 * hw].reshape(nc * wrows, ny, 3 * hw)
    o_cut = jnp.broadcast_to(cut[:, None, ny * 3 * hw : ny * 3 * hw + owh], (nc * wrows, ny, owh))
    up_cut = cut[:, ny * 3 * hw + owh :]
    qo = exchange(jnp.concatenate([o_cut, q_cut], -1).transpose(1, 0, 2), "y")
    qo = qo.reshape(dprows, owh + 3 * hw)

    small = jnp.concatenate([norm_gain, norm_bias], 0)
    for axis in "cyxz":
        small = in_order(direct_gather(small, axis), axis)
    small = small.reshape(chips * nc, 8, wrows).transpose(1, 0, 2).reshape(8, width).astype(F32)
    gains, biases = small[:4], small[4:]
    tok_all = []
    for item in tok_y:
        tok_all.append(item)
        tok_all.append(shift(item, "c"))

    qo_w, up_w, down_w = [], [], []
    qo_at, down_at = [], []
    for step, item in enumerate(ring_gather(qo, "z")):
        for far, piece in enumerate(ring_gather(item, "x")):
            qo_w.append(piece)
            qo_at.append(back("z", step) * nx + back("x", far))
    for item in ring_gather(up_cut, "z"):
        both = in_order(ring_gather(item, "y"), "y").reshape(dprows, ffh)
        up_w += ring_gather(both, "x")
    for step, item in enumerate(ring_gather(down_x, "z")):
        for far, piece in enumerate(ring_gather(item, "y")):
            down_w.append(piece)
            down_at.append(back("z", step) * ny + back("y", far))
    qo_at = jnp.stack(qo_at).astype(jnp.int32)
    down_at = jnp.stack(down_at).astype(jnp.int32)
    up_at = qo_at
    q_w, o_w, q_off = qo_w, qo_w, owh
    if hw % 128:
        q_w, o_w, q_off = [p[:, owh:] for p in qo_w], [p[:, :owh] for p in qo_w], 0
    nqo, nup, ndown = len(qo_w), len(up_w), len(down_w)

    def sems(count):
        return pltpu.SemaphoreType.DMA((count,))

    order = block_order[0].reshape(ny, nc)
    offsets = jnp.arange(rows_here, dtype=jnp.int32)
    places = []
    for sy in range(ny):
        for sc in range(nc):
            places.append(take(take(order, back("y", sy)), back("c", sc)))
    places = jnp.stack(places)
    ranks = jnp.arange(spans, dtype=jnp.int32)
    sorted_at = jnp.sum(jnp.where(places[None, :] == ranks[:, None], ranks[None, :], 0), -1)
    positions = (places[:, None] * rows_here + offsets[None, :]).reshape(length)
    cos_table, sine_table = rope_tables(positions)
    repeats = lanes // HD
    cos_lanes = jnp.tile(jnp.concatenate([cos_table, cos_table], -1), (1, repeats))
    sin_lanes = jnp.tile(jnp.concatenate([-sine_table, sine_table], -1), (1, repeats))
    x = tok.astype(F32)
    a1 = layer_norm(jnp.concatenate(tok_all, 0).astype(F32), gains[0], biases[0]).astype(BF16)

    qkv = call(
        functools.partial(qkv_kernel, nqo, lanes, q_off),
        shaped((length, 3 * hw), BF16),
        [IN_SMEM, IN_VMEM, IN_VMEM, IN_VMEM] + [ANYWHERE] * nqo,
        [pltpu.VMEM((width, 3 * hw), BF16), sems(nqo)],
        2 * length * width * 3 * hw,
        2 * (length * width + width * 3 * hw + length * 3 * hw),
    )(qo_at, a1, cos_lanes, sin_lanes, *q_w)
    attn, lse = call(
        functools.partial(attend_kernel, spans, lanes),
        (shaped((length, hw), BF16), shaped((mine, length, 128), F32)),
        [IN_SMEM, IN_VMEM],
        [],
        8 * length * length * hw,
        8 * length * hw,
    )(sorted_at, qkv)

    sent = attn.reshape(ny, nc, rows_here, hw)
    got = [sent[0]]
    for sy in range(1, ny):
        got.append(shift(sent[sy], "y", ny - sy))
    if ny == 2:
        o_y = pair(got[0], got[1], iy)
    else:
        o_y = jnp.zeros((ny,) + got[0].shape, BF16)
        for sy, item in enumerate(got):
            at = lax.rem(iy + sy, ny)
            o_y = lax.dynamic_update_slice(o_y, item[None], (at, 0, 0, 0))
    o_far = shift(o_y, "c")
    near = pair(o_y[:, 0], o_y[:, 1], ic)
    far = pair(o_far[:, 1], o_far[:, 0], ic)
    o_chip = pair(near, far, ic)
    o_chip = o_chip.transpose(1, 3, 2, 0, 4).reshape(crow, width)
    r_half = call(
        functools.partial(weight_kernel, nqo, 0, False),
        shaped((crow, owh), F32),
        [IN_SMEM, IN_VMEM] + [ANYWHERE] * nqo,
        [pltpu.VMEM((width, owh), BF16), sems(nqo)],
        2 * crow * width * owh,
        2 * (crow * width + width * owh + 2 * crow * owh),
    )(qo_at, o_chip, *o_w).reshape(nc, rows_here, owh)
    r = pair(take(r_half, ic), shift(take(r_half, 1 - ic), "c"), ic)
    r = r.transpose(1, 0, 2).reshape(rows_here, width)
    r_normed, pull_one = jax.vjp(layer_norm, r, gains[1], biases[1])
    h = x + r_normed
    a2_f32, pull_two = jax.vjp(layer_norm, h, gains[2], biases[2])
    a2_own = a2_f32.astype(BF16)
    a2 = pair(a2_own, shift(a2_own, "c"), ic).reshape(crow, width)
    m_part, u, slope = call(
        functools.partial(mlp_kernel, nup, ndown),
        (shaped((crow, width), F32), shaped((crow, ffh), BF16), shaped((crow, ffh), BF16)),
        [IN_SMEM, IN_SMEM, IN_VMEM] + [ANYWHERE] * (nup + ndown),
        [pltpu.VMEM((width, ffh), BF16), pltpu.VMEM((ffh, width), BF16), sems(nup + ndown)],
        4 * crow * width * ffh,
        4 * width * ffh + 8 * crow * width,
    )(up_at, down_at, a2, *up_w, *down_w)
    m_part = m_part.reshape(nc, rows_here, width)
    m = take(m_part, ic) + shift(take(m_part, 1 - ic).astype(BF16), "c").astype(F32)
    m_normed, pull_three = jax.vjp(layer_norm, m, gains[3], biases[3])
    out_tokens = (h + m_normed).astype(BF16).reshape(tokens.shape)

    match = group_ids[:, None] == jnp.arange(group_weight.shape[0], dtype=jnp.int32)[None, :]
    scale = jnp.sum(jnp.where(match, group_weight[None, :], 0.0))
    g = cotangent.astype(F32).reshape(rows_here, width) * scale
    dm_own, gain_three, bias_three = pull_three(g)
    dm_own = dm_own.astype(BF16)
    dm = pair(dm_own, shift(dm_own, "c"), ic).reshape(crow, width)
    grad_down = dot_tn(u, dm).astype(BF16).reshape(nz, ny, nx * ffrows, width)
    dm_next = after(dm, grad_down)
    da_part, dz = call(
        functools.partial(mlp_back_kernel, nup, ndown),
        (shaped((crow, width), F32), shaped((crow, ffh), BF16)),
        [IN_SMEM, IN_SMEM, IN_VMEM, IN_VMEM] + [ANYWHERE] * (nup + ndown),
        [pltpu.VMEM((width, ffh), BF16), pltpu.VMEM((ffh, width), BF16), sems(nup + ndown)],
        4 * crow * width * ffh,
        4 * width * ffh + 8 * crow * width,
    )(up_at, down_at, dm_next, slope, *up_w, *down_w)
    da_part = da_part.reshape(nc, rows_here, width)
    da = take(da_part, ic) + shift(take(da_part, 1 - ic).astype(BF16), "c").astype(F32)
    grad_up = dot_tn(a2, dz).astype(BF16).reshape(nz, nx, ny, nc * wrows, ffh)
    da = after(da, grad_up)
    dh, gain_two, bias_two = pull_two(da)
    dh = dh + g
    dr_own, gain_one, bias_one = pull_one(dh)
    dr_own = dr_own.astype(BF16).reshape(rows_here, nc, owh).transpose(1, 0, 2)
    dr = pair(take(dr_own, ic), shift(take(dr_own, 1 - ic), "c"), ic)
    dr = dr.reshape(crow, owh)
    do_part = call(
        functools.partial(weight_kernel, nqo, 0, True),
        shaped((crow, width), F32),
        [IN_SMEM, IN_VMEM] + [ANYWHERE] * nqo,
        [pltpu.VMEM((width, owh), BF16), sems(nqo)],
        2 * crow * width * owh,
        2 * (crow * width + width * owh + 2 * crow * owh),
    )(qo_at, dr, *o_w)
    do_part = do_part.reshape(nc, rows_here, ny, nc, hw).transpose(3, 2, 0, 1, 4)
    do = take(do_part, ic) + shift(take(do_part, 1 - ic).astype(BF16), "c").astype(F32)
    do = do.astype(BF16)
    parts = []
    for sy in range(ny):
        item = take(do, lax.rem(iy + sy, ny))
        item = item if sy == 0 else shift(item, "y", sy)
        parts += [take(item, back("c", sc)) for sc in range(nc)]
    do_all = jnp.concatenate(parts, 0)
    grad_out = dot_tn(o_chip, dr).astype(BF16).reshape(nz, nx, ny, nc * wrows, owh)

    dqkv = call(
        functools.partial(attend_back_kernel, spans, lanes),
        shaped((length, 3 * hw), BF16),
        [IN_SMEM] + [IN_VMEM] * 6,
        [pltpu.VMEM((length, lanes), F32)] * 2,
        20 * length * length * hw,
        16 * length * hw,
    )(sorted_at, qkv, attn, do_all, lse, cos_lanes, sin_lanes)
    da1 = call(
        functools.partial(weight_kernel, nqo, q_off, True),
        shaped((length, width), F32),
        [IN_SMEM, IN_VMEM] + [ANYWHERE] * nqo,
        [pltpu.VMEM((width, 3 * hw), BF16), sems(nqo)],
        2 * length * width * 3 * hw,
        2 * (length * width * 2 + width * 3 * hw + length * 3 * hw),
    )(qo_at, dqkv, *q_w).reshape(ny, nc, rows_here, width)
    near = da1[:, 0] + shift(da1[:, 1].astype(BF16), "c").astype(F32)
    da1_own = near[0]
    for sy in range(1, ny):
        da1_own = da1_own + shift(near[sy].astype(BF16), "y", ny - sy).astype(F32)
    grad_qkv = dot_tn(a1, dqkv).astype(BF16).reshape(nz, nx, dprows, 3 * hw)
    _, pull_zero = jax.vjp(layer_norm, x, gains[0], biases[0])
    dx, gain_zero, bias_zero = pull_zero(da1_own)
    grad_tokens = (dh + dx).astype(BF16).reshape(tokens.shape)

    sums = []
    for step in range(nz):
        part = take(grad_down, back("z", step))
        sums.append(scatter_sum(part, "y").astype(BF16))
    down = ring_scatter(sums, "z").astype(BF16)
    down = scatter_sum(down.reshape(nx, ffrows, width), "x")

    sums = []
    for step in range(nz):
        part = scatter_sum(take(grad_up, back("z", step)), "x").astype(BF16)
        sums.append(scatter_sum(part, "y").astype(BF16))
    up = ring_scatter(sums, "z").reshape(nc, wrows, ffh)
    up = pair(take(up, ic), shift(take(up, 1 - ic), "c"), ic)
    up = up.reshape(nc, wrows, nz, ny, nx, ffrows).transpose(1, 2, 4, 3, 0, 5).reshape(wrows, ff)

    out = scatter_sum(grad_out.transpose(1, 0, 2, 3, 4), "x").astype(BF16)
    out = out.reshape(nz, dprows, owh)
    qkv_g = scatter_sum(grad_qkv.transpose(1, 0, 2, 3), "x").astype(BF16)
    both = scatter_sum(jnp.concatenate([out, qkv_g], -1), "z").astype(BF16)
    out, qkv_g = both[:, :owh], both[:, owh:]
    out = scatter_sum(out.reshape(ny, nc * wrows, owh), "y").reshape(nc, wrows, owh)
    out = pair(take(out, ic), shift(take(out, 1 - ic), "c"), ic)
    out = out.transpose(1, 0, 2).reshape(wrows, width)
    qkv_g = exchange(qkv_g.reshape(ny, nc * wrows, 3 * hw), "y")
    qkv_g = qkv_g.reshape(ny, nc, wrows, 3 * hw).transpose(1, 0, 2, 3)
    qkv_g = pair(take(qkv_g, ic), shift(take(qkv_g, 1 - ic), "c"), ic)
    qkv_g = qkv_g.reshape(nc, ny, wrows, 3, hw).transpose(2, 3, 1, 0, 4)
    qkv_g = qkv_g.reshape(wrows, 3 * width).astype(F32)

    norms = jnp.stack(
        [
            gain_zero,
            gain_one,
            gain_two,
            gain_three,
            bias_zero,
            bias_one,
            bias_two,
            bias_three,
        ]
    )
    for axis in "cyxz":
        norms = all_sum(norms, axis)
    place = ((iz * nx + ix) * ny + iy) * nc + ic
    norms = lax.dynamic_slice(norms, (0, place * wrows), (8, wrows))
    return (out_tokens, grad_tokens, qkv_g, out, up, down, norms[:4], norms[4:])


def solution(mesh):
    fine = Mesh(
        mesh.devices.reshape(mesh.shape["dp"] // 2, 2, mesh.shape["blk"] // 2, 2),
        ("z", "x", "y", "c"),
    )
    dp, blk, every = ("z", "x"), ("y", "c"), ("z", "x", "y", "c")
    return jax.shard_map(
        on_device,
        mesh=fine,
        in_specs=(
            P(blk, dp, None),
            P(blk, dp, None),
            P(dp),
            P(),
            P(dp, None),
            P(every, None),
            P(every, None),
            P(every, None),
            P(every, None),
            P(None, every),
            P(None, every),
        ),
        out_specs=(
            P(blk, dp, None),
            P(blk, dp, None),
            P(every, None),
            P(every, None),
            P(every, None),
            P(every, None),
            P(None, every),
            P(None, every),
        ),
        check_vma=False,
    )
```

```python
import functools
import math

import jax
import jax.numpy as jnp
from jax import lax
from jax.experimental import pallas as pl
from jax.experimental.pallas import tpu as pltpu
from jax.sharding import Mesh
from jax.sharding import PartitionSpec as P

HD = 64
F32 = jnp.float32
BF16 = jnp.bfloat16


def shift(value, axis, step=1):
    size = lax.axis_size(axis)
    return lax.ppermute(value, axis, [(i, (i + step) % size) for i in range(size)])


def after(value, *others):
    return lax.optimization_barrier((value,) + others)[0]


def back(axis, step):
    size = lax.axis_size(axis)
    return lax.rem(lax.axis_index(axis) + size - step, size)


def take(array, at, axis=0):
    return lax.dynamic_index_in_dim(array, at, axis, keepdims=False)


def direct_gather(piece, axis):
    size = lax.axis_size(axis)
    return [piece] + [shift(piece, axis, step) for step in range(1, size)]


def ring_gather(piece, axis):
    size = lax.axis_size(axis)
    pieces = [piece] * size
    for step in range(1, size // 2 + 1):
        pieces[step] = shift(pieces[step - 1], axis)
    for step in range(size - 1, size // 2, -1):
        pieces[step] = shift(pieces[(step + 1) % size], axis, -1)
    return pieces


def in_order(pieces, axis):
    if len(pieces) == 2:
        return pair(pieces[0], pieces[1], lax.axis_index(axis))
    buffer = jnp.zeros((len(pieces),) + pieces[0].shape, pieces[0].dtype)
    for step, piece in enumerate(pieces):
        at = (back(axis, step),) + (0,) * piece.ndim
        buffer = lax.dynamic_update_slice(buffer, piece[None], at)
    return buffer


def pair(own, other, index):
    first = jnp.where(index == 0, own, other)
    second = jnp.where(index == 0, other, own)
    return jnp.stack([first, second])


def ring_first(parts, axis):
    size = len(parts)
    half = size // 2
    found = [shift(parts[half].astype(BF16), axis)]
    if size - 1 - half:
        found.append(shift(parts[size - 1 - half].astype(BF16), axis, -1))
    return found


def ring_rest(parts, arrived, axis):
    size = len(parts)
    half = size // 2
    total = parts[0].astype(F32)
    for carry, count, way in zip(arrived, (half, size - 1 - half), (1, -1)):
        for far in range(count - 1, 0, -1):
            part = parts[size - far if way == 1 else far]
            carry = shift((carry.astype(F32) + part.astype(F32)).astype(BF16), axis, way)
        total = total + carry.astype(F32)
    return total


def ring_scatter(parts, axis):
    return ring_rest(parts, ring_first(parts, axis), axis)


def scatter_sum(parts, axis):
    size = parts.shape[0]
    return ring_scatter([take(parts, back(axis, step)) for step in range(size)], axis)


def late_last(size):
    half = size // 2
    steps = list(range(half, 0, -1)) + list(range(half + 1, size)) + [0]
    return list(dict.fromkeys(steps))


def send_parts(parts, axis):
    size = parts.shape[0]
    got = [shift(take(parts, back(axis, step)), axis, size - step) for step in range(1, size)]
    return take(parts, lax.axis_index(axis)), got


def add_parts(own, got, when):
    total = own.astype(F32)
    for item in got:
        total = total + after(item, when).astype(F32)
    return total.astype(BF16)


def exchange(parts, axis):
    size = parts.shape[0]
    index = lax.axis_index(axis)
    pieces = [take(parts, index)]
    for step in range(1, size):
        pieces.append(shift(take(parts, lax.rem(index + step, size)), axis, step))
    return in_order(pieces, axis)


def all_sum(value, axis):
    pieces = direct_gather(value, axis)
    total = pieces[0]
    for piece in pieces[1:]:
        total = total + piece
    return total


IN_VMEM = pl.BlockSpec(memory_space=pltpu.VMEM)
IN_SMEM = pl.BlockSpec(memory_space=pltpu.SMEM)
ANYWHERE = pl.BlockSpec(memory_space=pl.ANY)


def call(kernel, out_shape, in_specs, scratch=()):
    several = isinstance(out_shape, (tuple, list))
    return pl.pallas_call(
        kernel,
        out_shape=out_shape,
        in_specs=in_specs,
        out_specs=[IN_VMEM] * len(out_shape) if several else IN_VMEM,
        scratch_shapes=list(scratch),
        compiler_params=pltpu.CompilerParams(vmem_limit_bytes=56 * 1024 * 1024),
        cost_estimate=pl.CostEstimate(flops=1024, bytes_accessed=1024, transcendentals=0),
    )


def fetch(pieces, at_ref, target, sems, first, offset=0, columns=None):
    copies = []
    for number, piece in enumerate(pieces):
        rows = piece.shape[0]
        source = piece if columns is None else piece.at[:, pl.ds(offset, columns)]
        place = pl.ds(pl.multiple_of(at_ref[number] * rows, rows), rows)
        copies.append(pltpu.make_async_copy(source, target.at[place], sems.at[first + number]))
    for copy in copies:
        copy.start()
    return copies


def wait_all(copies):
    for copy in copies:
        copy.wait()


def partner(values):
    half = HD // 2
    if values.shape[-1] == HD:
        return jnp.concatenate([values[:, half:], values[:, :half]], -1)
    lanes = values.shape[-1]
    lane = lax.broadcasted_iota(jnp.int32, values.shape, 1)
    low = lax.rem(lane, HD) < half
    return jnp.where(low, pltpu.roll(values, lanes - half, 1), pltpu.roll(values, half, 1))


def attend_kernel(blocks, lanes, order_ref, qkv_ref, o_ref, lse_ref):
    length, third = o_ref.shape
    size = length // blocks
    per = lanes // HD
    lane = lax.broadcasted_iota(jnp.int32, (1, lanes), 1) // HD
    row = lax.broadcasted_iota(jnp.int32, (size, size), 0)
    col = lax.broadcasted_iota(jnp.int32, (size, size), 1)
    for group in range(third // lanes):
        left = group * lanes

        def one_row(i):
            at = pl.multiple_of(order_ref[i] * size, size)
            q = qkv_ref[pl.ds(at, size), left : left + lanes]
            outs, totals = [], []
            for head in range(per):
                qh = q * (lane == head).astype(BF16)

                def scores(start):
                    k = qkv_ref[pl.ds(start, size), third + left : third + left + lanes]
                    return lax.dot_general(qh, k, (((1,), (1,)), ((), ())), preferred_element_type=F32)

                def values(p, start):
                    v = qkv_ref[pl.ds(start, size), 2 * third + left : 2 * third + left + lanes]
                    return jnp.dot(p.astype(BF16), v, preferred_element_type=F32)

                s = jnp.where(col <= row, scores(at), -1e30)
                top = jnp.max(s, -1, keepdims=True)
                p = jnp.exp(s - top)
                state = (top, jnp.sum(p, -1, keepdims=True), values(p, at))

                def step(j, state):
                    top, total, acc = state
                    start = pl.multiple_of(order_ref[j] * size, size)
                    s = scores(start)
                    new = jnp.maximum(top, jnp.max(s, -1, keepdims=True))
                    factor = jnp.exp(top - new)
                    p = jnp.exp(s - new)
                    total = total * factor + jnp.sum(p, -1, keepdims=True)
                    return new, total, acc * factor + values(p, start)

                if blocks <= 4:
                    for j in range(i):
                        state = step(j, state)
                else:
                    state = lax.fori_loop(0, i, step, state)
                top, total, acc = state
                outs.append(acc / total)
                lse = jnp.broadcast_to(top + jnp.log(total), (size, 128))
                lse_ref[group * per + head, pl.ds(at, size), :] = lse
            out = outs[0]
            for head in range(1, per):
                out = jnp.where(lane == head, outs[head], out)
            o_ref[pl.ds(at, size), left : left + lanes] = out.astype(BF16)

        if blocks <= 4:
            for i in range(blocks):
                one_row(i)
        else:
            pl.loop(0, blocks)(one_row)


def attend_back_kernel(
    blocks, lanes, order_ref, qkv_ref, o_ref, do_ref, lse_ref, cos_ref, sin_ref, out_ref, dk_ref, dv_ref
):
    length, third = o_ref.shape
    size = length // blocks
    per = lanes // HD
    lane = lax.broadcasted_iota(jnp.int32, (1, lanes), 1) // HD
    row = lax.broadcasted_iota(jnp.int32, (size, size), 0)
    col = lax.broadcasted_iota(jnp.int32, (size, size), 1)
    nt = (((1,), (1,)), ((), ()))
    tn = (((0,), (0,)), ((), ()))

    def unturn(values, rows):
        return values * cos_ref[rows, :] - partner(values) * sin_ref[rows, :]

    for group in range(third // lanes):
        left = group * lanes
        dk_ref[...] = jnp.zeros_like(dk_ref)
        dv_ref[...] = jnp.zeros_like(dv_ref)

        def one_row(i):
            at = pl.multiple_of(order_ref[i] * size, size)
            rows = pl.ds(at, size)
            q = qkv_ref[rows, left : left + lanes]
            do = do_ref[rows, left : left + lanes]
            prod = do.astype(F32) * o_ref[rows, left : left + lanes].astype(F32)
            grads = []
            for head in range(per):
                own = (lane == head).astype(BF16)
                qh, doh = q * own, do * own
                delta = jnp.sum(jnp.where(lane == head, prod, 0.0), -1, keepdims=True)
                lse = lse_ref[group * per + head, rows, 0:1]

                def step(start, diagonal):
                    where = pl.ds(start, size)
                    k = qkv_ref[where, third + left : third + left + lanes]
                    v = qkv_ref[where, 2 * third + left : 2 * third + left + lanes]
                    s = lax.dot_general(qh, k, nt, preferred_element_type=F32)
                    p = jnp.exp(s - lse)
                    if diagonal:
                        p = jnp.where(col <= row, p, 0.0)
                    dp = lax.dot_general(doh, v, nt, preferred_element_type=F32)
                    ds = (p * (dp - delta)).astype(BF16)
                    dv_ref[where, :] += lax.dot_general(p.astype(BF16), doh, tn, preferred_element_type=F32)
                    dk_ref[where, :] += lax.dot_general(ds, qh, tn, preferred_element_type=F32)
                    return jnp.dot(ds, k, preferred_element_type=F32)

                dq = step(at, True)
                if blocks <= 4:
                    for j in range(i):
                        dq = dq + step(pl.multiple_of(order_ref[j] * size, size), False)
                else:
                    dq = lax.fori_loop(
                        0, i, lambda j, c: c + step(pl.multiple_of(order_ref[j] * size, size), False), dq
                    )
                grads.append(dq)
            dq = grads[0]
            for head in range(1, per):
                dq = jnp.where(lane == head, grads[head], dq)
            out_ref[rows, left : left + lanes] = unturn(dq * 0.125, rows).astype(BF16)

        if blocks <= 4:
            for i in range(blocks):
                one_row(i)
        else:
            pl.loop(0, blocks)(one_row)
        for start in range(0, length, size):
            rows = pl.ds(start, size)
            out_ref[rows, third + left : third + left + lanes] = unturn(dk_ref[rows, :], rows).astype(BF16)
            out_ref[rows, 2 * third + left : 2 * third + left + lanes] = dv_ref[rows, :].astype(BF16)


GELU_A = math.sqrt(2.0 / math.pi)
GELU_B = 0.044715


NT = (((1,), (1,)), ((), ()))
TN = (((0,), (0,)), ((), ()))


def normed(values):
    centred = values - jnp.mean(values, -1, keepdims=True)
    scale = lax.rsqrt(jnp.mean(centred * centred, -1, keepdims=True) + 1e-05)
    return centred * scale, scale


def normed_back(grad, gain, vhat, scale):
    scaled = grad * gain
    return scale * (
        scaled - jnp.mean(scaled, -1, keepdims=True) - vhat * jnp.mean(scaled * vhat, -1, keepdims=True)
    )


def column_sum(values):
    return jnp.sum(values, 0, keepdims=True)


def halves(core_ref, width):
    own = pl.ds(pl.multiple_of(core_ref[0] * width, width), width)
    other = pl.ds(pl.multiple_of((1 - core_ref[0]) * width, width), width)
    return own, other


def input_kernel(count, blocks, lanes, q_off, n_off, at_ref, cos_ref, sin_ref, *refs):
    toks, refs = refs[:blocks], refs[blocks:]
    q_pieces, n_pieces, refs = refs[:count], refs[count : 2 * count], refs[2 * count :]
    a_ref, out_ref, norm_ref, weight, columns, sems = refs
    wide = out_ref.shape[1]
    first = fetch(n_pieces, at_ref, columns, sems, 0, n_off, 128)
    later = fetch(q_pieces, at_ref, weight, sems, count, q_off, wide)
    wait_all(first)
    norm_ref[...] = jnp.transpose(columns[...].astype(F32))[:8, :]
    gain, bias = norm_ref[0:1, :], norm_ref[4:5, :]
    rows_here = toks[0].shape[0]
    for number, tok_ref in enumerate(toks):
        vhat, _ = normed(tok_ref[...].astype(F32))
        a_ref[pl.ds(number * rows_here, rows_here), :] = (vhat * gain + bias).astype(BF16)
    wait_all(later)
    third = wide // 3
    block = 256
    for start in range(0, out_ref.shape[0], block):
        rows = pl.ds(start, block)
        acc = jnp.dot(a_ref[rows, :], weight[...], preferred_element_type=F32)
        cos, sin = cos_ref[rows, :], sin_ref[rows, :]
        for part in range(3):
            for left in range(0, third, lanes):
                at = part * third + left
                values = acc[:, at : at + lanes]
                if part < 2:
                    values = values * cos + partner(values) * sin
                if part == 0:
                    values = values * 0.125
                out_ref[rows, at : at + lanes] = values.astype(BF16)


def out_kernel(count, ny, at_ref, core_ref, *refs):
    near, far, refs = refs[:ny], refs[ny : 2 * ny], refs[2 * ny :]
    y_ref, pieces, refs = refs[0], refs[1 : 1 + count], refs[1 + count :]
    keep_ref, send_ref, chip_ref, weight, sems = refs
    copies = fetch(pieces, at_ref, weight, sems, 0, 0, weight.shape[1])
    core = core_ref[0]
    rows, hw = near[0].shape[1], near[0].shape[2]
    for parts, is_far in ((near, False), (far, True)):
        other = 1 - core if is_far else core
        for ahead in range(ny):
            yh = lax.rem(y_ref[0] + ahead, ny)
            for sc in range(2):
                token = pl.ds(((1 - sc) if is_far else sc) * rows, rows)
                value = parts[ahead][sc]
                if hw % 128 == 0:
                    left = pl.multiple_of((yh * 2 + other) * hw, hw)
                    chip_ref[token, pl.ds(left, hw)] = value
                else:
                    for place in range(2 * ny):

                        @pl.when(yh * 2 + other == place)
                        def _(place=place, value=value, token=token):
                            chip_ref[token, place * hw : place * hw + hw] = value

    wait_all(copies)
    send_ref[...] = jnp.dot(chip_ref[rows:, :], weight[...], preferred_element_type=F32)
    keep_ref[...] = jnp.dot(chip_ref[:rows, :], weight[...], preferred_element_type=F32)


def middle_kernel(core_ref, keep_ref, got_ref, tok_ref, norm_ref, h_ref, a_ref, r_ref):
    own, other = halves(core_ref, keep_ref.shape[1])
    r_ref[:, own] = keep_ref[...]
    r_ref[:, other] = got_ref[...]
    vhat, _ = normed(r_ref[...])
    h = tok_ref[...].astype(F32) + vhat * norm_ref[1:2, :] + norm_ref[5:6, :]
    h_ref[...] = h
    vhat, _ = normed(h)
    a_ref[...] = (vhat * norm_ref[2:3, :] + norm_ref[6:7, :]).astype(BF16)


def mlp_kernel(ups, downs, up_at, down_at, own_ref, got_ref, *refs):
    up_pieces, down_pieces = refs[:ups], refs[ups : ups + downs]
    keep_ref, send_ref, u_ref, slope_ref, up, down, sems = refs[ups + downs :]
    copies = fetch(up_pieces, up_at, up, sems, 0)
    later = fetch(down_pieces, down_at, down, sems, ups)
    wait_all(copies)
    count, wide = own_ref.shape[0], u_ref.shape[1]
    step = min(512, wide)
    for start, a_ref in ((count, got_ref), (0, own_ref)):
        rows = pl.ds(start, count)
        for left in range(0, wide, step):
            z = jnp.dot(a_ref[...], up[:, left : left + step], preferred_element_type=F32)
            square = z * z
            t = jnp.tanh(GELU_A * z * (1.0 + GELU_B * square))
            half = 0.5 * (1.0 + t)
            u_ref[rows, left : left + step] = (z * half).astype(BF16)
            slope = half + 0.5 * z * (1.0 - t * t) * (GELU_A * (1.0 + 3.0 * GELU_B * square))
            slope_ref[rows, left : left + step] = slope.astype(BF16)
    wait_all(later)
    send_ref[...] = jnp.dot(u_ref[count:, :], down[...], preferred_element_type=F32).astype(BF16)
    keep_ref[...] = jnp.dot(u_ref[:count, :], down[...], preferred_element_type=F32)


def top_kernel(scale_ref, keep_ref, got_ref, h_ref, cot_ref, norm_ref, out_ref, dm_ref, grad_ref):
    vhat, scale = normed(keep_ref[...] + got_ref[...].astype(F32))
    gain = norm_ref[3:4, :]
    out_ref[...] = (h_ref[...] + vhat * gain + norm_ref[7:8, :]).astype(BF16)
    g = cot_ref[...].astype(F32) * scale_ref[0]
    dm_ref[...] = normed_back(g, gain, vhat, scale).astype(BF16)
    grad_ref[0:1, :] = column_sum(g * vhat)
    grad_ref[1:2, :] = column_sum(g)


def mlp_back_kernel(ups, downs, up_at, down_at, own_ref, got_ref, slope_ref, *refs):
    up_pieces, down_pieces = refs[:ups], refs[ups : ups + downs]
    keep_ref, send_ref, dz_ref, up, down, sems = refs[ups + downs :]
    copies = fetch(down_pieces, down_at, down, sems, ups)
    later = fetch(up_pieces, up_at, up, sems, 0)
    wait_all(copies)
    count, wide = own_ref.shape[0], dz_ref.shape[1]
    step = min(512, wide)
    for start, dm_ref in ((count, got_ref), (0, own_ref)):
        rows = pl.ds(start, count)
        for left in range(0, wide, step):
            du = lax.dot_general(dm_ref[...], down[left : left + step, :], NT, preferred_element_type=F32)
            slope = slope_ref[rows, left : left + step].astype(F32)
            dz_ref[rows, left : left + step] = (du * slope).astype(BF16)
    wait_all(later)
    send = lax.dot_general(dz_ref[count:, :], up[...], NT, preferred_element_type=F32)
    send_ref[...] = send.astype(BF16)
    keep_ref[...] = lax.dot_general(dz_ref[:count, :], up[...], NT, preferred_element_type=F32)


def between_kernel(
    core_ref, scale_ref, da_ref, da_got_ref, h_ref, keep_ref, got_ref, cot_ref, norm_ref,
    dh_ref, own_ref, send_ref, grad_ref, r_ref, dr_ref,
):
    own, other = halves(core_ref, keep_ref.shape[1])
    r_ref[:, own] = keep_ref[...]
    r_ref[:, other] = got_ref[...]
    e = da_ref[...] + da_got_ref[...].astype(F32)
    vhat, scale = normed(h_ref[...])
    grad_ref[0:1, :] = column_sum(e * vhat)
    grad_ref[1:2, :] = column_sum(e)
    g = cot_ref[...].astype(F32) * scale_ref[0]
    dh = g + normed_back(e, norm_ref[2:3, :], vhat, scale)
    dh_ref[...] = dh
    vhat, scale = normed(r_ref[...])
    grad_ref[2:3, :] = column_sum(dh * vhat)
    grad_ref[3:4, :] = column_sum(dh)
    dr_ref[...] = normed_back(dh, norm_ref[1:2, :], vhat, scale).astype(BF16)
    own_ref[...] = dr_ref[:, own]
    send_ref[...] = dr_ref[:, other]


def out_back_kernel(count, ny, at_ref, core_ref, own_ref, got_ref, *refs):
    pieces = refs[:count]
    keep_ref, send_ref, weight, sems = refs[count:]
    wait_all(fetch(pieces, at_ref, weight, sems, 0, 0, weight.shape[1]))
    core = core_ref[0]
    hw = keep_ref.shape[2]
    size = own_ref.shape[0]
    for own in (False, True):
        head = core if own else 1 - core
        for yh in range(ny):
            rows = pl.ds(pl.multiple_of((yh * 2 + head) * hw, hw), hw)
            for start, dr_ref in ((0, own_ref), (size, got_ref)):
                value = lax.dot_general(dr_ref[...], weight[rows, :], NT, preferred_element_type=F32)
                if own:
                    keep_ref[yh, pl.ds(start, size), :] = value
                else:
                    send_ref[yh, pl.ds(start, size), :] = value.astype(BF16)


def input_back_kernel(count, offset, at_ref, a_ref, *refs):
    pieces = refs[:count]
    keep_ref, send_ref, weight, sems = refs[count:]
    wait_all(fetch(pieces, at_ref, weight, sems, 0, offset, weight.shape[1]))
    block = keep_ref.shape[1]
    for number in range(a_ref.shape[0] // block):
        rows = pl.ds(number * block, block)
        value = lax.dot_general(a_ref[rows, :], weight[...], NT, preferred_element_type=F32)
        if number % 2 == 0:
            keep_ref[number // 2] = value
        else:
            send_ref[number // 2] = value.astype(BF16)


def bottom_kernel(*refs):
    tok_ref, dh_ref, norm_ref = refs[:3]
    pieces, (out_ref, grad_ref) = refs[3:-2], refs[-2:]
    e = pieces[0][...].astype(F32)
    for piece in pieces[1:]:
        e = e + piece[...].astype(F32)
    vhat, scale = normed(tok_ref[...].astype(F32))
    out_ref[...] = (dh_ref[...] + normed_back(e, norm_ref[0:1, :], vhat, scale)).astype(BF16)
    grad_ref[0:1, :] = column_sum(e * vhat)
    grad_ref[1:2, :] = column_sum(e)


def grads(lefts, rights, at, cols, numbers):
    found = []
    for number in numbers:
        block = lax.dynamic_slice(lefts[0], (0, at[number] * cols), (lefts[0].shape[0], cols))
        found.append(lax.dot_general(block, rights[0], TN, preferred_element_type=F32).astype(BF16))
    return found


def on_device(
    tokens,
    cotangent,
    group_ids,
    group_weight,
    block_order,
    w_qkv,
    w_out,
    w_up,
    w_down,
    norm_gain,
    norm_bias,
):
    nz, nx, ny, nc = (lax.axis_size(a) for a in "zxyc")
    iz, ix, iy, ic = (lax.axis_index(a) for a in "zxyc")
    rows_here, _, width = tokens.shape
    heads = width // HD
    spans = ny * nc
    mine = heads // spans
    hw = mine * HD
    lanes = min(128, hw)
    wrows = w_qkv.shape[0]
    ffrows = w_down.shape[0]
    ff = w_up.shape[1]
    ffh = ff // nc
    owh = width // nc
    dprows = spans * wrows
    length = spans * rows_here
    crow = nc * rows_here
    half = nz // 2
    shaped = jax.ShapeDtypeStruct

    def middle(pieces):
        return pieces[1:2] + pieces[-1:]

    def sems(count):
        return pltpu.SemaphoreType.DMA((count,))

    tok = tokens.reshape(rows_here, width)
    cot = cotangent.reshape(rows_here, width)
    norm_rows = jnp.concatenate([norm_gain, norm_bias], 0).T
    norm_rows = jnp.pad(norm_rows, ((0, 0), (0, 120)))
    norm_rows = jnp.broadcast_to(norm_rows[None], (nc, wrows, 128))
    cut = jnp.concatenate(
        [
            w_qkv.reshape(wrows, 3, ny, nc, hw).transpose(3, 0, 2, 1, 4).reshape(nc, wrows, ny * 3 * hw),
            w_out.reshape(wrows, nc, owh).transpose(1, 0, 2),
            norm_rows,
            w_up.reshape(wrows, nz, nx, ny, nc, ffrows).transpose(4, 0, 1, 3, 2, 5).reshape(nc, wrows, ffh),
        ],
        -1,
    )
    cut = pair(take(cut, ic), shift(take(cut, 1 - ic), "c"), ic).reshape(nc * wrows, -1)
    q_cut = cut[:, : ny * 3 * hw].reshape(nc * wrows, ny, 3 * hw)
    left = ny * 3 * hw
    o_cut = jnp.broadcast_to(cut[:, None, left : left + owh + 128], (nc * wrows, ny, owh + 128))
    up_cut = cut[:, left + owh + 128 :]
    qo = exchange(jnp.concatenate([o_cut, q_cut], -1).transpose(1, 0, 2), "y")
    qo = qo.reshape(dprows, owh + 128 + 3 * hw)
    down_x = in_order(ring_gather(w_down, "x"), "x").reshape(nx * ffrows, width)
    core = ic.astype(jnp.int32).reshape(1)
    span_y = iy.astype(jnp.int32).reshape(1)

    qo_z = ring_gather(qo, "z")
    up_z = ring_gather(up_cut, "z")
    down_z = ring_gather(after(down_x, *middle(qo_z)), "z")
    tok_y = ring_gather(after(tok, *middle(qo_z)), "y")
    tok_all = []
    for item in tok_y:
        tok_all.append(item)
        tok_all.append(shift(item, "c"))
    qo_w, up_w, down_w = [], [], []
    up_at, down_at = [], []
    for step, item in enumerate(qo_z):
        for far, piece in enumerate(ring_gather(item, "x")):
            qo_w.append(piece)
            up_at.append(back("z", step) * nx + back("x", far))
    up_y = [in_order(ring_gather(item, "y"), "y").reshape(dprows, ffh) for item in up_z]
    for item in up_y:
        up_w += ring_gather(item, "x")
    for step, item in enumerate(down_z):
        for far, piece in enumerate(ring_gather(item, "y")):
            down_w.append(piece)
            down_at.append(back("z", step) * ny + back("y", far))
    up_at = jnp.stack(up_at).astype(jnp.int32)
    down_at = jnp.stack(down_at).astype(jnp.int32)
    q_w, o_w, q_off = qo_w, qo_w, owh + 128
    if hw % 128:
        q_w, o_w, q_off = [p[:, owh + 128 :] for p in qo_w], [p[:, : owh + 128] for p in qo_w], 0
    nqo, nup, ndown = len(qo_w), len(up_w), len(down_w)

    order = after(block_order, *middle(qo_z))[0].reshape(ny, nc)
    places = []
    for sy in range(ny):
        for sc in range(nc):
            places.append(take(take(order, back("y", sy)), back("c", sc)))
    places = jnp.stack(places)
    ranks = jnp.arange(spans, dtype=jnp.int32)
    sorted_at = jnp.sum(jnp.where(places[None, :] == ranks[:, None], ranks[None, :], 0), -1)
    offsets = jnp.arange(rows_here, dtype=jnp.int32)
    positions = (places[:, None] * rows_here + offsets[None, :]).reshape(length)
    lane = jnp.arange(lanes, dtype=jnp.int32)
    frequency = jnp.exp((lane % (HD // 2)).astype(F32) * (-2.0 * math.log(10000.0) / HD))
    angles = positions.astype(F32)[:, None] * frequency[None, :]
    cos_lanes = jnp.cos(angles)
    sin_lanes = jnp.sin(angles) * jnp.where(lane % HD < HD // 2, -1.0, 1.0)

    a1, qkv, norms = call(
        functools.partial(input_kernel, nqo, spans, lanes, q_off, owh),
        (shaped((length, width), BF16), shaped((length, 3 * hw), BF16), shaped((8, width), F32)),
        [IN_SMEM] + [IN_VMEM] * (2 + spans) + [ANYWHERE] * (2 * nqo),
        [pltpu.VMEM((width, 3 * hw), BF16), pltpu.VMEM((width, 128), BF16), sems(2 * nqo)],
    )(up_at, cos_lanes, sin_lanes, *tok_all, *q_w, *o_w)
    qkv_now = after(qkv, *(middle(down_z) + up_w[: 2 * nx] + up_w[-nx:] + down_w[:ny]))
    attn, lse = call(
        functools.partial(attend_kernel, spans, lanes),
        (shaped((length, hw), BF16), shaped((mine, length, 128), F32)),
        [IN_SMEM, IN_VMEM],
    )(sorted_at, qkv_now)

    attn_now = after(attn, *[up_y[half]])
    sent = attn_now.reshape(ny, nc, rows_here, hw)
    o_near = [sent[0]] + [shift(sent[sy], "y", ny - sy) for sy in range(1, ny)]
    o_far = [shift(item, "c") for item in o_near]
    o_near[0] = after(o_near[0], *[down_z[half]])
    r_keep, r_send, o_chip = call(
        functools.partial(out_kernel, nqo, ny),
        (shaped((rows_here, owh), F32), shaped((rows_here, owh), F32), shaped((crow, width), BF16)),
        [IN_SMEM, IN_SMEM] + [IN_VMEM] * (2 * ny) + [IN_SMEM] + [ANYWHERE] * nqo,
        [pltpu.VMEM((width, owh), BF16), sems(nqo)],
    )(up_at, core, *o_near, *o_far, span_y, *o_w)
    r_send = after(r_send, *(down_w[ny : 2 * ny] + down_w[-ny:] + up_w[half * nx : half * nx + nx]))
    r_got = shift(r_send, "c")
    h, a2 = call(
        middle_kernel,
        (shaped((rows_here, width), F32), shaped((rows_here, width), BF16)),
        [IN_SMEM] + [IN_VMEM] * 4,
        [pltpu.VMEM((rows_here, width), F32)],
    )(core, r_keep, r_got, tok, norms)
    a2 = after(a2)
    a2_got = shift(a2, "c")
    m_keep, m_send, u, slope = call(
        functools.partial(mlp_kernel, nup, ndown),
        (
            shaped((rows_here, width), F32),
            shaped((rows_here, width), BF16),
            shaped((crow, ffh), BF16),
            shaped((crow, ffh), BF16),
        ),
        [IN_SMEM, IN_SMEM, IN_VMEM, IN_VMEM] + [ANYWHERE] * (nup + ndown),
        [pltpu.VMEM((width, ffh), BF16), pltpu.VMEM((ffh, width), BF16), sems(nup + ndown)],
    )(up_at, down_at, a2, a2_got, *up_w, *down_w)
    m_got = shift(m_send, "c")
    match = group_ids[:, None] == jnp.arange(group_weight.shape[0], dtype=jnp.int32)[None, :]
    scale = jnp.sum(jnp.where(match, group_weight[None, :], 0.0)).reshape(1)
    out_tokens, dm, grads_3 = call(
        top_kernel,
        (shaped((rows_here, width), BF16), shaped((rows_here, width), BF16), shaped((2, width), F32)),
        [IN_SMEM] + [IN_VMEM] * 5,
    )(scale, m_keep, m_got, h, cot, norms)

    dm_got = shift(dm, "c")
    dm_all = jnp.concatenate([dm, dm_got], 0)
    down_own, down_got = [None] * nz, [None] * nz
    up_own, up_got = [None] * nz, [None] * nz
    early, late = late_last(nz)[:2], late_last(nz)[2:]

    def down_block(step, right, *when):
        blocks = grads([u], [right], down_at, nx * ffrows, range(step * ny, step * ny + ny))
        down_own[step] = blocks[0]
        down_got[step] = [shift(after(blocks[far], *when), "y", ny - far) for far in range(1, ny)]

    def up_block(step, right):
        blocks = grads([a2_all], [right], up_at, dprows, range(step * nx, step * nx + nx))
        up_own[step] = blocks[0]
        up_got[step] = [shift(blocks[far], "x", nx - far) for far in range(1, nx)]

    right = dm_all
    for step in early:
        down_block(step, right, right)
        right = after(dm_all, down_own[step])
    blocks = [down_own[early[-1]]]
    dm = after(dm, blocks[0])
    da_keep, da_send, dz = call(
        functools.partial(mlp_back_kernel, nup, ndown),
        (
            shaped((rows_here, width), F32),
            shaped((rows_here, width), BF16),
            shaped((crow, ffh), BF16),
        ),
        [IN_SMEM, IN_SMEM, IN_VMEM, IN_VMEM, IN_VMEM] + [ANYWHERE] * (nup + ndown),
        [pltpu.VMEM((width, ffh), BF16), pltpu.VMEM((ffh, width), BF16), sems(nup + ndown)],
    )(up_at, down_at, dm, dm_got, slope, *up_w, *down_w)
    da_got = shift(da_send, "c")
    a2_all = jnp.concatenate([a2, a2_got], 0)
    right = after(dz, *down_got[early[0]])
    for step in early:
        up_block(step, right)
        right = after(dz, up_own[step])
    blocks = [up_own[early[-1]]]
    da_keep = after(da_keep, blocks[0])
    dh, dr, dr_send, grads_21 = call(
        between_kernel,
        (
            shaped((rows_here, width), F32),
            shaped((rows_here, owh), BF16),
            shaped((rows_here, owh), BF16),
            shaped((4, width), F32),
        ),
        [IN_SMEM, IN_SMEM] + [IN_VMEM] * 7,
        [pltpu.VMEM((rows_here, width), F32), pltpu.VMEM((rows_here, width), BF16)],
    )(core, scale, da_keep, da_got, h, r_keep, r_got, cot, norms)
    dr_send = after(dr_send, *down_got[early[1]])
    dr_got = shift(dr_send, "c")
    do_keep, do_send = call(
        functools.partial(out_back_kernel, nqo, ny),
        (shaped((ny, crow, hw), F32), shaped((ny, crow, hw), BF16)),
        [IN_SMEM, IN_SMEM, IN_VMEM, IN_VMEM] + [ANYWHERE] * nqo,
        [pltpu.VMEM((width, owh), BF16), sems(nqo)],
    )(up_at, core, dr, dr_got, *o_w)
    do_got = shift(do_send, "c")
    do_got = jnp.concatenate([do_got[:, rows_here:], do_got[:, :rows_here]], 1)
    do = (do_keep + do_got.astype(F32)).astype(BF16)
    parts = []
    for sy in range(ny):
        item = take(do, lax.rem(iy + sy, ny))
        parts.append(item if sy == 0 else shift(item, "y", sy))
    do_all = jnp.concatenate(parts, 0)
    down_y, up_x = [None] * nz, [None] * nz
    right, wide_right = after(dm_all, do), after(dz, do)
    for step in late:
        up_block(step, wide_right)
        down_block(step, right, do_all)
    for step in early:
        down_y[step] = add_parts(down_own[step], down_got[step], do)
        up_x[step] = add_parts(up_own[step], up_got[step], do)
    out_blocks = grads([o_chip], [jnp.concatenate([dr, dr_got], 0)], up_at, dprows, range(nz * nx))
    out_own = jnp.stack(out_blocks[0::nx])
    out_x = add_parts(out_own, [shift(jnp.stack(out_blocks[1::nx]), "x")], do_all)

    down_first = ring_first(down_y, "z")
    sums = [None] * nz
    for step in early:
        sums[step] = scatter_sum(up_x[step].reshape(ny, nc * wrows, ffh), "y").astype(BF16)
    up_first = ring_first(sums, "z")
    do_all = after(do_all, *[t for t in down_y + up_x + sums + down_own + up_own if t is not None])
    dqkv = call(
        functools.partial(attend_back_kernel, spans, lanes),
        shaped((length, 3 * hw), BF16),
        [IN_SMEM] + [IN_VMEM] * 6,
        [pltpu.VMEM((length, lanes), F32)] * 2,
    )(sorted_at, qkv, attn, do_all, lse, cos_lanes, sin_lanes)
    dqkv = after(dqkv, *down_first)
    qkv_blocks = grads([a1], [dqkv], up_at, dprows, range(nz * nx))
    qkv_own = jnp.stack(qkv_blocks[0::nx])
    qkv_got = shift(jnp.stack(qkv_blocks[1::nx]), "x")
    da1_keep, da1_send = call(
        functools.partial(input_back_kernel, nqo, q_off),
        (shaped((ny, rows_here, width), F32), shaped((ny, rows_here, width), BF16)),
        [IN_SMEM, IN_VMEM] + [ANYWHERE] * nqo,
        [pltpu.VMEM((width, 3 * hw), BF16), sems(nqo)],
    )(up_at, after(dqkv, qkv_own, *up_first), *q_w)
    da1_got = shift(da1_send, "c")
    arrived = [
        shift((da1_keep[sy] + da1_got[sy].astype(F32)).astype(BF16), "y", ny - sy) for sy in range(1, ny)
    ]
    grad_tokens, grads_0 = call(
        bottom_kernel,
        (shaped((rows_here, width), BF16), shaped((2, width), F32)),
        [IN_VMEM] * (5 + len(arrived)),
    )(tok, dh, norms, da1_keep[0], da1_got[0], *arrived)
    grad_tokens = grad_tokens.reshape(tokens.shape)
    out_tokens = out_tokens.reshape(tokens.shape)

    for step in range(nz):
        if down_y[step] is None:
            down_y[step] = add_parts(down_own[step], down_got[step], dqkv)
            up_x[step] = add_parts(up_own[step], up_got[step], dqkv)
    down = ring_rest(down_y, down_first, "z").astype(BF16)
    down = scatter_sum(down.reshape(nx, ffrows, width), "x")
    for step in late:
        sums[step] = scatter_sum(up_x[step].reshape(ny, nc * wrows, ffh), "y").astype(BF16)
    up = ring_rest(sums, up_first, "z").reshape(nc, wrows, ffh)
    up = pair(take(up, ic), shift(take(up, 1 - ic), "c"), ic)
    up = up.reshape(nc, wrows, nz, ny, nx, ffrows).transpose(1, 2, 4, 3, 0, 5).reshape(wrows, ff)

    qkv_x = (qkv_own.astype(F32) + qkv_got.astype(F32)).astype(BF16)
    both = jnp.concatenate([out_x, qkv_x], -1)
    both = ring_scatter([both[step] for step in range(nz)], "z").astype(BF16)
    out, qkv_g = both[:, :owh], both[:, owh:]
    out = scatter_sum(out.reshape(ny, nc * wrows, owh), "y").reshape(nc, wrows, owh)
    out = pair(take(out, ic), shift(take(out, 1 - ic), "c"), ic)
    out = out.transpose(1, 0, 2).reshape(wrows, width)
    qkv_g = exchange(qkv_g.reshape(ny, nc * wrows, 3 * hw), "y")
    qkv_g = qkv_g.reshape(ny, nc, wrows, 3 * hw).transpose(1, 0, 2, 3)
    qkv_g = pair(take(qkv_g, ic), shift(take(qkv_g, 1 - ic), "c"), ic)
    qkv_g = qkv_g.reshape(nc, ny, wrows, 3, hw).transpose(2, 3, 1, 0, 4)
    qkv_g = qkv_g.reshape(wrows, 3 * width).astype(F32)

    norm_sums = jnp.concatenate(
        [
            grads_0[0:1],
            grads_21[2:3],
            grads_21[0:1],
            grads_3[0:1],
            grads_0[1:2],
            grads_21[3:4],
            grads_21[1:2],
            grads_3[1:2],
        ],
        0,
    )
    for axis in "cyxz":
        norm_sums = all_sum(norm_sums, axis)
    place = ((iz * nx + ix) * ny + iy) * nc + ic
    norm_sums = lax.dynamic_slice(norm_sums, (0, place * wrows), (8, wrows))
    return (out_tokens, grad_tokens, qkv_g, out, up, down, norm_sums[:4], norm_sums[4:])


def solution(mesh):
    fine = Mesh(
        mesh.devices.reshape(mesh.shape["dp"] // 2, 2, mesh.shape["blk"] // 2, 2),
        ("z", "x", "y", "c"),
    )
    dp, blk, every = ("z", "x"), ("y", "c"), ("z", "x", "y", "c")
    return jax.shard_map(
        on_device,
        mesh=fine,
        in_specs=(
            P(blk, dp, None),
            P(blk, dp, None),
            P(dp),
            P(),
            P(dp, None),
            P(every, None),
            P(every, None),
            P(every, None),
            P(every, None),
            P(None, every),
            P(None, every),
        ),
        out_specs=(
            P(blk, dp, None),
            P(blk, dp, None),
            P(every, None),
            P(every, None),
            P(every, None),
            P(every, None),
            P(None, every),
            P(None, every),
        ),
        check_vma=False,
    )
```

```python
import functools
import math

import jax
import jax.numpy as jnp
from jax import lax
from jax.experimental import pallas as pl
from jax.experimental.pallas import tpu as pltpu
from jax.sharding import Mesh
from jax.sharding import PartitionSpec as P

HD = 64
F32 = jnp.float32
BF16 = jnp.bfloat16


def shift(value, axis, step=1):
    size = lax.axis_size(axis)
    return lax.ppermute(value, axis, [(i, (i + step) % size) for i in range(size)])


def after(value, *others):
    return lax.optimization_barrier((value,) + others)[0]


def back(axis, step):
    size = lax.axis_size(axis)
    return lax.rem(lax.axis_index(axis) + size - step, size)


def take(array, at, axis=0):
    return lax.dynamic_index_in_dim(array, at, axis, keepdims=False)


def direct_gather(piece, axis):
    size = lax.axis_size(axis)
    return [piece] + [shift(piece, axis, step) for step in range(1, size)]


def ring_gather(piece, axis):
    size = lax.axis_size(axis)
    pieces = [piece] * size
    for step in range(1, size // 2 + 1):
        pieces[step] = shift(pieces[step - 1], axis)
    for step in range(size - 1, size // 2, -1):
        pieces[step] = shift(pieces[(step + 1) % size], axis, -1)
    return pieces


def in_order(pieces, axis):
    if len(pieces) == 2:
        return pair(pieces[0], pieces[1], lax.axis_index(axis))
    buffer = jnp.zeros((len(pieces),) + pieces[0].shape, pieces[0].dtype)
    for step, piece in enumerate(pieces):
        at = (back(axis, step),) + (0,) * piece.ndim
        buffer = lax.dynamic_update_slice(buffer, piece[None], at)
    return buffer


def pair(own, other, index):
    first = jnp.where(index == 0, own, other)
    second = jnp.where(index == 0, other, own)
    return jnp.stack([first, second])


def ring_first(parts, axis):
    size = len(parts)
    half = size // 2
    found = [shift(parts[half].astype(BF16), axis)]
    if size - 1 - half:
        found.append(shift(parts[size - 1 - half].astype(BF16), axis, -1))
    return found


def ring_rest(parts, arrived, axis):
    size = len(parts)
    half = size // 2
    total = parts[0].astype(F32)
    for carry, count, way in zip(arrived, (half, size - 1 - half), (1, -1)):
        for far in range(count - 1, 0, -1):
            part = parts[size - far if way == 1 else far]
            carry = shift((carry.astype(F32) + part.astype(F32)).astype(BF16), axis, way)
        total = total + carry.astype(F32)
    return total


def ring_scatter(parts, axis):
    return ring_rest(parts, ring_first(parts, axis), axis)


def scatter_sum(parts, axis):
    size = parts.shape[0]
    return ring_scatter([take(parts, back(axis, step)) for step in range(size)], axis)


def late_last(size):
    half = size // 2
    steps = list(range(half, 0, -1)) + list(range(half + 1, size)) + [0]
    return list(dict.fromkeys(steps))


def send_parts(parts, axis):
    size = parts.shape[0]
    got = [shift(take(parts, back(axis, step)), axis, size - step) for step in range(1, size)]
    return take(parts, lax.axis_index(axis)), got


def add_parts(own, got, when):
    total = own.astype(F32)
    for item in got:
        total = total + after(item, when).astype(F32)
    return total.astype(BF16)


def exchange(parts, axis):
    size = parts.shape[0]
    index = lax.axis_index(axis)
    pieces = [take(parts, index)]
    for step in range(1, size):
        pieces.append(shift(take(parts, lax.rem(index + step, size)), axis, step))
    return in_order(pieces, axis)


def all_sum(value, axis):
    pieces = direct_gather(value, axis)
    total = pieces[0]
    for piece in pieces[1:]:
        total = total + piece
    return total


IN_VMEM = pl.BlockSpec(memory_space=pltpu.VMEM)
IN_SMEM = pl.BlockSpec(memory_space=pltpu.SMEM)
ANYWHERE = pl.BlockSpec(memory_space=pl.ANY)
IN_HBM = pl.BlockSpec(memory_space=pltpu.HBM)


def call(kernel, out_shape, in_specs, scratch=(), vmem=16):
    several = isinstance(out_shape, (tuple, list))
    return pl.pallas_call(
        kernel,
        out_shape=out_shape,
        in_specs=in_specs,
        out_specs=[IN_VMEM] * len(out_shape) if several else IN_VMEM,
        scratch_shapes=list(scratch),
        compiler_params=pltpu.CompilerParams(vmem_limit_bytes=vmem * 1024 * 1024),
        cost_estimate=pl.CostEstimate(flops=1024, bytes_accessed=1024, transcendentals=0),
    )


def fetch(pieces, at_ref, target, sems, first, offset=0, columns=None):
    copies = []
    for number, piece in enumerate(pieces):
        rows = piece.shape[0]
        source = piece if columns is None else piece.at[:, pl.ds(offset, columns)]
        place = pl.ds(pl.multiple_of(at_ref[number] * rows, rows), rows)
        copies.append(pltpu.make_async_copy(source, target.at[place], sems.at[first + number]))
    for copy in copies:
        copy.start()
    return copies


def wait_all(copies):
    for copy in copies:
        copy.wait()


def partner(values):
    half = HD // 2
    if values.shape[-1] == HD:
        return jnp.concatenate([values[:, half:], values[:, :half]], -1)
    lanes = values.shape[-1]
    lane = lax.broadcasted_iota(jnp.int32, values.shape, 1)
    low = lax.rem(lane, HD) < half
    return jnp.where(low, pltpu.roll(values, lanes - half, 1), pltpu.roll(values, half, 1))


def attend_kernel(blocks, lanes, order_ref, qkv_ref, o_ref, lse_ref):
    length, third = o_ref.shape
    size = length // blocks
    per = lanes // HD
    lane = lax.broadcasted_iota(jnp.int32, (1, lanes), 1) // HD
    row = lax.broadcasted_iota(jnp.int32, (size, size), 0)
    col = lax.broadcasted_iota(jnp.int32, (size, size), 1)
    for group in range(third // lanes):
        left = group * lanes

        def one_row(i):
            at = pl.multiple_of(order_ref[i] * size, size)
            q = qkv_ref[pl.ds(at, size), left : left + lanes]
            outs, totals = [], []
            for head in range(per):
                qh = q * (lane == head).astype(BF16)

                def scores(start):
                    k = qkv_ref[pl.ds(start, size), third + left : third + left + lanes]
                    return lax.dot_general(qh, k, (((1,), (1,)), ((), ())), preferred_element_type=F32)

                def values(p, start):
                    v = qkv_ref[pl.ds(start, size), 2 * third + left : 2 * third + left + lanes]
                    return jnp.dot(p.astype(BF16), v, preferred_element_type=F32)

                s = jnp.where(col <= row, scores(at), -1e30)
                top = jnp.max(s, -1, keepdims=True)
                p = jnp.exp(s - top)
                state = (top, jnp.sum(p, -1, keepdims=True), values(p, at))

                def step(j, state):
                    top, total, acc = state
                    start = pl.multiple_of(order_ref[j] * size, size)
                    s = scores(start)
                    new = jnp.maximum(top, jnp.max(s, -1, keepdims=True))
                    factor = jnp.exp(top - new)
                    p = jnp.exp(s - new)
                    total = total * factor + jnp.sum(p, -1, keepdims=True)
                    return new, total, acc * factor + values(p, start)

                if blocks <= 4:
                    for j in range(i):
                        state = step(j, state)
                else:
                    state = lax.fori_loop(0, i, step, state)
                top, total, acc = state
                outs.append(acc / total)
                lse = jnp.broadcast_to(top + jnp.log(total), (size, 128))
                lse_ref[group * per + head, pl.ds(at, size), :] = lse
            out = outs[0]
            for head in range(1, per):
                out = jnp.where(lane == head, outs[head], out)
            o_ref[pl.ds(at, size), left : left + lanes] = out.astype(BF16)

        if blocks <= 4:
            for i in range(blocks):
                one_row(i)
        else:
            pl.loop(0, blocks)(one_row)


def attend_back_kernel(
    blocks, lanes, order_ref, qkv_ref, o_ref, do_ref, lse_ref, cos_ref, sin_ref, out_ref, dk_ref, dv_ref
):
    length, third = o_ref.shape
    size = length // blocks
    per = lanes // HD
    lane = lax.broadcasted_iota(jnp.int32, (1, lanes), 1) // HD
    row = lax.broadcasted_iota(jnp.int32, (size, size), 0)
    col = lax.broadcasted_iota(jnp.int32, (size, size), 1)
    nt = (((1,), (1,)), ((), ()))
    tn = (((0,), (0,)), ((), ()))

    def unturn(values, rows):
        return values * cos_ref[rows, :] - partner(values) * sin_ref[rows, :]

    for group in range(third // lanes):
        left = group * lanes
        dk_ref[...] = jnp.zeros_like(dk_ref)
        dv_ref[...] = jnp.zeros_like(dv_ref)

        def one_row(i):
            at = pl.multiple_of(order_ref[i] * size, size)
            rows = pl.ds(at, size)
            q = qkv_ref[rows, left : left + lanes]
            do = do_ref[rows, left : left + lanes]
            prod = do.astype(F32) * o_ref[rows, left : left + lanes].astype(F32)
            grads = []
            for head in range(per):
                own = (lane == head).astype(BF16)
                qh, doh = q * own, do * own
                delta = jnp.sum(jnp.where(lane == head, prod, 0.0), -1, keepdims=True)
                lse = lse_ref[group * per + head, rows, 0:1]

                def step(start, diagonal):
                    where = pl.ds(start, size)
                    k = qkv_ref[where, third + left : third + left + lanes]
                    v = qkv_ref[where, 2 * third + left : 2 * third + left + lanes]
                    s = lax.dot_general(qh, k, nt, preferred_element_type=F32)
                    p = jnp.exp(s - lse)
                    if diagonal:
                        p = jnp.where(col <= row, p, 0.0)
                    dp = lax.dot_general(doh, v, nt, preferred_element_type=F32)
                    ds = (p * (dp - delta)).astype(BF16)
                    dv_ref[where, :] += lax.dot_general(p.astype(BF16), doh, tn, preferred_element_type=F32)
                    dk_ref[where, :] += lax.dot_general(ds, qh, tn, preferred_element_type=F32)
                    return jnp.dot(ds, k, preferred_element_type=F32)

                dq = step(at, True)
                if blocks <= 4:
                    for j in range(i):
                        dq = dq + step(pl.multiple_of(order_ref[j] * size, size), False)
                else:
                    dq = lax.fori_loop(
                        0, i, lambda j, c: c + step(pl.multiple_of(order_ref[j] * size, size), False), dq
                    )
                grads.append(dq)
            dq = grads[0]
            for head in range(1, per):
                dq = jnp.where(lane == head, grads[head], dq)
            out_ref[rows, left : left + lanes] = unturn(dq * 0.125, rows).astype(BF16)

        if blocks <= 4:
            for i in range(blocks):
                one_row(i)
        else:
            pl.loop(0, blocks)(one_row)
        for start in range(0, length, size):
            rows = pl.ds(start, size)
            out_ref[rows, third + left : third + left + lanes] = unturn(dk_ref[rows, :], rows).astype(BF16)
            out_ref[rows, 2 * third + left : 2 * third + left + lanes] = dv_ref[rows, :].astype(BF16)


GELU_A = math.sqrt(2.0 / math.pi)
GELU_B = 0.044715


NT = (((1,), (1,)), ((), ()))
TN = (((0,), (0,)), ((), ()))


def normed(values):
    centred = values - jnp.mean(values, -1, keepdims=True)
    scale = lax.rsqrt(jnp.mean(centred * centred, -1, keepdims=True) + 1e-05)
    return centred * scale, scale


def normed_back(grad, gain, vhat, scale):
    scaled = grad * gain
    return scale * (
        scaled - jnp.mean(scaled, -1, keepdims=True) - vhat * jnp.mean(scaled * vhat, -1, keepdims=True)
    )


def column_sum(values):
    return jnp.sum(values, 0, keepdims=True)


def halves(core_ref, width):
    own = pl.ds(pl.multiple_of(core_ref[0] * width, width), width)
    other = pl.ds(pl.multiple_of((1 - core_ref[0]) * width, width), width)
    return own, other


def input_kernel(count, blocks, lanes, q_off, n_off, at_ref, cos_ref, sin_ref, *refs):
    toks, refs = refs[:blocks], refs[blocks:]
    q_pieces, n_pieces, refs = refs[:count], refs[count : 2 * count], refs[2 * count :]
    a_ref, out_ref, norm_ref, weight, columns, sems = refs
    wide = out_ref.shape[1]
    first = fetch(n_pieces, at_ref, columns, sems, 0, n_off, 128)
    later = fetch(q_pieces, at_ref, weight, sems, count, q_off, wide)
    wait_all(first)
    norm_ref[...] = jnp.transpose(columns[...].astype(F32))[:8, :]
    gain, bias = norm_ref[0:1, :], norm_ref[4:5, :]
    rows_here = toks[0].shape[0]
    for number, tok_ref in enumerate(toks):
        vhat, _ = normed(tok_ref[...].astype(F32))
        a_ref[pl.ds(number * rows_here, rows_here), :] = (vhat * gain + bias).astype(BF16)
    wait_all(later)
    third = wide // 3
    block = 256
    for start in range(0, out_ref.shape[0], block):
        rows = pl.ds(start, block)
        acc = jnp.dot(a_ref[rows, :], weight[...], preferred_element_type=F32)
        cos, sin = cos_ref[rows, :], sin_ref[rows, :]
        for part in range(3):
            for left in range(0, third, lanes):
                at = part * third + left
                values = acc[:, at : at + lanes]
                if part < 2:
                    values = values * cos + partner(values) * sin
                if part == 0:
                    values = values * 0.125
                out_ref[rows, at : at + lanes] = values.astype(BF16)


def out_kernel(count, ny, at_ref, core_ref, *refs):
    near, far, refs = refs[:ny], refs[ny : 2 * ny], refs[2 * ny :]
    y_ref, pieces, refs = refs[0], refs[1 : 1 + count], refs[1 + count :]
    keep_ref, send_ref, chip_ref, weight, sems = refs
    copies = fetch(pieces, at_ref, weight, sems, 0, 0, weight.shape[1])
    core = core_ref[0]
    rows, hw = near[0].shape[1], near[0].shape[2]
    for parts, is_far in ((near, False), (far, True)):
        other = 1 - core if is_far else core
        for ahead in range(ny):
            yh = lax.rem(y_ref[0] + ahead, ny)
            for sc in range(2):
                token = pl.ds(((1 - sc) if is_far else sc) * rows, rows)
                value = parts[ahead][sc]
                if hw % 128 == 0:
                    left = pl.multiple_of((yh * 2 + other) * hw, hw)
                    chip_ref[token, pl.ds(left, hw)] = value
                else:
                    for place in range(2 * ny):

                        @pl.when(yh * 2 + other == place)
                        def _(place=place, value=value, token=token):
                            chip_ref[token, place * hw : place * hw + hw] = value

    wait_all(copies)
    send_ref[...] = jnp.dot(chip_ref[rows:, :], weight[...], preferred_element_type=F32)
    keep_ref[...] = jnp.dot(chip_ref[:rows, :], weight[...], preferred_element_type=F32)


def middle_kernel(core_ref, keep_ref, got_ref, tok_ref, norm_ref, h_ref, a_ref, r_ref):
    own, other = halves(core_ref, keep_ref.shape[1])
    r_ref[:, own] = keep_ref[...]
    r_ref[:, other] = got_ref[...]
    vhat, _ = normed(r_ref[...])
    h = tok_ref[...].astype(F32) + vhat * norm_ref[1:2, :] + norm_ref[5:6, :]
    h_ref[...] = h
    vhat, _ = normed(h)
    a_ref[...] = (vhat * norm_ref[2:3, :] + norm_ref[6:7, :]).astype(BF16)


def mlp_kernel(ups, downs, up_at, down_at, own_ref, got_ref, *refs):
    up_pieces, down_pieces = refs[:ups], refs[ups : ups + downs]
    keep_ref, send_ref, u_ref, slope_ref, up, down, sems = refs[ups + downs :]
    copies = fetch(up_pieces, up_at, up, sems, 0)
    later = fetch(down_pieces, down_at, down, sems, ups)
    wait_all(copies)
    count, wide = own_ref.shape[0], u_ref.shape[1]
    step = min(512, wide)
    for start, a_ref in ((count, got_ref), (0, own_ref)):
        rows = pl.ds(start, count)
        for left in range(0, wide, step):
            z = jnp.dot(a_ref[...], up[:, left : left + step], preferred_element_type=F32)
            square = z * z
            t = jnp.tanh(GELU_A * z * (1.0 + GELU_B * square))
            half = 0.5 * (1.0 + t)
            u_ref[rows, left : left + step] = (z * half).astype(BF16)
            slope = half + 0.5 * z * (1.0 - t * t) * (GELU_A * (1.0 + 3.0 * GELU_B * square))
            slope_ref[rows, left : left + step] = slope.astype(BF16)
    wait_all(later)
    send_ref[...] = jnp.dot(u_ref[count:, :], down[...], preferred_element_type=F32).astype(BF16)
    keep_ref[...] = jnp.dot(u_ref[:count, :], down[...], preferred_element_type=F32)


def top_kernel(scale_ref, keep_ref, got_ref, h_ref, cot_ref, norm_ref, out_ref, dm_ref, grad_ref):
    vhat, scale = normed(keep_ref[...] + got_ref[...].astype(F32))
    gain = norm_ref[3:4, :]
    out_ref[...] = (h_ref[...] + vhat * gain + norm_ref[7:8, :]).astype(BF16)
    g = cot_ref[...].astype(F32) * scale_ref[0]
    dm_ref[...] = normed_back(g, gain, vhat, scale).astype(BF16)
    grad_ref[0:1, :] = column_sum(g * vhat)
    grad_ref[1:2, :] = column_sum(g)


def mlp_back_kernel(ups, downs, up_at, down_at, own_ref, got_ref, slope_ref, *refs):
    up_pieces, down_pieces = refs[:ups], refs[ups : ups + downs]
    keep_ref, send_ref, dz_ref, up, down, sems = refs[ups + downs :]
    copies = fetch(down_pieces, down_at, down, sems, ups)
    later = fetch(up_pieces, up_at, up, sems, 0)
    wait_all(copies)
    count, wide = own_ref.shape[0], dz_ref.shape[1]
    step = min(512, wide)
    for start, dm_ref in ((count, got_ref), (0, own_ref)):
        rows = pl.ds(start, count)
        for left in range(0, wide, step):
            du = lax.dot_general(dm_ref[...], down[left : left + step, :], NT, preferred_element_type=F32)
            slope = slope_ref[rows, left : left + step].astype(F32)
            dz_ref[rows, left : left + step] = (du * slope).astype(BF16)
    wait_all(later)
    send = lax.dot_general(dz_ref[count:, :], up[...], NT, preferred_element_type=F32)
    send_ref[...] = send.astype(BF16)
    keep_ref[...] = lax.dot_general(dz_ref[:count, :], up[...], NT, preferred_element_type=F32)


def between_kernel(
    core_ref, scale_ref, da_ref, da_got_ref, h_ref, keep_ref, got_ref, cot_ref, norm_ref,
    dh_ref, own_ref, send_ref, grad_ref, r_ref, dr_ref,
):
    own, other = halves(core_ref, keep_ref.shape[1])
    r_ref[:, own] = keep_ref[...]
    r_ref[:, other] = got_ref[...]
    e = da_ref[...] + da_got_ref[...].astype(F32)
    vhat, scale = normed(h_ref[...])
    grad_ref[0:1, :] = column_sum(e * vhat)
    grad_ref[1:2, :] = column_sum(e)
    g = cot_ref[...].astype(F32) * scale_ref[0]
    dh = g + normed_back(e, norm_ref[2:3, :], vhat, scale)
    dh_ref[...] = dh
    vhat, scale = normed(r_ref[...])
    grad_ref[2:3, :] = column_sum(dh * vhat)
    grad_ref[3:4, :] = column_sum(dh)
    dr_ref[...] = normed_back(dh, norm_ref[1:2, :], vhat, scale).astype(BF16)
    own_ref[...] = dr_ref[:, own]
    send_ref[...] = dr_ref[:, other]


def out_back_kernel(count, ny, at_ref, core_ref, own_ref, got_ref, *refs):
    pieces = refs[:count]
    keep_ref, send_ref, weight, sems = refs[count:]
    wait_all(fetch(pieces, at_ref, weight, sems, 0, 0, weight.shape[1]))
    core = core_ref[0]
    hw = keep_ref.shape[2]
    size = own_ref.shape[0]
    for own in (False, True):
        head = core if own else 1 - core
        for yh in range(ny):
            rows = pl.ds(pl.multiple_of((yh * 2 + head) * hw, hw), hw)
            for start, dr_ref in ((0, own_ref), (size, got_ref)):
                value = lax.dot_general(dr_ref[...], weight[rows, :], NT, preferred_element_type=F32)
                if own:
                    keep_ref[yh, pl.ds(start, size), :] = value
                else:
                    send_ref[yh, pl.ds(start, size), :] = value.astype(BF16)


def input_back_kernel(count, offset, at_ref, a_ref, *refs):
    pieces = refs[:count]
    keep_ref, send_ref, weight, sems = refs[count:]
    wait_all(fetch(pieces, at_ref, weight, sems, 0, offset, weight.shape[1]))
    block = keep_ref.shape[1]
    for number in range(a_ref.shape[0] // block):
        rows = pl.ds(number * block, block)
        value = lax.dot_general(a_ref[rows, :], weight[...], NT, preferred_element_type=F32)
        if number % 2 == 0:
            keep_ref[number // 2] = value
        else:
            send_ref[number // 2] = value.astype(BF16)


def bottom_kernel(*refs):
    tok_ref, dh_ref, norm_ref = refs[:3]
    pieces, (out_ref, grad_ref) = refs[3:-2], refs[-2:]
    e = pieces[0][...].astype(F32)
    for piece in pieces[1:]:
        e = e + piece[...].astype(F32)
    vhat, scale = normed(tok_ref[...].astype(F32))
    out_ref[...] = (dh_ref[...] + normed_back(e, norm_ref[0:1, :], vhat, scale)).astype(BF16)
    grad_ref[0:1, :] = column_sum(e * vhat)
    grad_ref[1:2, :] = column_sum(e)


def stacked_kernel(parts, cols, at_ref, left_ref, *refs):
    rights, (own_ref, send_ref) = refs[:parts], refs[parts:]
    size = rights[0].shape[0]
    for number in range(2 * own_ref.shape[0]):
        columns = pl.ds(pl.multiple_of(at_ref[number] * cols, cols), cols)
        total = None
        for place, right in enumerate(rights):
            left = left_ref[place * size : place * size + size, columns]
            value = lax.dot_general(left, right[...], TN, preferred_element_type=F32)
            total = value if total is None else total + value
        target = send_ref if number % 2 else own_ref
        target[number // 2] = total.astype(BF16)


def stacked_grads(left, rights, at, cols):
    wide, count = rights[0].shape[1], left.shape[1] // cols // 2
    if cols % 128:
        blocks = grads(left, rights, at, cols, range(2 * count))
        return jnp.stack(blocks[0::2]), jnp.stack(blocks[1::2])
    return call(
        functools.partial(stacked_kernel, len(rights), cols),
        [jax.ShapeDtypeStruct((count, cols, wide), BF16)] * 2,
        [IN_SMEM] + [IN_VMEM] * (1 + len(rights)),
    )(at, left, *rights)


def blocks_kernel(parts, cols, numbers, at_ref, left_ref, *refs):
    rights, outs = refs[:parts], refs[parts:]
    size = rights[0].shape[0]
    for number, out_ref in zip(numbers, outs):
        columns = pl.ds(pl.multiple_of(at_ref[number] * cols, cols), cols)
        total = None
        for place, right in enumerate(rights):
            left = left_ref[place * size : place * size + size, columns]
            value = lax.dot_general(left, right[...], TN, preferred_element_type=F32)
            total = value if total is None else total + value
        out_ref[...] = total.astype(BF16)


def grads(left, rights, at, cols, numbers):
    if cols % 128 == 0:
        return call(
            functools.partial(blocks_kernel, len(rights), cols, tuple(numbers)),
            [jax.ShapeDtypeStruct((cols, rights[0].shape[1]), BF16)] * len(numbers),
            [IN_SMEM] + [IN_VMEM] * (1 + len(rights)),
        )(at, left, *rights)
    right = jnp.concatenate(rights, 0)
    found = []
    for number in numbers:
        block = lax.dynamic_slice(left, (0, at[number] * cols), (left.shape[0], cols))
        found.append(lax.dot_general(block, right, TN, preferred_element_type=F32).astype(BF16))
    return found


def on_device(
    tokens,
    cotangent,
    group_ids,
    group_weight,
    block_order,
    w_qkv,
    w_out,
    w_up,
    w_down,
    norm_gain,
    norm_bias,
):
    nz, nx, ny, nc = (lax.axis_size(a) for a in "zxyc")
    iz, ix, iy, ic = (lax.axis_index(a) for a in "zxyc")
    rows_here, _, width = tokens.shape
    heads = width // HD
    spans = ny * nc
    mine = heads // spans
    hw = mine * HD
    lanes = min(128, hw)
    wrows = w_qkv.shape[0]
    ffrows = w_down.shape[0]
    ff = w_up.shape[1]
    ffh = ff // nc
    owh = width // nc
    dprows = spans * wrows
    length = spans * rows_here
    crow = nc * rows_here
    half = nz // 2
    shaped = jax.ShapeDtypeStruct

    def middle(pieces):
        return pieces[1:2] + pieces[-1:]

    def sems(count):
        return pltpu.SemaphoreType.DMA((count,))

    tok = tokens.reshape(rows_here, width)
    cot = cotangent.reshape(rows_here, width)
    norm_rows = jnp.concatenate([norm_gain, norm_bias], 0).T
    norm_rows = jnp.pad(norm_rows, ((0, 0), (0, 120)))
    norm_rows = jnp.broadcast_to(norm_rows[None], (nc, wrows, 128))
    cut = jnp.concatenate(
        [
            w_qkv.reshape(wrows, 3, ny, nc, hw).transpose(3, 0, 2, 1, 4).reshape(nc, wrows, ny * 3 * hw),
            w_out.reshape(wrows, nc, owh).transpose(1, 0, 2),
            norm_rows,
            w_up.reshape(wrows, nz, nx, ny, nc, ffrows).transpose(4, 0, 1, 3, 2, 5).reshape(nc, wrows, ffh),
        ],
        -1,
    )
    cut = pair(take(cut, ic), shift(take(cut, 1 - ic), "c"), ic).reshape(nc * wrows, -1)
    q_cut = cut[:, : ny * 3 * hw].reshape(nc * wrows, ny, 3 * hw)
    left = ny * 3 * hw
    o_cut = jnp.broadcast_to(cut[:, None, left : left + owh + 128], (nc * wrows, ny, owh + 128))
    up_cut = cut[:, left + owh + 128 :]
    qo = exchange(jnp.concatenate([o_cut, q_cut], -1).transpose(1, 0, 2), "y")
    qo = qo.reshape(dprows, owh + 128 + 3 * hw)
    down_pieces = ring_gather(w_down, "x")
    core = ic.astype(jnp.int32).reshape(1)
    span_y = iy.astype(jnp.int32).reshape(1)

    qo_z = ring_gather(qo, "z")
    up_z = ring_gather(up_cut, "z")
    tok_y = ring_gather(after(tok, qo), "y")
    tok_all = []
    for item in tok_y:
        item = item if not tok_all else after(item, *qo_z)
        tok_all.append(item)
        tok_all.append(shift(item, "c"))
    qo_w, up_w, down_w = [], [], []
    up_at, down_at = [], []
    for step, item in enumerate(qo_z):
        for far, piece in enumerate(ring_gather(item, "x")):
            qo_w.append(piece)
            up_at.append(back("z", step) * nx + back("x", far))
    up_use = [after(up_z[0], qo)] + [after(item, *middle(qo_z)) for item in up_z[1:]]
    up_use[half] = after(up_use[half], qo_z[half])
    up_y = []
    for item in up_use:
        pieces = ring_gather(item, "y")
        pieces = pieces[:1] + [after(piece, *qo_w) for piece in pieces[1:]]
        up_y.append(in_order(pieces, "y").reshape(dprows, ffh))
        up_w += ring_gather(up_y[-1], "x")
    down_pieces = [down_pieces[0]] + [after(item, *qo_z) for item in down_pieces[1:]]
    down_z = ring_gather(in_order(down_pieces, "x").reshape(nx * ffrows, width), "z")
    for step, item in enumerate(down_z):
        for far, piece in enumerate(ring_gather(item, "y")):
            down_w.append(piece)
            down_at.append(back("z", step) * ny + back("y", far))
    up_at = jnp.stack(up_at).astype(jnp.int32)
    down_at = jnp.stack(down_at).astype(jnp.int32)
    q_w, o_w, q_off = qo_w, qo_w, owh + 128
    if hw % 128:
        q_w, o_w, q_off = [p[:, owh + 128 :] for p in qo_w], [p[:, : owh + 128] for p in qo_w], 0
    nqo, nup, ndown = len(qo_w), len(up_w), len(down_w)

    order = after(block_order, *middle(qo_z))[0].reshape(ny, nc)
    places = []
    for sy in range(ny):
        for sc in range(nc):
            places.append(take(take(order, back("y", sy)), back("c", sc)))
    places = jnp.stack(places)
    ranks = jnp.arange(spans, dtype=jnp.int32)
    sorted_at = jnp.sum(jnp.where(places[None, :] == ranks[:, None], ranks[None, :], 0), -1)
    offsets = jnp.arange(rows_here, dtype=jnp.int32)
    positions = (places[:, None] * rows_here + offsets[None, :]).reshape(length)
    lane = jnp.arange(lanes, dtype=jnp.int32)
    frequency = jnp.exp((lane % (HD // 2)).astype(F32) * (-2.0 * math.log(10000.0) / HD))
    angles = positions.astype(F32)[:, None] * frequency[None, :]
    cos_lanes = jnp.cos(angles)
    sin_lanes = jnp.sin(angles) * jnp.where(lane % HD < HD // 2, -1.0, 1.0)

    a1, qkv, norms = call(
        functools.partial(input_kernel, nqo, spans, lanes, q_off, owh),
        (shaped((length, width), BF16), shaped((length, 3 * hw), BF16), shaped((8, width), F32)),
        [IN_SMEM] + [IN_VMEM] * (2 + spans) + [ANYWHERE] * (2 * nqo),
        [pltpu.VMEM((width, 3 * hw), BF16), pltpu.VMEM((width, 128), BF16), sems(2 * nqo)],
    )(up_at, cos_lanes, sin_lanes, *tok_all, *q_w, *o_w)
    qkv_now = after(qkv, *middle(down_z))
    attn, lse = call(
        functools.partial(attend_kernel, spans, lanes),
        (shaped((length, hw), BF16), shaped((mine, length, 128), F32)),
        [IN_SMEM, IN_VMEM],
    )(sorted_at, qkv_now)

    attn_now = after(attn, *(up_y[half : half + 1] + down_w[:ny]))
    sent = attn_now.reshape(ny, nc, rows_here, hw)
    o_near = [sent[0]] + [shift(sent[sy], "y", ny - sy) for sy in range(1, ny)]
    o_far = [shift(item, "c") for item in o_near]
    o_near[0] = after(o_near[0], *([down_z[half]] + up_w[: 2 * nx] + up_w[-nx:]))
    r_keep, r_send, o_chip = call(
        functools.partial(out_kernel, nqo, ny),
        (shaped((rows_here, owh), F32), shaped((rows_here, owh), F32), shaped((crow, width), BF16)),
        [IN_SMEM, IN_SMEM] + [IN_VMEM] * (2 * ny) + [IN_SMEM] + [ANYWHERE] * nqo,
        [pltpu.VMEM((width, owh), BF16), sems(nqo)],
    )(up_at, core, *o_near, *o_far, span_y, *o_w)
    r_send = after(r_send, *(down_w[ny : 2 * ny] + down_w[-ny:] + up_w[half * nx : half * nx + nx]))
    r_got = shift(r_send, "c")
    h, a2 = call(
        middle_kernel,
        (shaped((rows_here, width), F32), shaped((rows_here, width), BF16)),
        [IN_SMEM] + [IN_VMEM] * 4,
        [pltpu.VMEM((rows_here, width), F32)],
    )(core, r_keep, r_got, tok, norms)
    a2 = after(a2)
    a2_got = shift(a2, "c")
    m_keep, m_send, u, slope = call(
        functools.partial(mlp_kernel, nup, ndown),
        (
            shaped((rows_here, width), F32),
            shaped((rows_here, width), BF16),
            shaped((crow, ffh), BF16),
            shaped((crow, ffh), BF16),
        ),
        [IN_SMEM, IN_SMEM, IN_VMEM, IN_VMEM] + [IN_HBM] * (nup + ndown),
        [pltpu.VMEM((width, ffh), BF16), pltpu.VMEM((ffh, width), BF16), sems(nup + ndown)],
        vmem=56,
    )(up_at, down_at, a2, a2_got, *up_w, *down_w)
    m_got = shift(m_send, "c")
    match = group_ids[:, None] == jnp.arange(group_weight.shape[0], dtype=jnp.int32)[None, :]
    scale = jnp.sum(jnp.where(match, group_weight[None, :], 0.0)).reshape(1)
    out_tokens, dm, grads_3 = call(
        top_kernel,
        (shaped((rows_here, width), BF16), shaped((rows_here, width), BF16), shaped((2, width), F32)),
        [IN_SMEM] + [IN_VMEM] * 5,
    )(scale, m_keep, m_got, h, cot, norms)

    dm_got = shift(dm, "c")
    down_own, down_got = [None] * nz, [None] * nz
    up_own, up_got = [None] * nz, [None] * nz
    early, late = late_last(nz)[:2], late_last(nz)[2:]

    def down_block(step, right, *when):
        blocks = grads(u, [right, dm_got], down_at, nx * ffrows, range(step * ny, step * ny + ny))
        down_own[step] = blocks[0]
        down_got[step] = [shift(after(blocks[far], *when), "y", ny - far) for far in range(1, ny)]

    def up_block(step, right):
        blocks = grads(a2_all, [right], up_at, dprows, range(step * nx, step * nx + nx))
        up_own[step] = blocks[0]
        up_got[step] = [shift(blocks[far], "x", nx - far) for far in range(1, nx)]

    right = dm
    for step in early:
        down_block(step, right, right)
        right = after(dm, down_own[step])
    blocks = [down_own[early[-1]]]
    dm = after(dm, blocks[0])
    da_keep, da_send, dz = call(
        functools.partial(mlp_back_kernel, nup, ndown),
        (
            shaped((rows_here, width), F32),
            shaped((rows_here, width), BF16),
            shaped((crow, ffh), BF16),
        ),
        [IN_SMEM, IN_SMEM, IN_VMEM, IN_VMEM, IN_VMEM] + [IN_HBM] * (nup + ndown),
        [pltpu.VMEM((width, ffh), BF16), pltpu.VMEM((ffh, width), BF16), sems(nup + ndown)],
        vmem=56,
    )(up_at, down_at, dm, dm_got, slope, *up_w, *down_w)
    da_got = shift(da_send, "c")
    a2_all = jnp.concatenate([a2, a2_got], 0)
    right = after(dz, *down_got[early[0]])
    for step in early + late:
        up_block(step, right)
        right = after(dz, up_own[step])
    blocks = [up_own[early[-1]]]
    da_keep = after(da_keep, blocks[0])
    dh, dr, dr_send, grads_21 = call(
        between_kernel,
        (
            shaped((rows_here, width), F32),
            shaped((rows_here, owh), BF16),
            shaped((rows_here, owh), BF16),
            shaped((4, width), F32),
        ),
        [IN_SMEM, IN_SMEM] + [IN_VMEM] * 7,
        [pltpu.VMEM((rows_here, width), F32), pltpu.VMEM((rows_here, width), BF16)],
    )(core, scale, da_keep, da_got, h, r_keep, r_got, cot, norms)
    dr_send = after(dr_send, *down_got[early[1]])
    dr_got = shift(dr_send, "c")
    do_keep, do_send = call(
        functools.partial(out_back_kernel, nqo, ny),
        (shaped((ny, crow, hw), F32), shaped((ny, crow, hw), BF16)),
        [IN_SMEM, IN_SMEM, IN_VMEM, IN_VMEM] + [ANYWHERE] * nqo,
        [pltpu.VMEM((width, owh), BF16), sems(nqo)],
    )(up_at, core, dr, dr_got, *o_w)
    do_got = shift(do_send, "c")
    do_got = jnp.concatenate([do_got[:, rows_here:], do_got[:, :rows_here]], 1)
    do = (do_keep + do_got.astype(F32)).astype(BF16)
    parts = []
    for sy in range(ny):
        item = take(do, lax.rem(iy + sy, ny))
        parts.append(item if sy == 0 else shift(item, "y", sy))
    do_all = jnp.concatenate(parts, 0)
    down_y, up_x = [None] * nz, [None] * nz
    right = after(dm, do)
    down_block(late[0], right, do_all)
    for step in late[1:]:
        down_block(step, after(dm, do), do_all)
    for step in early:
        down_y[step] = add_parts(down_own[step], down_got[step], do)
        up_x[step] = add_parts(up_own[step], up_got[step], do_all)
    out_own, out_send = stacked_grads(o_chip, [dr, dr_got], up_at, dprows)
    out_got = shift(out_send, "x")

    down_first = ring_first(down_y, "z")
    sums = [None] * nz
    for step in early:
        own_y, got_y = send_parts(up_x[step].reshape(ny, nc * wrows, ffh), "y")
        sums[step] = add_parts(own_y, got_y, do_all)
    up_first = ring_first(sums, "z")
    do_all = after(do_all, *[t for t in down_y + up_x + down_own + up_own if t is not None])
    dqkv = call(
        functools.partial(attend_back_kernel, spans, lanes),
        shaped((length, 3 * hw), BF16),
        [IN_SMEM] + [IN_VMEM] * 6,
        [pltpu.VMEM((length, lanes), F32)] * 2,
        vmem=20,
    )(sorted_at, qkv, attn, do_all, lse, cos_lanes, sin_lanes)
    dqkv = after(dqkv, *([t for step in late for t in down_got[step] + up_got[step]] + [sums[step] for step in early]))
    qkv_own, qkv_send = stacked_grads(a1, [dqkv], up_at, dprows)
    qkv_got = shift(qkv_send, "x")
    da1_keep, da1_send = call(
        functools.partial(input_back_kernel, nqo, q_off),
        (shaped((ny, rows_here, width), F32), shaped((ny, rows_here, width), BF16)),
        [IN_SMEM, IN_VMEM] + [ANYWHERE] * nqo,
        [pltpu.VMEM((width, 3 * hw), BF16), sems(nqo)],
    )(up_at, after(dqkv, qkv_own, *down_first), *q_w)
    da1_got = shift(da1_send, "c")
    arrived = [
        shift((da1_keep[sy] + da1_got[sy].astype(F32)).astype(BF16), "y", ny - sy) for sy in range(1, ny)
    ]
    da1_keep = after(da1_keep, *up_first)
    grad_tokens, grads_0 = call(
        bottom_kernel,
        (shaped((rows_here, width), BF16), shaped((2, width), F32)),
        [IN_VMEM] * (5 + len(arrived)),
    )(tok, dh, norms, da1_keep[0], da1_got[0], *arrived)
    grad_tokens = grad_tokens.reshape(tokens.shape)
    out_tokens = out_tokens.reshape(tokens.shape)

    for step in range(nz):
        if down_y[step] is None:
            down_y[step] = add_parts(down_own[step], down_got[step], da1_got)
    down = ring_rest(down_y, down_first, "z").astype(BF16)
    down = scatter_sum(down.reshape(nx, ffrows, width), "x")
    for step in late:
        part = add_parts(up_own[step], up_got[step], dqkv)
        own_y, got_y = send_parts(part.reshape(ny, nc * wrows, ffh), "y")
        sums[step] = add_parts(own_y, got_y, arrived[0])
    up = ring_rest(sums, up_first, "z").reshape(nc, wrows, ffh)
    up = pair(take(up, ic), shift(take(up, 1 - ic), "c"), ic)
    up = up.reshape(nc, wrows, nz, ny, nx, ffrows).transpose(1, 2, 4, 3, 0, 5).reshape(wrows, ff)

    out_x = add_parts(out_own, [out_got], da1_got)
    qkv_x = (qkv_own.astype(F32) + qkv_got.astype(F32)).astype(BF16)
    both = jnp.concatenate([out_x, qkv_x], -1)
    both = ring_scatter([both[step] for step in range(nz)], "z").astype(BF16)
    out, qkv_g = both[:, :owh], both[:, owh:]
    out = scatter_sum(out.reshape(ny, nc * wrows, owh), "y").reshape(nc, wrows, owh)
    out = pair(take(out, ic), shift(take(out, 1 - ic), "c"), ic)
    out = out.transpose(1, 0, 2).reshape(wrows, width)
    qkv_g = exchange(qkv_g.reshape(ny, nc * wrows, 3 * hw), "y")
    qkv_g = qkv_g.reshape(ny, nc, wrows, 3 * hw).transpose(1, 0, 2, 3)
    qkv_g = pair(take(qkv_g, ic), shift(take(qkv_g, 1 - ic), "c"), ic)
    qkv_g = qkv_g.reshape(nc, ny, wrows, 3, hw).transpose(2, 3, 1, 0, 4)
    qkv_g = qkv_g.reshape(wrows, 3 * width).astype(F32)

    norm_sums = jnp.concatenate(
        [
            grads_0[0:1],
            grads_21[2:3],
            grads_21[0:1],
            grads_3[0:1],
            grads_0[1:2],
            grads_21[3:4],
            grads_21[1:2],
            grads_3[1:2],
        ],
        0,
    )
    for axis in "cyxz":
        norm_sums = all_sum(norm_sums, axis)
    place = ((iz * nx + ix) * ny + iy) * nc + ic
    norm_sums = lax.dynamic_slice(norm_sums, (0, place * wrows), (8, wrows))
    return (out_tokens, grad_tokens, qkv_g, out, up, down, norm_sums[:4], norm_sums[4:])


def solution(mesh):
    fine = Mesh(
        mesh.devices.reshape(mesh.shape["dp"] // 2, 2, mesh.shape["blk"] // 2, 2),
        ("z", "x", "y", "c"),
    )
    dp, blk, every = ("z", "x"), ("y", "c"), ("z", "x", "y", "c")
    return jax.shard_map(
        on_device,
        mesh=fine,
        in_specs=(
            P(blk, dp, None),
            P(blk, dp, None),
            P(dp),
            P(),
            P(dp, None),
            P(every, None),
            P(every, None),
            P(every, None),
            P(every, None),
            P(None, every),
            P(None, every),
        ),
        out_specs=(
            P(blk, dp, None),
            P(blk, dp, None),
            P(every, None),
            P(every, None),
            P(every, None),
            P(every, None),
            P(None, every),
            P(None, every),
        ),
        check_vma=False,
    )
```

```python
import functools
import math

import jax
import jax.numpy as jnp
from jax import lax
from jax.experimental import pallas as pl
from jax.experimental.pallas import tpu as pltpu
from jax.sharding import Mesh
from jax.sharding import PartitionSpec as P

HD = 64
F32 = jnp.float32
BF16 = jnp.bfloat16


def shift(value, axis, step=1):
    size = lax.axis_size(axis)
    return lax.ppermute(value, axis, [(i, (i + step) % size) for i in range(size)])


def after(value, *others):
    return lax.optimization_barrier((value,) + others)[0]


def back(axis, step):
    size = lax.axis_size(axis)
    return lax.rem(lax.axis_index(axis) + size - step, size)


def take(array, at, axis=0):
    return lax.dynamic_index_in_dim(array, at, axis, keepdims=False)


def direct_gather(piece, axis):
    size = lax.axis_size(axis)
    return [piece] + [shift(piece, axis, step) for step in range(1, size)]


def ring_gather(piece, axis, gate=()):
    size = lax.axis_size(axis)
    pieces = [piece] * size
    for step in range(1, size // 2 + 1):
        last = pieces[step - 1]
        pieces[step] = shift(after(last, *gate) if gate and step > 1 else last, axis)
    for step in range(size - 1, size // 2, -1):
        last = pieces[(step + 1) % size]
        pieces[step] = shift(after(last, *gate) if gate and step < size - 1 else last, axis, -1)
    return pieces


def in_order(pieces, axis):
    if len(pieces) == 2:
        return pair(pieces[0], pieces[1], lax.axis_index(axis))
    buffer = jnp.zeros((len(pieces),) + pieces[0].shape, pieces[0].dtype)
    for step, piece in enumerate(pieces):
        at = (back(axis, step),) + (0,) * piece.ndim
        buffer = lax.dynamic_update_slice(buffer, piece[None], at)
    return buffer


def pair(own, other, index):
    first = jnp.where(index == 0, own, other)
    second = jnp.where(index == 0, other, own)
    return jnp.stack([first, second])


def ring_first(parts, axis):
    size = len(parts)
    half = size // 2
    found = [shift(parts[half].astype(BF16), axis)]
    if size - 1 - half:
        found.append(shift(parts[size - 1 - half].astype(BF16), axis, -1))
    return found


def ring_rest(parts, arrived, axis):
    size = len(parts)
    half = size // 2
    total = parts[0].astype(F32)
    for carry, count, way in zip(arrived, (half, size - 1 - half), (1, -1)):
        for far in range(count - 1, 0, -1):
            part = parts[size - far if way == 1 else far]
            carry = shift((carry.astype(F32) + part.astype(F32)).astype(BF16), axis, way)
        total = total + carry.astype(F32)
    return total


def ring_scatter(parts, axis):
    return ring_rest(parts, ring_first(parts, axis), axis)


def scatter_sum(parts, axis):
    size = parts.shape[0]
    return ring_scatter([take(parts, back(axis, step)) for step in range(size)], axis)


def late_last(size):
    half = size // 2
    steps = list(range(half, 0, -1)) + list(range(half + 1, size)) + [0]
    return list(dict.fromkeys(steps))


def send_parts(parts, axis):
    size = parts.shape[0]
    got = [shift(take(parts, back(axis, step)), axis, size - step) for step in range(1, size)]
    return take(parts, lax.axis_index(axis)), got


def add_parts(own, got, when):
    total = own.astype(F32)
    for item in got:
        total = total + after(item, when).astype(F32)
    return total.astype(BF16)


def exchange(parts, axis):
    size = parts.shape[0]
    index = lax.axis_index(axis)
    pieces = [take(parts, index)]
    for step in range(1, size):
        pieces.append(shift(take(parts, lax.rem(index + step, size)), axis, step))
    return in_order(pieces, axis)


def all_sum(value, axis):
    pieces = direct_gather(value, axis)
    total = pieces[0]
    for piece in pieces[1:]:
        total = total + piece
    return total


IN_VMEM = pl.BlockSpec(memory_space=pltpu.VMEM)
IN_SMEM = pl.BlockSpec(memory_space=pltpu.SMEM)
ANYWHERE = pl.BlockSpec(memory_space=pl.ANY)
IN_HBM = pl.BlockSpec(memory_space=pltpu.HBM)


def call(kernel, out_shape, in_specs, scratch=(), vmem=16):
    several = isinstance(out_shape, (tuple, list))
    return pl.pallas_call(
        kernel,
        out_shape=out_shape,
        in_specs=in_specs,
        out_specs=[IN_VMEM] * len(out_shape) if several else IN_VMEM,
        scratch_shapes=list(scratch),
        compiler_params=pltpu.CompilerParams(vmem_limit_bytes=vmem * 1024 * 1024),
        cost_estimate=pl.CostEstimate(flops=1024, bytes_accessed=1024, transcendentals=0),
    )


def fetch(pieces, at_ref, target, sems, first, offset=0, columns=None):
    copies = []
    for number, piece in enumerate(pieces):
        rows = piece.shape[0]
        source = piece if columns is None else piece.at[:, pl.ds(offset, columns)]
        place = pl.ds(pl.multiple_of(at_ref[number] * rows, rows), rows)
        copies.append(pltpu.make_async_copy(source, target.at[place], sems.at[first + number]))
    for copy in copies:
        copy.start()
    return copies


def wait_all(copies):
    for copy in copies:
        copy.wait()


def partner(values):
    half = HD // 2
    if values.shape[-1] == HD:
        return jnp.concatenate([values[:, half:], values[:, :half]], -1)
    lanes = values.shape[-1]
    lane = lax.broadcasted_iota(jnp.int32, values.shape, 1)
    low = lax.rem(lane, HD) < half
    return jnp.where(low, pltpu.roll(values, lanes - half, 1), pltpu.roll(values, half, 1))


def attend_kernel(blocks, lanes, order_ref, qkv_ref, o_ref, lse_ref):
    length, third = o_ref.shape
    size = length // blocks
    per = lanes // HD
    lane = lax.broadcasted_iota(jnp.int32, (1, lanes), 1) // HD
    row = lax.broadcasted_iota(jnp.int32, (size, size), 0)
    col = lax.broadcasted_iota(jnp.int32, (size, size), 1)
    for group in range(third // lanes):
        left = group * lanes

        def one_row(i):
            at = pl.multiple_of(order_ref[i] * size, size)
            q = qkv_ref[pl.ds(at, size), left : left + lanes]
            outs, totals = [], []
            for head in range(per):
                qh = q * (lane == head).astype(BF16)

                def scores(start):
                    k = qkv_ref[pl.ds(start, size), third + left : third + left + lanes]
                    return lax.dot_general(qh, k, (((1,), (1,)), ((), ())), preferred_element_type=F32)

                def values(p, start):
                    v = qkv_ref[pl.ds(start, size), 2 * third + left : 2 * third + left + lanes]
                    return jnp.dot(p.astype(BF16), v, preferred_element_type=F32)

                s = jnp.where(col <= row, scores(at), -1e30)
                top = jnp.max(s, -1, keepdims=True)
                p = jnp.exp(s - top)
                state = (top, jnp.sum(p, -1, keepdims=True), values(p, at))

                def step(j, state):
                    top, total, acc = state
                    start = pl.multiple_of(order_ref[j] * size, size)
                    s = scores(start)
                    new = jnp.maximum(top, jnp.max(s, -1, keepdims=True))
                    factor = jnp.exp(top - new)
                    p = jnp.exp(s - new)
                    total = total * factor + jnp.sum(p, -1, keepdims=True)
                    return new, total, acc * factor + values(p, start)

                if blocks <= 4:
                    for j in range(i):
                        state = step(j, state)
                else:
                    state = lax.fori_loop(0, i, step, state)
                top, total, acc = state
                outs.append(acc / total)
                lse = jnp.broadcast_to(top + jnp.log(total), (size, 128))
                lse_ref[group * per + head, pl.ds(at, size), :] = lse
            out = outs[0]
            for head in range(1, per):
                out = jnp.where(lane == head, outs[head], out)
            o_ref[pl.ds(at, size), left : left + lanes] = out.astype(BF16)

        if blocks <= 4:
            for i in range(blocks):
                one_row(i)
        else:
            pl.loop(0, blocks)(one_row)


def attend_back_kernel(
    blocks, lanes, order_ref, qkv_ref, o_ref, do_ref, lse_ref, cos_ref, sin_ref, out_ref, dk_ref, dv_ref
):
    length, third = o_ref.shape
    size = length // blocks
    per = lanes // HD
    lane = lax.broadcasted_iota(jnp.int32, (1, lanes), 1) // HD
    row = lax.broadcasted_iota(jnp.int32, (size, size), 0)
    col = lax.broadcasted_iota(jnp.int32, (size, size), 1)
    nt = (((1,), (1,)), ((), ()))
    tn = (((0,), (0,)), ((), ()))

    def unturn(values, rows):
        return values * cos_ref[rows, :] - partner(values) * sin_ref[rows, :]

    for group in range(third // lanes):
        left = group * lanes
        dk_ref[...] = jnp.zeros_like(dk_ref)
        dv_ref[...] = jnp.zeros_like(dv_ref)

        def one_row(i):
            at = pl.multiple_of(order_ref[i] * size, size)
            rows = pl.ds(at, size)
            q = qkv_ref[rows, left : left + lanes]
            do = do_ref[rows, left : left + lanes]
            prod = do.astype(F32) * o_ref[rows, left : left + lanes].astype(F32)
            grads = []
            for head in range(per):
                own = (lane == head).astype(BF16)
                qh, doh = q * own, do * own
                delta = jnp.sum(jnp.where(lane == head, prod, 0.0), -1, keepdims=True)
                lse = lse_ref[group * per + head, rows, 0:1]

                def step(start, diagonal):
                    where = pl.ds(start, size)
                    k = qkv_ref[where, third + left : third + left + lanes]
                    v = qkv_ref[where, 2 * third + left : 2 * third + left + lanes]
                    s = lax.dot_general(qh, k, nt, preferred_element_type=F32)
                    p = jnp.exp(s - lse)
                    if diagonal:
                        p = jnp.where(col <= row, p, 0.0)
                    dp = lax.dot_general(doh, v, nt, preferred_element_type=F32)
                    ds = (p * (dp - delta)).astype(BF16)
                    dv_ref[where, :] += lax.dot_general(p.astype(BF16), doh, tn, preferred_element_type=F32)
                    dk_ref[where, :] += lax.dot_general(ds, qh, tn, preferred_element_type=F32)
                    return jnp.dot(ds, k, preferred_element_type=F32)

                dq = step(at, True)
                if blocks <= 4:
                    for j in range(i):
                        dq = dq + step(pl.multiple_of(order_ref[j] * size, size), False)
                else:
                    dq = lax.fori_loop(
                        0, i, lambda j, c: c + step(pl.multiple_of(order_ref[j] * size, size), False), dq
                    )
                grads.append(dq)
            dq = grads[0]
            for head in range(1, per):
                dq = jnp.where(lane == head, grads[head], dq)
            out_ref[rows, left : left + lanes] = unturn(dq * 0.125, rows).astype(BF16)

        if blocks <= 4:
            for i in range(blocks):
                one_row(i)
        else:
            pl.loop(0, blocks)(one_row)
        for start in range(0, length, size):
            rows = pl.ds(start, size)
            out_ref[rows, third + left : third + left + lanes] = unturn(dk_ref[rows, :], rows).astype(BF16)
            out_ref[rows, 2 * third + left : 2 * third + left + lanes] = dv_ref[rows, :].astype(BF16)


GELU_A = math.sqrt(2.0 / math.pi)
GELU_B = 0.044715


NT = (((1,), (1,)), ((), ()))
TN = (((0,), (0,)), ((), ()))


def normed(values):
    centred = values - jnp.mean(values, -1, keepdims=True)
    scale = lax.rsqrt(jnp.mean(centred * centred, -1, keepdims=True) + 1e-05)
    return centred * scale, scale


def normed_back(grad, gain, vhat, scale):
    scaled = grad * gain
    return scale * (
        scaled - jnp.mean(scaled, -1, keepdims=True) - vhat * jnp.mean(scaled * vhat, -1, keepdims=True)
    )


def column_sum(values):
    return jnp.sum(values, 0, keepdims=True)


def halves(core_ref, width):
    own = pl.ds(pl.multiple_of(core_ref[0] * width, width), width)
    other = pl.ds(pl.multiple_of((1 - core_ref[0]) * width, width), width)
    return own, other


def input_kernel(count, blocks, lanes, q_off, n_off, at_ref, cos_ref, sin_ref, *refs):
    toks, refs = refs[:blocks], refs[blocks:]
    q_pieces, n_pieces, refs = refs[:count], refs[count : 2 * count], refs[2 * count :]
    a_ref, out_ref, norm_ref, weight, columns, sems = refs
    wide = out_ref.shape[1]
    first = fetch(n_pieces, at_ref, columns, sems, 0, n_off, 128)
    later = fetch(q_pieces, at_ref, weight, sems, count, q_off, wide)
    wait_all(first)
    norm_ref[...] = jnp.transpose(columns[...].astype(F32))[:8, :]
    gain, bias = norm_ref[0:1, :], norm_ref[4:5, :]
    rows_here = toks[0].shape[0]
    for number, tok_ref in enumerate(toks):
        vhat, _ = normed(tok_ref[...].astype(F32))
        a_ref[pl.ds(number * rows_here, rows_here), :] = (vhat * gain + bias).astype(BF16)
    wait_all(later)
    third = wide // 3
    block = 256
    for start in range(0, out_ref.shape[0], block):
        rows = pl.ds(start, block)
        acc = jnp.dot(a_ref[rows, :], weight[...], preferred_element_type=F32)
        cos, sin = cos_ref[rows, :], sin_ref[rows, :]
        for part in range(3):
            for left in range(0, third, lanes):
                at = part * third + left
                values = acc[:, at : at + lanes]
                if part < 2:
                    values = values * cos + partner(values) * sin
                if part == 0:
                    values = values * 0.125
                out_ref[rows, at : at + lanes] = values.astype(BF16)


def out_kernel(count, ny, at_ref, core_ref, *refs):
    near, far, refs = refs[:ny], refs[ny : 2 * ny], refs[2 * ny :]
    y_ref, pieces, refs = refs[0], refs[1 : 1 + count], refs[1 + count :]
    keep_ref, send_ref, chip_ref, weight, sems = refs
    copies = fetch(pieces, at_ref, weight, sems, 0, 0, weight.shape[1])
    core = core_ref[0]
    rows, hw = near[0].shape[1], near[0].shape[2]
    for parts, is_far in ((near, False), (far, True)):
        other = 1 - core if is_far else core
        for ahead in range(ny):
            yh = lax.rem(y_ref[0] + ahead, ny)
            for sc in range(2):
                token = pl.ds(((1 - sc) if is_far else sc) * rows, rows)
                value = parts[ahead][sc]
                if hw % 128 == 0:
                    left = pl.multiple_of((yh * 2 + other) * hw, hw)
                    chip_ref[token, pl.ds(left, hw)] = value
                else:
                    for place in range(2 * ny):

                        @pl.when(yh * 2 + other == place)
                        def _(place=place, value=value, token=token):
                            chip_ref[token, place * hw : place * hw + hw] = value

    wait_all(copies)
    send_ref[...] = jnp.dot(chip_ref[rows:, :], weight[...], preferred_element_type=F32)
    keep_ref[...] = jnp.dot(chip_ref[:rows, :], weight[...], preferred_element_type=F32)


def middle_kernel(core_ref, keep_ref, got_ref, tok_ref, norm_ref, h_ref, a_ref, r_ref):
    own, other = halves(core_ref, keep_ref.shape[1])
    r_ref[:, own] = keep_ref[...]
    r_ref[:, other] = got_ref[...]
    vhat, _ = normed(r_ref[...])
    h = tok_ref[...].astype(F32) + vhat * norm_ref[1:2, :] + norm_ref[5:6, :]
    h_ref[...] = h
    vhat, _ = normed(h)
    a_ref[...] = (vhat * norm_ref[2:3, :] + norm_ref[6:7, :]).astype(BF16)


def mlp_kernel(ups, downs, up_at, down_at, own_ref, got_ref, *refs):
    up_pieces, down_pieces = refs[:ups], refs[ups : ups + downs]
    keep_ref, send_ref, u_ref, slope_ref, up, down, sems = refs[ups + downs :]
    copies = fetch(up_pieces, up_at, up, sems, 0)
    later = fetch(down_pieces, down_at, down, sems, ups)
    wait_all(copies)
    count, wide = own_ref.shape[0], u_ref.shape[1]
    step = min(512, wide)
    for start, a_ref in ((count, got_ref), (0, own_ref)):
        rows = pl.ds(start, count)
        for left in range(0, wide, step):
            z = jnp.dot(a_ref[...], up[:, left : left + step], preferred_element_type=F32)
            square = z * z
            t = jnp.tanh(GELU_A * z * (1.0 + GELU_B * square))
            half = 0.5 * (1.0 + t)
            u_ref[rows, left : left + step] = (z * half).astype(BF16)
            slope = half + 0.5 * z * (1.0 - t * t) * (GELU_A * (1.0 + 3.0 * GELU_B * square))
            slope_ref[rows, left : left + step] = slope.astype(BF16)
    wait_all(later)
    send_ref[...] = jnp.dot(u_ref[count:, :], down[...], preferred_element_type=F32).astype(BF16)
    keep_ref[...] = jnp.dot(u_ref[:count, :], down[...], preferred_element_type=F32)


def top_kernel(scale_ref, keep_ref, got_ref, h_ref, cot_ref, norm_ref, out_ref, dm_ref, grad_ref):
    vhat, scale = normed(keep_ref[...] + got_ref[...].astype(F32))
    gain = norm_ref[3:4, :]
    out_ref[...] = (h_ref[...] + vhat * gain + norm_ref[7:8, :]).astype(BF16)
    g = cot_ref[...].astype(F32) * scale_ref[0]
    dm_ref[...] = normed_back(g, gain, vhat, scale).astype(BF16)
    grad_ref[0:1, :] = column_sum(g * vhat)
    grad_ref[1:2, :] = column_sum(g)


def mlp_back_kernel(ups, downs, up_at, down_at, own_ref, got_ref, slope_ref, *refs):
    up_pieces, down_pieces = refs[:ups], refs[ups : ups + downs]
    keep_ref, send_ref, dz_ref, up, down, sems = refs[ups + downs :]
    copies = fetch(down_pieces, down_at, down, sems, ups)
    later = fetch(up_pieces, up_at, up, sems, 0)
    wait_all(copies)
    count, wide = own_ref.shape[0], dz_ref.shape[1]
    step = min(512, wide)
    for start, dm_ref in ((count, got_ref), (0, own_ref)):
        rows = pl.ds(start, count)
        for left in range(0, wide, step):
            du = lax.dot_general(dm_ref[...], down[left : left + step, :], NT, preferred_element_type=F32)
            slope = slope_ref[rows, left : left + step].astype(F32)
            dz_ref[rows, left : left + step] = (du * slope).astype(BF16)
    wait_all(later)
    send = lax.dot_general(dz_ref[count:, :], up[...], NT, preferred_element_type=F32)
    send_ref[...] = send.astype(BF16)
    keep_ref[...] = lax.dot_general(dz_ref[:count, :], up[...], NT, preferred_element_type=F32)


def between_kernel(
    core_ref, scale_ref, da_ref, da_got_ref, h_ref, keep_ref, got_ref, cot_ref, norm_ref,
    dh_ref, own_ref, send_ref, grad_ref, r_ref, dr_ref,
):
    own, other = halves(core_ref, keep_ref.shape[1])
    r_ref[:, own] = keep_ref[...]
    r_ref[:, other] = got_ref[...]
    e = da_ref[...] + da_got_ref[...].astype(F32)
    vhat, scale = normed(h_ref[...])
    grad_ref[0:1, :] = column_sum(e * vhat)
    grad_ref[1:2, :] = column_sum(e)
    g = cot_ref[...].astype(F32) * scale_ref[0]
    dh = g + normed_back(e, norm_ref[2:3, :], vhat, scale)
    dh_ref[...] = dh
    vhat, scale = normed(r_ref[...])
    grad_ref[2:3, :] = column_sum(dh * vhat)
    grad_ref[3:4, :] = column_sum(dh)
    dr_ref[...] = normed_back(dh, norm_ref[1:2, :], vhat, scale).astype(BF16)
    own_ref[...] = dr_ref[:, own]
    send_ref[...] = dr_ref[:, other]


def out_back_kernel(count, ny, at_ref, core_ref, own_ref, got_ref, *refs):
    pieces = refs[:count]
    keep_ref, send_ref, weight, sems = refs[count:]
    wait_all(fetch(pieces, at_ref, weight, sems, 0, 0, weight.shape[1]))
    core = core_ref[0]
    hw = keep_ref.shape[2]
    size = own_ref.shape[0]
    for own in (False, True):
        head = core if own else 1 - core
        for yh in range(ny):
            rows = pl.ds(pl.multiple_of((yh * 2 + head) * hw, hw), hw)
            for start, dr_ref in ((0, own_ref), (size, got_ref)):
                value = lax.dot_general(dr_ref[...], weight[rows, :], NT, preferred_element_type=F32)
                if own:
                    keep_ref[yh, pl.ds(start, size), :] = value
                else:
                    send_ref[yh, pl.ds(start, size), :] = value.astype(BF16)


def input_back_kernel(count, offset, at_ref, a_ref, *refs):
    pieces = refs[:count]
    keep_ref, send_ref, weight, sems = refs[count:]
    wait_all(fetch(pieces, at_ref, weight, sems, 0, offset, weight.shape[1]))
    block = keep_ref.shape[1]
    for number in range(a_ref.shape[0] // block):
        rows = pl.ds(number * block, block)
        value = lax.dot_general(a_ref[rows, :], weight[...], NT, preferred_element_type=F32)
        if number % 2 == 0:
            keep_ref[number // 2] = value
        else:
            send_ref[number // 2] = value.astype(BF16)


def bottom_kernel(*refs):
    tok_ref, dh_ref, norm_ref = refs[:3]
    pieces, (out_ref, grad_ref) = refs[3:-2], refs[-2:]
    e = pieces[0][...].astype(F32)
    for piece in pieces[1:]:
        e = e + piece[...].astype(F32)
    vhat, scale = normed(tok_ref[...].astype(F32))
    out_ref[...] = (dh_ref[...] + normed_back(e, norm_ref[0:1, :], vhat, scale)).astype(BF16)
    grad_ref[0:1, :] = column_sum(e * vhat)
    grad_ref[1:2, :] = column_sum(e)


def stacked_kernel(parts, cols, at_ref, left_ref, *refs):
    rights, (own_ref, send_ref) = refs[:parts], refs[parts:]
    size = rights[0].shape[0]
    for number in range(2 * own_ref.shape[0]):
        columns = pl.ds(pl.multiple_of(at_ref[number] * cols, cols), cols)
        total = None
        for place, right in enumerate(rights):
            left = left_ref[place * size : place * size + size, columns]
            value = lax.dot_general(left, right[...], TN, preferred_element_type=F32)
            total = value if total is None else total + value
        target = send_ref if number % 2 else own_ref
        target[number // 2] = total.astype(BF16)


def stacked_grads(left, rights, at, cols):
    wide, count = rights[0].shape[1], left.shape[1] // cols // 2
    if cols % 128:
        blocks = grads(left, rights, at, cols, range(2 * count))
        return jnp.stack(blocks[0::2]), jnp.stack(blocks[1::2])
    return call(
        functools.partial(stacked_kernel, len(rights), cols),
        [jax.ShapeDtypeStruct((count, cols, wide), BF16)] * 2,
        [IN_SMEM] + [IN_VMEM] * (1 + len(rights)),
    )(at, left, *rights)


def blocks_kernel(parts, cols, numbers, at_ref, left_ref, *refs):
    rights, outs = refs[:parts], refs[parts:]
    size = rights[0].shape[0]
    for number, out_ref in zip(numbers, outs):
        columns = pl.ds(pl.multiple_of(at_ref[number] * cols, cols), cols)
        total = None
        for place, right in enumerate(rights):
            left = left_ref[place * size : place * size + size, columns]
            value = lax.dot_general(left, right[...], TN, preferred_element_type=F32)
            total = value if total is None else total + value
        out_ref[...] = total.astype(BF16)


def grads(left, rights, at, cols, numbers):
    if cols % 128 == 0:
        return call(
            functools.partial(blocks_kernel, len(rights), cols, tuple(numbers)),
            [jax.ShapeDtypeStruct((cols, rights[0].shape[1]), BF16)] * len(numbers),
            [IN_SMEM] + [IN_VMEM] * (1 + len(rights)),
        )(at, left, *rights)
    right = jnp.concatenate(rights, 0)
    found = []
    for number in numbers:
        block = lax.dynamic_slice(left, (0, at[number] * cols), (left.shape[0], cols))
        found.append(lax.dot_general(block, right, TN, preferred_element_type=F32).astype(BF16))
    return found


def on_device(
    tokens,
    cotangent,
    group_ids,
    group_weight,
    block_order,
    w_qkv,
    w_out,
    w_up,
    w_down,
    norm_gain,
    norm_bias,
):
    nz, nx, ny, nc = (lax.axis_size(a) for a in "zxyc")
    iz, ix, iy, ic = (lax.axis_index(a) for a in "zxyc")
    rows_here, _, width = tokens.shape
    heads = width // HD
    spans = ny * nc
    mine = heads // spans
    hw = mine * HD
    lanes = min(128, hw)
    wrows = w_qkv.shape[0]
    ffrows = w_down.shape[0]
    ff = w_up.shape[1]
    ffh = ff // nc
    owh = width // nc
    dprows = spans * wrows
    length = spans * rows_here
    crow = nc * rows_here
    half = nz // 2
    shaped = jax.ShapeDtypeStruct

    def middle(pieces):
        return pieces[1:2] + pieces[-1:]

    def sems(count):
        return pltpu.SemaphoreType.DMA((count,))

    tok = tokens.reshape(rows_here, width)
    cot = cotangent.reshape(rows_here, width)
    norm_rows = jnp.concatenate([norm_gain, norm_bias], 0).T
    norm_rows = jnp.pad(norm_rows, ((0, 0), (0, 120)))
    norm_rows = jnp.broadcast_to(norm_rows[None], (nc, wrows, 128))
    cut = jnp.concatenate(
        [
            w_qkv.reshape(wrows, 3, ny, nc, hw).transpose(3, 0, 2, 1, 4).reshape(nc, wrows, ny * 3 * hw),
            w_out.reshape(wrows, nc, owh).transpose(1, 0, 2),
            norm_rows,
            w_up.reshape(wrows, nz, nx, ny, nc, ffrows).transpose(4, 0, 1, 3, 2, 5).reshape(nc, wrows, ffh),
        ],
        -1,
    )
    cut = pair(take(cut, ic), shift(take(cut, 1 - ic), "c"), ic).reshape(nc * wrows, -1)
    q_cut = cut[:, : ny * 3 * hw].reshape(nc * wrows, ny, 3 * hw)
    left = ny * 3 * hw
    o_cut = jnp.broadcast_to(cut[:, None, left : left + owh + 128], (nc * wrows, ny, owh + 128))
    up_cut = cut[:, left + owh + 128 :]
    qo = exchange(jnp.concatenate([o_cut, q_cut], -1).transpose(1, 0, 2), "y")
    qo = qo.reshape(dprows, owh + 128 + 3 * hw)
    down_pieces = ring_gather(w_down, "x")
    core = ic.astype(jnp.int32).reshape(1)
    span_y = iy.astype(jnp.int32).reshape(1)

    qo_z = ring_gather(qo, "z")
    up_z = ring_gather(up_cut, "z")
    tok_y = ring_gather(after(tok, qo), "y")
    tok_all = []
    for item in tok_y:
        item = item if not tok_all else after(item, *qo_z)
        tok_all.append(item)
        tok_all.append(shift(item, "c"))
    qo_w, up_w, down_w = [], [], []
    up_at, down_at = [], []
    for step, item in enumerate(qo_z):
        for far, piece in enumerate(ring_gather(item, "x")):
            qo_w.append(piece)
            up_at.append(back("z", step) * nx + back("x", far))
    up_use = [after(up_z[0], qo)] + [after(item, *middle(qo_z)) for item in up_z[1:]]
    up_use[half] = after(up_use[half], qo_z[half])
    up_y = []
    for item in up_use:
        pieces = ring_gather(item, "y")
        pieces = pieces[:1] + [after(piece, *qo_w) for piece in pieces[1:]]
        up_y.append(in_order(pieces, "y").reshape(dprows, ffh))
        up_w += ring_gather(up_y[-1], "x")
    down_pieces = [down_pieces[0]] + [after(item, *qo_z) for item in down_pieces[1:]]
    down_z = ring_gather(in_order(down_pieces, "x").reshape(nx * ffrows, width), "z")
    for step, item in enumerate(down_z):
        for far, piece in enumerate(ring_gather(item, "y")):
            down_w.append(piece)
            down_at.append(back("z", step) * ny + back("y", far))
    up_at = jnp.stack(up_at).astype(jnp.int32)
    down_at = jnp.stack(down_at).astype(jnp.int32)
    q_w, o_w, q_off = qo_w, qo_w, owh + 128
    if hw % 128:
        q_w, o_w, q_off = [p[:, owh + 128 :] for p in qo_w], [p[:, : owh + 128] for p in qo_w], 0
    nqo, nup, ndown = len(qo_w), len(up_w), len(down_w)
    up_w, down_w, q_back, o_back = (
        [pltpu.with_memory_space_constraint(piece, pltpu.HBM) for piece in pieces]
        for pieces in (up_w, down_w, q_w, o_w)
    )

    order = after(block_order, *middle(qo_z))[0].reshape(ny, nc)
    places = []
    for sy in range(ny):
        for sc in range(nc):
            places.append(take(take(order, back("y", sy)), back("c", sc)))
    places = jnp.stack(places)
    ranks = jnp.arange(spans, dtype=jnp.int32)
    sorted_at = jnp.sum(jnp.where(places[None, :] == ranks[:, None], ranks[None, :], 0), -1)
    offsets = jnp.arange(rows_here, dtype=jnp.int32)
    positions = (places[:, None] * rows_here + offsets[None, :]).reshape(length)
    lane = jnp.arange(lanes, dtype=jnp.int32)
    frequency = jnp.exp((lane % (HD // 2)).astype(F32) * (-2.0 * math.log(10000.0) / HD))
    angles = positions.astype(F32)[:, None] * frequency[None, :]
    cos_lanes = jnp.cos(angles)
    sin_lanes = jnp.sin(angles) * jnp.where(lane % HD < HD // 2, -1.0, 1.0)

    a1, qkv, norms = call(
        functools.partial(input_kernel, nqo, spans, lanes, q_off, owh),
        (shaped((length, width), BF16), shaped((length, 3 * hw), BF16), shaped((8, width), F32)),
        [IN_SMEM] + [IN_VMEM] * (2 + spans) + [ANYWHERE] * (2 * nqo),
        [pltpu.VMEM((width, 3 * hw), BF16), pltpu.VMEM((width, 128), BF16), sems(2 * nqo)],
    )(up_at, cos_lanes, sin_lanes, *tok_all, *q_w, *o_w)
    qkv_now = after(qkv, *middle(down_z))
    attn, lse = call(
        functools.partial(attend_kernel, spans, lanes),
        (shaped((length, hw), BF16), shaped((mine, length, 128), F32)),
        [IN_SMEM, IN_VMEM],
    )(sorted_at, qkv_now)

    attn_now = after(attn, *(up_y[half : half + 1] + down_w[:ny]))
    sent = attn_now.reshape(ny, nc, rows_here, hw)
    o_near = [sent[0]] + [shift(sent[sy], "y", ny - sy) for sy in range(1, ny)]
    o_far = [shift(item, "c") for item in o_near]
    o_near[0] = after(o_near[0], *([down_z[half]] + up_w[: 2 * nx] + up_w[-nx:]))
    r_keep, r_send, o_chip = call(
        functools.partial(out_kernel, nqo, ny),
        (shaped((rows_here, owh), F32), shaped((rows_here, owh), F32), shaped((crow, width), BF16)),
        [IN_SMEM, IN_SMEM] + [IN_VMEM] * (2 * ny) + [IN_SMEM] + [ANYWHERE] * nqo,
        [pltpu.VMEM((width, owh), BF16), sems(nqo)],
    )(up_at, core, *o_near, *o_far, span_y, *o_w)
    r_send = after(r_send, *(down_w[ny : 2 * ny] + down_w[-ny:] + up_w[half * nx : half * nx + nx]))
    r_got = shift(r_send, "c")
    h, a2 = call(
        middle_kernel,
        (shaped((rows_here, width), F32), shaped((rows_here, width), BF16)),
        [IN_SMEM] + [IN_VMEM] * 4,
        [pltpu.VMEM((rows_here, width), F32)],
    )(core, r_keep, r_got, tok, norms)
    a2 = after(a2)
    a2_got = shift(a2, "c")
    m_keep, m_send, u, slope = call(
        functools.partial(mlp_kernel, nup, ndown),
        (
            shaped((rows_here, width), F32),
            shaped((rows_here, width), BF16),
            shaped((crow, ffh), BF16),
            shaped((crow, ffh), BF16),
        ),
        [IN_SMEM, IN_SMEM, IN_VMEM, IN_VMEM] + [IN_HBM] * (nup + ndown),
        [pltpu.VMEM((width, ffh), BF16), pltpu.VMEM((ffh, width), BF16), sems(nup + ndown)],
        vmem=26,
    )(up_at, down_at, a2, a2_got, *up_w, *down_w)
    m_got = shift(m_send, "c")
    match = group_ids[:, None] == jnp.arange(group_weight.shape[0], dtype=jnp.int32)[None, :]
    scale = jnp.sum(jnp.where(match, group_weight[None, :], 0.0)).reshape(1)
    out_tokens, dm, grads_3 = call(
        top_kernel,
        (shaped((rows_here, width), BF16), shaped((rows_here, width), BF16), shaped((2, width), F32)),
        [IN_SMEM] + [IN_VMEM] * 5,
    )(scale, m_keep, m_got, h, cot, norms)

    dm_got = shift(dm, "c")
    down_own, down_got = [None] * nz, [None] * nz
    up_own, up_got = [None] * nz, [None] * nz
    early, late = late_last(nz)[:2], late_last(nz)[2:]

    def down_block(step, right, *when):
        blocks = grads(u, [right, dm_got], down_at, nx * ffrows, range(step * ny, step * ny + ny))
        down_own[step] = blocks[0]
        down_got[step] = [shift(after(blocks[far], *when), "y", ny - far) for far in range(1, ny)]

    def up_block(step, right):
        blocks = grads(a2_all, [right], up_at, dprows, range(step * nx, step * nx + nx))
        up_own[step] = blocks[0]
        up_got[step] = [shift(blocks[far], "x", nx - far) for far in range(1, nx)]

    right = dm
    for step in early:
        down_block(step, right, right)
        right = after(dm, down_own[step])
    blocks = [down_own[early[-1]]]
    dm = after(dm, blocks[0])
    da_keep, da_send, dz = call(
        functools.partial(mlp_back_kernel, nup, ndown),
        (
            shaped((rows_here, width), F32),
            shaped((rows_here, width), BF16),
            shaped((crow, ffh), BF16),
        ),
        [IN_SMEM, IN_SMEM, IN_VMEM, IN_VMEM, IN_VMEM] + [IN_HBM] * (nup + ndown),
        [pltpu.VMEM((width, ffh), BF16), pltpu.VMEM((ffh, width), BF16), sems(nup + ndown)],
        vmem=26,
    )(up_at, down_at, dm, dm_got, slope, *up_w, *down_w)
    da_got = shift(da_send, "c")
    a2_all = jnp.concatenate([a2, a2_got], 0)
    right = after(dz, *down_got[early[0]])
    for step in early + late:
        up_block(step, right)
        right = after(dz, up_own[step])
    blocks = [up_own[early[-1]]]
    da_keep = after(da_keep, blocks[0])
    dh, dr, dr_send, grads_21 = call(
        between_kernel,
        (
            shaped((rows_here, width), F32),
            shaped((rows_here, owh), BF16),
            shaped((rows_here, owh), BF16),
            shaped((4, width), F32),
        ),
        [IN_SMEM, IN_SMEM] + [IN_VMEM] * 7,
        [pltpu.VMEM((rows_here, width), F32), pltpu.VMEM((rows_here, width), BF16)],
    )(core, scale, da_keep, da_got, h, r_keep, r_got, cot, norms)
    dr_send = after(dr_send, *down_got[early[1]])
    dr_got = shift(dr_send, "c")
    do_keep, do_send = call(
        functools.partial(out_back_kernel, nqo, ny),
        (shaped((ny, crow, hw), F32), shaped((ny, crow, hw), BF16)),
        [IN_SMEM, IN_SMEM, IN_VMEM, IN_VMEM] + [ANYWHERE] * nqo,
        [pltpu.VMEM((width, owh), BF16), sems(nqo)],
    )(up_at, core, dr, dr_got, *o_back)
    do_got = shift(do_send, "c")
    do_got = jnp.concatenate([do_got[:, rows_here:], do_got[:, :rows_here]], 1)
    do = (do_keep + do_got.astype(F32)).astype(BF16)
    parts = []
    for sy in range(ny):
        item = take(do, lax.rem(iy + sy, ny))
        parts.append(item if sy == 0 else shift(item, "y", sy))
    do_all = jnp.concatenate(parts, 0)
    down_y, up_x = [None] * nz, [None] * nz
    right = after(dm, do)
    down_block(late[0], right, do_all)
    for step in late[1:]:
        down_block(step, after(dm, do), do_all)
    for step in early:
        down_y[step] = add_parts(down_own[step], down_got[step], do)
        up_x[step] = add_parts(up_own[step], up_got[step], do_all)
    out_own, out_send = stacked_grads(o_chip, [dr, dr_got], up_at, dprows)
    out_got = shift(out_send, "x")

    down_first = ring_first(down_y, "z")
    sums = [None] * nz
    for step in early:
        own_y, got_y = send_parts(up_x[step].reshape(ny, nc * wrows, ffh), "y")
        sums[step] = add_parts(own_y, got_y, do_all)
    up_first = ring_first(sums, "z")
    do_all = after(do_all, *[t for t in down_y + up_x + down_own + up_own if t is not None])
    dqkv = call(
        functools.partial(attend_back_kernel, spans, lanes),
        shaped((length, 3 * hw), BF16),
        [IN_SMEM] + [IN_VMEM] * 6,
        [pltpu.VMEM((length, lanes), F32)] * 2,
        vmem=20,
    )(sorted_at, qkv, attn, do_all, lse, cos_lanes, sin_lanes)
    dqkv = after(dqkv, *([t for step in late for t in up_got[step]] + [sums[step] for step in early]))
    qkv_own, qkv_send = stacked_grads(a1, [dqkv], up_at, dprows)
    qkv_got = shift(qkv_send, "x")
    da1_keep, da1_send = call(
        functools.partial(input_back_kernel, nqo, q_off),
        (shaped((ny, rows_here, width), F32), shaped((ny, rows_here, width), BF16)),
        [IN_SMEM, IN_VMEM] + [ANYWHERE] * nqo,
        [pltpu.VMEM((width, 3 * hw), BF16), sems(nqo)],
    )(up_at, after(dqkv, qkv_own), *q_back)
    da1_got = shift(da1_send, "c")
    sent_on = [(da1_keep[sy] + da1_got[sy].astype(F32)).astype(BF16) for sy in range(1, ny)]
    arrived = [shift(item, "y", ny - sy) for sy, item in enumerate(sent_on, 1)]
    da1_keep = after(da1_keep, *(up_first + down_first + [t for step in late for t in down_got[step]]))
    grad_tokens, grads_0 = call(
        bottom_kernel,
        (shaped((rows_here, width), BF16), shaped((2, width), F32)),
        [IN_VMEM] * (5 + len(arrived)),
    )(tok, dh, norms, da1_keep[0], da1_got[0], *arrived)
    grad_tokens = grad_tokens.reshape(tokens.shape)
    out_tokens = out_tokens.reshape(tokens.shape)

    for step in range(nz):
        if down_y[step] is None:
            down_y[step] = add_parts(down_own[step], down_got[step], sent_on[0])
    down = ring_rest(down_y, down_first, "z").astype(BF16)
    down = scatter_sum(down.reshape(nx, ffrows, width), "x")
    for step in late:
        part = add_parts(up_own[step], up_got[step], dqkv)
        own_y, got_y = send_parts(part.reshape(ny, nc * wrows, ffh), "y")
        sums[step] = add_parts(own_y, got_y, arrived[0])
    up = ring_rest(sums, up_first, "z").reshape(nc, wrows, ffh)
    up = pair(take(up, ic), shift(take(up, 1 - ic), "c"), ic)
    up = up.reshape(nc, wrows, nz, ny, nx, ffrows).transpose(1, 2, 4, 3, 0, 5).reshape(wrows, ff)

    out_x = add_parts(out_own, [out_got], sent_on[0])
    qkv_x = (qkv_own.astype(F32) + qkv_got.astype(F32)).astype(BF16)
    both = jnp.concatenate([out_x, qkv_x], -1)
    both = ring_scatter([both[step] for step in range(nz)], "z").astype(BF16)
    out, qkv_g = both[:, :owh], both[:, owh:]
    out = scatter_sum(out.reshape(ny, nc * wrows, owh), "y").reshape(nc, wrows, owh)
    out = pair(take(out, ic), shift(take(out, 1 - ic), "c"), ic)
    out = out.transpose(1, 0, 2).reshape(wrows, width)
    qkv_g = exchange(qkv_g.reshape(ny, nc * wrows, 3 * hw), "y")
    qkv_g = qkv_g.reshape(ny, nc, wrows, 3 * hw).transpose(1, 0, 2, 3)
    qkv_g = pair(take(qkv_g, ic), shift(take(qkv_g, 1 - ic), "c"), ic)
    qkv_g = qkv_g.reshape(nc, ny, wrows, 3, hw).transpose(2, 3, 1, 0, 4)
    qkv_g = qkv_g.reshape(wrows, 3 * width).astype(F32)

    norm_sums = jnp.concatenate(
        [
            grads_0[0:1],
            grads_21[2:3],
            grads_21[0:1],
            grads_3[0:1],
            grads_0[1:2],
            grads_21[3:4],
            grads_21[1:2],
            grads_3[1:2],
        ],
        0,
    )
    norm_sums = after(norm_sums)
    for axis in "cyxz":
        norm_sums = all_sum(norm_sums, axis)
    place = ((iz * nx + ix) * ny + iy) * nc + ic
    norm_sums = lax.dynamic_slice(norm_sums, (0, place * wrows), (8, wrows))
    return (out_tokens, grad_tokens, qkv_g, out, up, down, norm_sums[:4], norm_sums[4:])


def solution(mesh):
    fine = Mesh(
        mesh.devices.reshape(mesh.shape["dp"] // 2, 2, mesh.shape["blk"] // 2, 2),
        ("z", "x", "y", "c"),
    )
    dp, blk, every = ("z", "x"), ("y", "c"), ("z", "x", "y", "c")
    return jax.shard_map(
        on_device,
        mesh=fine,
        in_specs=(
            P(blk, dp, None),
            P(blk, dp, None),
            P(dp),
            P(),
            P(dp, None),
            P(every, None),
            P(every, None),
            P(every, None),
            P(every, None),
            P(None, every),
            P(None, every),
        ),
        out_specs=(
            P(blk, dp, None),
            P(blk, dp, None),
            P(every, None),
            P(every, None),
            P(every, None),
            P(every, None),
            P(None, every),
            P(None, every),
        ),
        check_vma=False,
    )
```

```python
import functools
import math

import jax
import jax.numpy as jnp
from jax import lax
from jax.experimental import pallas as pl
from jax.experimental.pallas import tpu as pltpu
from jax.sharding import Mesh
from jax.sharding import PartitionSpec as P

HD = 64
F32 = jnp.float32
BF16 = jnp.bfloat16


def shift(value, axis, step=1):
    size = lax.axis_size(axis)
    return lax.ppermute(value, axis, [(i, (i + step) % size) for i in range(size)])


def after(value, *others):
    return lax.optimization_barrier((value,) + others)[0]


def back(axis, step):
    size = lax.axis_size(axis)
    return lax.rem(lax.axis_index(axis) + size - step, size)


def take(array, at, axis=0):
    return lax.dynamic_index_in_dim(array, at, axis, keepdims=False)


def direct_gather(piece, axis):
    size = lax.axis_size(axis)
    return [piece] + [shift(piece, axis, step) for step in range(1, size)]


def ring_gather(piece, axis, gate=()):
    size = lax.axis_size(axis)
    pieces = [piece] * size
    for step in range(1, size // 2 + 1):
        last = pieces[step - 1]
        pieces[step] = shift(after(last, *gate) if gate and step > 1 else last, axis)
    for step in range(size - 1, size // 2, -1):
        last = pieces[(step + 1) % size]
        pieces[step] = shift(after(last, *gate) if gate and step < size - 1 else last, axis, -1)
    return pieces


def in_order(pieces, axis):
    if len(pieces) == 2:
        return pair(pieces[0], pieces[1], lax.axis_index(axis))
    buffer = jnp.zeros((len(pieces),) + pieces[0].shape, pieces[0].dtype)
    for step, piece in enumerate(pieces):
        at = (back(axis, step),) + (0,) * piece.ndim
        buffer = lax.dynamic_update_slice(buffer, piece[None], at)
    return buffer


def pair(own, other, index):
    first = jnp.where(index == 0, own, other)
    second = jnp.where(index == 0, other, own)
    return jnp.stack([first, second])


def ring_first(parts, axis):
    size = len(parts)
    half = size // 2
    found = [shift(parts[half].astype(BF16), axis)]
    if size - 1 - half:
        found.append(shift(parts[size - 1 - half].astype(BF16), axis, -1))
    return found


def ring_rest(parts, arrived, axis):
    size = len(parts)
    half = size // 2
    total = parts[0].astype(F32)
    for carry, count, way in zip(arrived, (half, size - 1 - half), (1, -1)):
        for far in range(count - 1, 0, -1):
            part = parts[size - far if way == 1 else far]
            carry = shift((carry.astype(F32) + part.astype(F32)).astype(BF16), axis, way)
        total = total + carry.astype(F32)
    return total


def ring_scatter(parts, axis):
    return ring_rest(parts, ring_first(parts, axis), axis)


def scatter_sum(parts, axis):
    size = parts.shape[0]
    return ring_scatter([take(parts, back(axis, step)) for step in range(size)], axis)


def late_last(size):
    half = size // 2
    steps = list(range(half, 0, -1)) + list(range(half + 1, size)) + [0]
    return list(dict.fromkeys(steps))


def send_parts(parts, axis):
    size = parts.shape[0]
    got = [shift(take(parts, back(axis, step)), axis, size - step) for step in range(1, size)]
    return take(parts, lax.axis_index(axis)), got


def add_parts(own, got, when):
    total = own.astype(F32)
    for item in got:
        total = total + after(item, when).astype(F32)
    return total.astype(BF16)


def exchange(parts, axis):
    size = parts.shape[0]
    index = lax.axis_index(axis)
    pieces = [take(parts, index)]
    for step in range(1, size):
        pieces.append(shift(take(parts, lax.rem(index + step, size)), axis, step))
    return in_order(pieces, axis)


def all_sum(value, axis):
    pieces = direct_gather(value, axis)
    total = pieces[0]
    for piece in pieces[1:]:
        total = total + piece
    return total


IN_VMEM = pl.BlockSpec(memory_space=pltpu.VMEM)
IN_SMEM = pl.BlockSpec(memory_space=pltpu.SMEM)
ANYWHERE = pl.BlockSpec(memory_space=pl.ANY)
IN_HBM = pl.BlockSpec(memory_space=pltpu.HBM)


def call(kernel, out_shape, in_specs, scratch=(), vmem=16):
    several = isinstance(out_shape, (tuple, list))
    return pl.pallas_call(
        kernel,
        out_shape=out_shape,
        in_specs=in_specs,
        out_specs=[IN_VMEM] * len(out_shape) if several else IN_VMEM,
        scratch_shapes=list(scratch),
        compiler_params=pltpu.CompilerParams(vmem_limit_bytes=vmem * 1024 * 1024),
        cost_estimate=pl.CostEstimate(flops=1024, bytes_accessed=1024, transcendentals=0),
    )


def fetch(pieces, at_ref, target, sems, first, offset=0, columns=None):
    copies = []
    for number, piece in enumerate(pieces):
        rows = piece.shape[0]
        source = piece if columns is None else piece.at[:, pl.ds(offset, columns)]
        place = pl.ds(pl.multiple_of(at_ref[number] * rows, rows), rows)
        copies.append(pltpu.make_async_copy(source, target.at[place], sems.at[first + number]))
    for copy in copies:
        copy.start()
    return copies


def wait_all(copies):
    for copy in copies:
        copy.wait()


def partner(values):
    half = HD // 2
    if values.shape[-1] == HD:
        return jnp.concatenate([values[:, half:], values[:, :half]], -1)
    lanes = values.shape[-1]
    lane = lax.broadcasted_iota(jnp.int32, values.shape, 1)
    low = lax.rem(lane, HD) < half
    return jnp.where(low, pltpu.roll(values, lanes - half, 1), pltpu.roll(values, half, 1))


def attend_kernel(blocks, lanes, order_ref, qkv_ref, o_ref, lse_ref):
    length, third = o_ref.shape
    size = length // blocks
    per = lanes // HD
    lane = lax.broadcasted_iota(jnp.int32, (1, lanes), 1) // HD
    row = lax.broadcasted_iota(jnp.int32, (size, size), 0)
    col = lax.broadcasted_iota(jnp.int32, (size, size), 1)
    for group in range(third // lanes):
        left = group * lanes

        def one_row(i):
            at = pl.multiple_of(order_ref[i] * size, size)
            q = qkv_ref[pl.ds(at, size), left : left + lanes]
            outs, totals = [], []
            for head in range(per):
                qh = q * (lane == head).astype(BF16)

                def scores(start):
                    k = qkv_ref[pl.ds(start, size), third + left : third + left + lanes]
                    return lax.dot_general(qh, k, (((1,), (1,)), ((), ())), preferred_element_type=F32)

                def values(p, start):
                    v = qkv_ref[pl.ds(start, size), 2 * third + left : 2 * third + left + lanes]
                    return jnp.dot(p.astype(BF16), v, preferred_element_type=F32)

                s = jnp.where(col <= row, scores(at), -1e30)
                top = jnp.max(s, -1, keepdims=True)
                p = jnp.exp(s - top)
                state = (top, jnp.sum(p, -1, keepdims=True), values(p, at))

                def step(j, state):
                    top, total, acc = state
                    start = pl.multiple_of(order_ref[j] * size, size)
                    s = scores(start)
                    new = jnp.maximum(top, jnp.max(s, -1, keepdims=True))
                    factor = jnp.exp(top - new)
                    p = jnp.exp(s - new)
                    total = total * factor + jnp.sum(p, -1, keepdims=True)
                    return new, total, acc * factor + values(p, start)

                if blocks <= 4:
                    for j in range(i):
                        state = step(j, state)
                else:
                    state = lax.fori_loop(0, i, step, state)
                top, total, acc = state
                outs.append(acc / total)
                lse = jnp.broadcast_to(top + jnp.log(total), (size, 128))
                lse_ref[group * per + head, pl.ds(at, size), :] = lse
            out = outs[0]
            for head in range(1, per):
                out = jnp.where(lane == head, outs[head], out)
            o_ref[pl.ds(at, size), left : left + lanes] = out.astype(BF16)

        if blocks <= 4:
            for i in range(blocks):
                one_row(i)
        else:
            pl.loop(0, blocks)(one_row)


def attend_back_kernel(
    blocks, lanes, order_ref, qkv_ref, o_ref, do_ref, lse_ref, cos_ref, sin_ref, out_ref, dk_ref, dv_ref
):
    length, third = o_ref.shape
    size = length // blocks
    per = lanes // HD
    lane = lax.broadcasted_iota(jnp.int32, (1, lanes), 1) // HD
    row = lax.broadcasted_iota(jnp.int32, (size, size), 0)
    col = lax.broadcasted_iota(jnp.int32, (size, size), 1)
    nt = (((1,), (1,)), ((), ()))
    tn = (((0,), (0,)), ((), ()))

    def unturn(values, rows):
        return values * cos_ref[rows, :] - partner(values) * sin_ref[rows, :]

    for group in range(third // lanes):
        left = group * lanes
        dk_ref[...] = jnp.zeros_like(dk_ref)
        dv_ref[...] = jnp.zeros_like(dv_ref)

        def one_row(i):
            at = pl.multiple_of(order_ref[i] * size, size)
            rows = pl.ds(at, size)
            q = qkv_ref[rows, left : left + lanes]
            do = do_ref[rows, left : left + lanes]
            prod = do.astype(F32) * o_ref[rows, left : left + lanes].astype(F32)
            grads = []
            for head in range(per):
                own = (lane == head).astype(BF16)
                qh, doh = q * own, do * own
                delta = jnp.sum(jnp.where(lane == head, prod, 0.0), -1, keepdims=True)
                lse = lse_ref[group * per + head, rows, 0:1]

                def step(start, diagonal):
                    where = pl.ds(start, size)
                    k = qkv_ref[where, third + left : third + left + lanes]
                    v = qkv_ref[where, 2 * third + left : 2 * third + left + lanes]
                    s = lax.dot_general(qh, k, nt, preferred_element_type=F32)
                    p = jnp.exp(s - lse)
                    if diagonal:
                        p = jnp.where(col <= row, p, 0.0)
                    dp = lax.dot_general(doh, v, nt, preferred_element_type=F32)
                    ds = (p * (dp - delta)).astype(BF16)
                    dv_ref[where, :] += lax.dot_general(p.astype(BF16), doh, tn, preferred_element_type=F32)
                    dk_ref[where, :] += lax.dot_general(ds, qh, tn, preferred_element_type=F32)
                    return jnp.dot(ds, k, preferred_element_type=F32)

                dq = step(at, True)
                if blocks <= 4:
                    for j in range(i):
                        dq = dq + step(pl.multiple_of(order_ref[j] * size, size), False)
                else:
                    dq = lax.fori_loop(
                        0, i, lambda j, c: c + step(pl.multiple_of(order_ref[j] * size, size), False), dq
                    )
                grads.append(dq)
            dq = grads[0]
            for head in range(1, per):
                dq = jnp.where(lane == head, grads[head], dq)
            out_ref[rows, left : left + lanes] = unturn(dq * 0.125, rows).astype(BF16)

        if blocks <= 4:
            for i in range(blocks):
                one_row(i)
        else:
            pl.loop(0, blocks)(one_row)
        for start in range(0, length, size):
            rows = pl.ds(start, size)
            out_ref[rows, third + left : third + left + lanes] = unturn(dk_ref[rows, :], rows).astype(BF16)
            out_ref[rows, 2 * third + left : 2 * third + left + lanes] = dv_ref[rows, :].astype(BF16)


GELU_A = math.sqrt(2.0 / math.pi)
GELU_B = 0.044715


NT = (((1,), (1,)), ((), ()))
TN = (((0,), (0,)), ((), ()))


def normed(values):
    centred = values - jnp.mean(values, -1, keepdims=True)
    scale = lax.rsqrt(jnp.mean(centred * centred, -1, keepdims=True) + 1e-05)
    return centred * scale, scale


def normed_back(grad, gain, vhat, scale):
    scaled = grad * gain
    return scale * (
        scaled - jnp.mean(scaled, -1, keepdims=True) - vhat * jnp.mean(scaled * vhat, -1, keepdims=True)
    )


def column_sum(values):
    return jnp.sum(values, 0, keepdims=True)


def halves(core_ref, width):
    own = pl.ds(pl.multiple_of(core_ref[0] * width, width), width)
    other = pl.ds(pl.multiple_of((1 - core_ref[0]) * width, width), width)
    return own, other


def cut_kernel(sizes, core_ref, qkv_ref, out_ref, norm_ref, up_ref, keep_ref, send_ref):
    nz, nx, ny, hw, ffrows = sizes
    width, owh = out_ref.shape[1], out_ref.shape[1] // 2
    for target, core in ((keep_ref, core_ref[0]), (send_ref, 1 - core_ref[0])):
        at = 0
        for y in range(ny):
            for part in range(3):
                left = pl.multiple_of(part * width + (y * 2 + core) * hw, hw)
                target[:, at : at + hw] = qkv_ref[:, pl.ds(left, hw)]
                at += hw
        target[:, at : at + owh] = out_ref[:, pl.ds(pl.multiple_of(core * owh, owh), owh)]
        at += owh
        target[:, at : at + 128] = norm_ref[...]
        at += 128
        for z in range(nz):
            for y in range(ny):
                for x in range(nx):
                    left = pl.multiple_of((((z * nx + x) * ny + y) * 2 + core) * ffrows, ffrows)
                    target[:, at : at + ffrows] = up_ref[:, pl.ds(left, ffrows)]
                    at += ffrows


def up_kernel(sizes, core_ref, own_ref, got_ref, up_ref):
    nz, nx, ny, ffrows = sizes
    for source, core in ((own_ref, core_ref[0]), (got_ref, 1 - core_ref[0])):
        at = 0
        for z in range(nz):
            for y in range(ny):
                for x in range(nx):
                    left = pl.multiple_of((((z * nx + x) * ny + y) * 2 + core) * ffrows, ffrows)
                    up_ref[:, pl.ds(left, ffrows)] = source[:, at : at + ffrows]
                    at += ffrows


def qkv_out_kernel(core_ref, own_ref, got_ref, out_own_ref, out_got_ref, qkv_ref, out_ref):
    ny, hw = own_ref.shape[0], own_ref.shape[2] // 3
    width, owh = out_ref.shape[1], out_own_ref.shape[1]
    own, other = halves(core_ref, owh)
    out_ref[:, own] = out_own_ref[...]
    out_ref[:, other] = out_got_ref[...]
    for source, core in ((own_ref, core_ref[0]), (got_ref, 1 - core_ref[0])):
        for y in range(ny):
            for part in range(3):
                left = pl.multiple_of(part * width + (y * 2 + core) * hw, hw)
                qkv_ref[:, pl.ds(left, hw)] = source[y, :, part * hw : part * hw + hw].astype(F32)


def input_kernel(count, blocks, lanes, q_off, n_off, at_ref, cos_ref, sin_ref, *refs):
    toks, refs = refs[:blocks], refs[blocks:]
    q_pieces, n_pieces, refs = refs[:count], refs[count : 2 * count], refs[2 * count :]
    a_ref, out_ref, norm_ref, weight, columns, sems = refs
    wide = out_ref.shape[1]
    first = fetch(n_pieces, at_ref, columns, sems, 0, n_off, 128)
    later = fetch(q_pieces, at_ref, weight, sems, count, q_off, wide)
    wait_all(first)
    norm_ref[...] = jnp.transpose(columns[...].astype(F32))[:8, :]
    gain, bias = norm_ref[0:1, :], norm_ref[4:5, :]
    rows_here = toks[0].shape[0]
    for number, tok_ref in enumerate(toks):
        vhat, _ = normed(tok_ref[...].astype(F32))
        a_ref[pl.ds(number * rows_here, rows_here), :] = (vhat * gain + bias).astype(BF16)
    wait_all(later)
    third = wide // 3
    block = 256
    for start in range(0, out_ref.shape[0], block):
        rows = pl.ds(start, block)
        acc = jnp.dot(a_ref[rows, :], weight[...], preferred_element_type=F32)
        cos, sin = cos_ref[rows, :], sin_ref[rows, :]
        for part in range(3):
            for left in range(0, third, lanes):
                at = part * third + left
                values = acc[:, at : at + lanes]
                if part < 2:
                    values = values * cos + partner(values) * sin
                if part == 0:
                    values = values * 0.125
                out_ref[rows, at : at + lanes] = values.astype(BF16)


def out_kernel(count, ny, at_ref, core_ref, *refs):
    near, far, refs = refs[:ny], refs[ny : 2 * ny], refs[2 * ny :]
    y_ref, pieces, refs = refs[0], refs[1 : 1 + count], refs[1 + count :]
    keep_ref, send_ref, chip_ref, weight, sems = refs
    copies = fetch(pieces, at_ref, weight, sems, 0, 0, weight.shape[1])
    core = core_ref[0]
    rows, hw = near[0].shape[1], near[0].shape[2]
    for parts, is_far in ((near, False), (far, True)):
        other = 1 - core if is_far else core
        for ahead in range(ny):
            yh = lax.rem(y_ref[0] + ahead, ny)
            for sc in range(2):
                token = pl.ds(((1 - sc) if is_far else sc) * rows, rows)
                value = parts[ahead][sc]
                if hw % 128 == 0:
                    left = pl.multiple_of((yh * 2 + other) * hw, hw)
                    chip_ref[token, pl.ds(left, hw)] = value
                else:
                    for place in range(2 * ny):

                        @pl.when(yh * 2 + other == place)
                        def _(place=place, value=value, token=token):
                            chip_ref[token, place * hw : place * hw + hw] = value

    wait_all(copies)
    send_ref[...] = jnp.dot(chip_ref[rows:, :], weight[...], preferred_element_type=F32)
    keep_ref[...] = jnp.dot(chip_ref[:rows, :], weight[...], preferred_element_type=F32)


def middle_kernel(core_ref, keep_ref, got_ref, tok_ref, norm_ref, h_ref, a_ref, r_ref):
    own, other = halves(core_ref, keep_ref.shape[1])
    r_ref[:, own] = keep_ref[...]
    r_ref[:, other] = got_ref[...]
    vhat, _ = normed(r_ref[...])
    h = tok_ref[...].astype(F32) + vhat * norm_ref[1:2, :] + norm_ref[5:6, :]
    h_ref[...] = h
    vhat, _ = normed(h)
    a_ref[...] = (vhat * norm_ref[2:3, :] + norm_ref[6:7, :]).astype(BF16)


def mlp_kernel(ups, downs, up_at, down_at, own_ref, got_ref, *refs):
    up_pieces, down_pieces = refs[:ups], refs[ups : ups + downs]
    keep_ref, send_ref, u_ref, slope_ref, up, down, sems = refs[ups + downs :]
    copies = fetch(up_pieces, up_at, up, sems, 0)
    later = fetch(down_pieces, down_at, down, sems, ups)
    wait_all(copies)
    count, wide = own_ref.shape[0], u_ref.shape[1]
    step = min(512, wide)
    for start, a_ref in ((count, got_ref), (0, own_ref)):
        rows = pl.ds(start, count)
        for left in range(0, wide, step):
            z = jnp.dot(a_ref[...], up[:, left : left + step], preferred_element_type=F32)
            square = z * z
            t = jnp.tanh(GELU_A * z * (1.0 + GELU_B * square))
            half = 0.5 * (1.0 + t)
            u_ref[rows, left : left + step] = (z * half).astype(BF16)
            slope = half + 0.5 * z * (1.0 - t * t) * (GELU_A * (1.0 + 3.0 * GELU_B * square))
            slope_ref[rows, left : left + step] = slope.astype(BF16)
    wait_all(later)
    send_ref[...] = jnp.dot(u_ref[count:, :], down[...], preferred_element_type=F32).astype(BF16)
    keep_ref[...] = jnp.dot(u_ref[:count, :], down[...], preferred_element_type=F32)


def top_kernel(scale_ref, keep_ref, got_ref, h_ref, cot_ref, norm_ref, out_ref, dm_ref, grad_ref):
    vhat, scale = normed(keep_ref[...] + got_ref[...].astype(F32))
    gain = norm_ref[3:4, :]
    out_ref[...] = (h_ref[...] + vhat * gain + norm_ref[7:8, :]).astype(BF16)
    g = cot_ref[...].astype(F32) * scale_ref[0]
    dm_ref[...] = normed_back(g, gain, vhat, scale).astype(BF16)
    grad_ref[0:1, :] = column_sum(g * vhat)
    grad_ref[1:2, :] = column_sum(g)


def mlp_back_kernel(ups, downs, up_at, down_at, own_ref, got_ref, slope_ref, *refs):
    up_pieces, down_pieces = refs[:ups], refs[ups : ups + downs]
    keep_ref, send_ref, dz_ref, up, down, sems = refs[ups + downs :]
    copies = fetch(down_pieces, down_at, down, sems, ups)
    later = fetch(up_pieces, up_at, up, sems, 0)
    wait_all(copies)
    count, wide = own_ref.shape[0], dz_ref.shape[1]
    step = min(512, wide)
    for start, dm_ref in ((count, got_ref), (0, own_ref)):
        rows = pl.ds(start, count)
        for left in range(0, wide, step):
            du = lax.dot_general(dm_ref[...], down[left : left + step, :], NT, preferred_element_type=F32)
            slope = slope_ref[rows, left : left + step].astype(F32)
            dz_ref[rows, left : left + step] = (du * slope).astype(BF16)
    wait_all(later)
    send = lax.dot_general(dz_ref[count:, :], up[...], NT, preferred_element_type=F32)
    send_ref[...] = send.astype(BF16)
    keep_ref[...] = lax.dot_general(dz_ref[:count, :], up[...], NT, preferred_element_type=F32)


def between_kernel(
    core_ref, scale_ref, da_ref, da_got_ref, h_ref, keep_ref, got_ref, cot_ref, norm_ref,
    dh_ref, own_ref, send_ref, grad_ref, r_ref, dr_ref,
):
    own, other = halves(core_ref, keep_ref.shape[1])
    r_ref[:, own] = keep_ref[...]
    r_ref[:, other] = got_ref[...]
    e = da_ref[...] + da_got_ref[...].astype(F32)
    vhat, scale = normed(h_ref[...])
    grad_ref[0:1, :] = column_sum(e * vhat)
    grad_ref[1:2, :] = column_sum(e)
    g = cot_ref[...].astype(F32) * scale_ref[0]
    dh = g + normed_back(e, norm_ref[2:3, :], vhat, scale)
    dh_ref[...] = dh
    vhat, scale = normed(r_ref[...])
    grad_ref[2:3, :] = column_sum(dh * vhat)
    grad_ref[3:4, :] = column_sum(dh)
    dr_ref[...] = normed_back(dh, norm_ref[1:2, :], vhat, scale).astype(BF16)
    own_ref[...] = dr_ref[:, own]
    send_ref[...] = dr_ref[:, other]


def out_back_kernel(count, ny, at_ref, core_ref, own_ref, got_ref, *refs):
    pieces = refs[:count]
    keep_ref, send_ref, weight, sems = refs[count:]
    wait_all(fetch(pieces, at_ref, weight, sems, 0, 0, weight.shape[1]))
    core = core_ref[0]
    hw = keep_ref.shape[2]
    size = own_ref.shape[0]
    for own in (False, True):
        head = core if own else 1 - core
        for yh in range(ny):
            rows = pl.ds(pl.multiple_of((yh * 2 + head) * hw, hw), hw)
            for start, dr_ref in ((0, own_ref), (size, got_ref)):
                value = lax.dot_general(dr_ref[...], weight[rows, :], NT, preferred_element_type=F32)
                if own:
                    keep_ref[yh, pl.ds(start, size), :] = value
                else:
                    send_ref[yh, pl.ds(start, size), :] = value.astype(BF16)


def input_back_kernel(count, offset, at_ref, a_ref, *refs):
    pieces = refs[:count]
    keep_ref, send_ref, weight, sems = refs[count:]
    wait_all(fetch(pieces, at_ref, weight, sems, 0, offset, weight.shape[1]))
    block = keep_ref.shape[1]
    for number in range(a_ref.shape[0] // block):
        rows = pl.ds(number * block, block)
        value = lax.dot_general(a_ref[rows, :], weight[...], NT, preferred_element_type=F32)
        if number % 2 == 0:
            keep_ref[number // 2] = value
        else:
            send_ref[number // 2] = value.astype(BF16)


def bottom_kernel(*refs):
    tok_ref, dh_ref, norm_ref = refs[:3]
    pieces, (out_ref, grad_ref) = refs[3:-2], refs[-2:]
    e = pieces[0][...].astype(F32)
    for piece in pieces[1:]:
        e = e + piece[...].astype(F32)
    vhat, scale = normed(tok_ref[...].astype(F32))
    out_ref[...] = (dh_ref[...] + normed_back(e, norm_ref[0:1, :], vhat, scale)).astype(BF16)
    grad_ref[0:1, :] = column_sum(e * vhat)
    grad_ref[1:2, :] = column_sum(e)


def stacked_kernel(parts, cols, at_ref, left_ref, *refs):
    rights, (own_ref, send_ref) = refs[:parts], refs[parts:]
    size = rights[0].shape[0]
    for number in range(2 * own_ref.shape[0]):
        columns = pl.ds(pl.multiple_of(at_ref[number] * cols, cols), cols)
        total = None
        for place, right in enumerate(rights):
            left = left_ref[place * size : place * size + size, columns]
            value = lax.dot_general(left, right[...], TN, preferred_element_type=F32)
            total = value if total is None else total + value
        target = send_ref if number % 2 else own_ref
        target[number // 2] = total.astype(BF16)


def stacked_grads(left, rights, at, cols):
    wide, count = rights[0].shape[1], left.shape[1] // cols // 2
    if cols % 128:
        blocks = grads(left, rights, at, cols, range(2 * count))
        return jnp.stack(blocks[0::2]), jnp.stack(blocks[1::2])
    return call(
        functools.partial(stacked_kernel, len(rights), cols),
        [jax.ShapeDtypeStruct((count, cols, wide), BF16)] * 2,
        [IN_SMEM] + [IN_VMEM] * (1 + len(rights)),
    )(at, left, *rights)


def blocks_kernel(parts, cols, numbers, at_ref, left_ref, *refs):
    rights, outs = refs[:parts], refs[parts:]
    size = rights[0].shape[0]
    for number, out_ref in zip(numbers, outs):
        columns = pl.ds(pl.multiple_of(at_ref[number] * cols, cols), cols)
        total = None
        for place, right in enumerate(rights):
            left = left_ref[place * size : place * size + size, columns]
            value = lax.dot_general(left, right[...], TN, preferred_element_type=F32)
            total = value if total is None else total + value
        out_ref[...] = total.astype(BF16)


def grads(left, rights, at, cols, numbers):
    if cols % 128 == 0:
        return call(
            functools.partial(blocks_kernel, len(rights), cols, tuple(numbers)),
            [jax.ShapeDtypeStruct((cols, rights[0].shape[1]), BF16)] * len(numbers),
            [IN_SMEM] + [IN_VMEM] * (1 + len(rights)),
        )(at, left, *rights)
    right = jnp.concatenate(rights, 0)
    found = []
    for number in numbers:
        block = lax.dynamic_slice(left, (0, at[number] * cols), (left.shape[0], cols))
        found.append(lax.dot_general(block, right, TN, preferred_element_type=F32).astype(BF16))
    return found


def on_device(
    tokens,
    cotangent,
    group_ids,
    group_weight,
    block_order,
    w_qkv,
    w_out,
    w_up,
    w_down,
    norm_gain,
    norm_bias,
):
    nz, nx, ny, nc = (lax.axis_size(a) for a in "zxyc")
    iz, ix, iy, ic = (lax.axis_index(a) for a in "zxyc")
    rows_here, _, width = tokens.shape
    heads = width // HD
    spans = ny * nc
    mine = heads // spans
    hw = mine * HD
    lanes = min(128, hw)
    wrows = w_qkv.shape[0]
    ffrows = w_down.shape[0]
    ff = w_up.shape[1]
    ffh = ff // nc
    owh = width // nc
    dprows = spans * wrows
    length = spans * rows_here
    crow = nc * rows_here
    half = nz // 2
    shaped = jax.ShapeDtypeStruct

    def middle(pieces):
        return pieces[1:2] + pieces[-1:]

    def sems(count):
        return pltpu.SemaphoreType.DMA((count,))

    tok = tokens.reshape(rows_here, width)
    cot = cotangent.reshape(rows_here, width)
    norm_rows = jnp.concatenate([norm_gain, norm_bias], 0).T
    norm_rows = jnp.pad(norm_rows, ((0, 0), (0, 120)))
    core = ic.astype(jnp.int32).reshape(1)
    aligned = hw % 128 == 0 and ffrows % 128 == 0
    if aligned:
        keep, send = call(
            functools.partial(cut_kernel, (nz, nx, ny, hw, ffrows)),
            [shaped((wrows, ny * 3 * hw + owh + 128 + ffh), BF16)] * 2,
            [IN_SMEM] + [IN_VMEM] * 4,
        )(core, w_qkv, w_out, norm_rows, w_up)
    else:
        norm_rows = jnp.broadcast_to(norm_rows[None], (nc, wrows, 128))
        cut = jnp.concatenate(
            [
                w_qkv.reshape(wrows, 3, ny, nc, hw).transpose(3, 0, 2, 1, 4).reshape(nc, wrows, -1),
                w_out.reshape(wrows, nc, owh).transpose(1, 0, 2),
                norm_rows,
                w_up.reshape(wrows, nz, nx, ny, nc, ffrows)
                .transpose(4, 0, 1, 3, 2, 5)
                .reshape(nc, wrows, ffh),
            ],
            -1,
        )
        keep, send = take(cut, ic), take(cut, 1 - ic)
    cut = pair(keep, shift(send, "c"), ic).reshape(nc * wrows, -1)
    q_cut = cut[:, : ny * 3 * hw].reshape(nc * wrows, ny, 3 * hw)
    left = ny * 3 * hw
    o_cut = jnp.broadcast_to(cut[:, None, left : left + owh + 128], (nc * wrows, ny, owh + 128))
    up_cut = cut[:, left + owh + 128 :]
    qo = exchange(jnp.concatenate([o_cut, q_cut], -1).transpose(1, 0, 2), "y")
    qo = qo.reshape(dprows, owh + 128 + 3 * hw)
    down_pieces = ring_gather(w_down, "x")
    span_y = iy.astype(jnp.int32).reshape(1)

    qo_z = ring_gather(qo, "z")
    up_z = ring_gather(up_cut, "z")
    tok_y = ring_gather(after(tok, *[qo]), "y")
    tok_all = []
    for item in tok_y:
        item = item if not tok_all else after(item, *qo_z)
        tok_all.append(item)
        tok_all.append(shift(item, "c"))
    qo_w, up_w, down_w = [], [], []
    up_at, down_at = [], []
    for step, item in enumerate(qo_z):
        for far, piece in enumerate(ring_gather(item, "x")):
            qo_w.append(piece)
            up_at.append(back("z", step) * nx + back("x", far))
    up_use = [after(up_z[0], *[qo])] + [after(item, *middle(qo_z)) for item in up_z[1:]]
    up_use[half] = after(up_use[half], *[qo_z[half]])
    up_y = []
    for item in up_use:
        pieces = ring_gather(item, "y")
        pieces = pieces[:1] + [after(piece, *qo_w) for piece in pieces[1:]]
        up_y.append(in_order(pieces, "y").reshape(dprows, ffh))
        up_w += ring_gather(up_y[-1], "x")
    down_pieces = [down_pieces[0]] + [after(item, *qo_z) for item in down_pieces[1:]]
    down_z = ring_gather(in_order(down_pieces, "x").reshape(nx * ffrows, width), "z")
    for step, item in enumerate(down_z):
        for far, piece in enumerate(ring_gather(item, "y")):
            down_w.append(piece)
            down_at.append(back("z", step) * ny + back("y", far))
    up_at = jnp.stack(up_at).astype(jnp.int32)
    down_at = jnp.stack(down_at).astype(jnp.int32)
    q_w, o_w, q_off = qo_w, qo_w, owh + 128
    if hw % 128:
        q_w, o_w, q_off = [p[:, owh + 128 :] for p in qo_w], [p[:, : owh + 128] for p in qo_w], 0
    nqo, nup, ndown = len(qo_w), len(up_w), len(down_w)
    up_w, down_w, q_back, o_back = (
        [pltpu.with_memory_space_constraint(piece, pltpu.HBM) for piece in pieces]
        for pieces in (up_w, down_w, q_w, o_w)
    )

    order = after(block_order, *middle(qo_z))[0].reshape(ny, nc)
    places = []
    for sy in range(ny):
        for sc in range(nc):
            places.append(take(take(order, back("y", sy)), back("c", sc)))
    places = jnp.stack(places)
    ranks = jnp.arange(spans, dtype=jnp.int32)
    sorted_at = jnp.sum(jnp.where(places[None, :] == ranks[:, None], ranks[None, :], 0), -1)
    offsets = jnp.arange(rows_here, dtype=jnp.int32)
    positions = (places[:, None] * rows_here + offsets[None, :]).reshape(length)
    lane = jnp.arange(lanes, dtype=jnp.int32)
    frequency = jnp.exp((lane % (HD // 2)).astype(F32) * (-2.0 * math.log(10000.0) / HD))
    angles = positions.astype(F32)[:, None] * frequency[None, :]
    cos_lanes = after(jnp.cos(angles))
    sin_lanes = jnp.sin(angles) * jnp.where(lane % HD < HD // 2, -1.0, 1.0)

    a1, qkv, norms = call(
        functools.partial(input_kernel, nqo, spans, lanes, q_off, owh),
        (shaped((length, width), BF16), shaped((length, 3 * hw), BF16), shaped((8, width), F32)),
        [IN_SMEM] + [IN_VMEM] * (2 + spans) + [ANYWHERE] * (2 * nqo),
        [pltpu.VMEM((width, 3 * hw), BF16), pltpu.VMEM((width, 128), BF16), sems(2 * nqo)],
    )(up_at, cos_lanes, sin_lanes, *tok_all, *q_w, *o_w)
    qkv_now = after(qkv, *middle(down_z))
    attn, lse = call(
        functools.partial(attend_kernel, spans, lanes),
        (shaped((length, hw), BF16), shaped((mine, length, 128), F32)),
        [IN_SMEM, IN_VMEM],
    )(sorted_at, qkv_now)

    attn_now = after(attn, *(up_y[half : half + 1] + down_w[:ny]))
    sent = attn_now.reshape(ny, nc, rows_here, hw)
    o_near = [sent[0]] + [shift(sent[sy], "y", ny - sy) for sy in range(1, ny)]
    o_far = [shift(item, "c") for item in o_near]
    o_near[0] = after(o_near[0], *([down_z[half]] + up_w[: 2 * nx] + up_w[-nx:] + down_w[ny : 2 * ny]))
    r_keep, r_send, o_chip = call(
        functools.partial(out_kernel, nqo, ny),
        (shaped((rows_here, owh), F32), shaped((rows_here, owh), F32), shaped((crow, width), BF16)),
        [IN_SMEM, IN_SMEM] + [IN_VMEM] * (2 * ny) + [IN_SMEM] + [ANYWHERE] * nqo,
        [pltpu.VMEM((width, owh), BF16), sems(nqo)],
    )(up_at, core, *o_near, *o_far, span_y, *o_w)
    r_send = after(r_send, *(down_w[ny : 2 * ny] + down_w[-ny:] + up_w[half * nx : half * nx + nx]))
    r_got = shift(r_send, "c")
    h, a2 = call(
        middle_kernel,
        (shaped((rows_here, width), F32), shaped((rows_here, width), BF16)),
        [IN_SMEM] + [IN_VMEM] * 4,
        [pltpu.VMEM((rows_here, width), F32)],
    )(core, r_keep, r_got, tok, norms)
    a2 = after(a2)
    a2_got = shift(a2, "c")
    m_keep, m_send, u, slope = call(
        functools.partial(mlp_kernel, nup, ndown),
        (
            shaped((rows_here, width), F32),
            shaped((rows_here, width), BF16),
            shaped((crow, ffh), BF16),
            shaped((crow, ffh), BF16),
        ),
        [IN_SMEM, IN_SMEM, IN_VMEM, IN_VMEM] + [IN_HBM] * (nup + ndown),
        [pltpu.VMEM((width, ffh), BF16), pltpu.VMEM((ffh, width), BF16), sems(nup + ndown)],
        vmem=26,
    )(up_at, down_at, a2, a2_got, *up_w, *down_w)
    m_got = shift(m_send, "c")
    match = group_ids[:, None] == jnp.arange(group_weight.shape[0], dtype=jnp.int32)[None, :]
    scale = jnp.sum(jnp.where(match, group_weight[None, :], 0.0)).reshape(1)
    out_tokens, dm, grads_3 = call(
        top_kernel,
        (shaped((rows_here, width), BF16), shaped((rows_here, width), BF16), shaped((2, width), F32)),
        [IN_SMEM] + [IN_VMEM] * 5,
    )(scale, m_keep, m_got, h, cot, norms)

    dm_got = shift(dm, "c")
    down_own, down_got = [None] * nz, [None] * nz
    up_own, up_got = [None] * nz, [None] * nz
    early, late = late_last(nz)[:2], late_last(nz)[2:]

    def down_block(step, right, *when):
        blocks = grads(u, [right, dm_got], down_at, nx * ffrows, range(step * ny, step * ny + ny))
        down_own[step] = blocks[0]
        down_got[step] = [shift(after(blocks[far], *when), "y", ny - far) for far in range(1, ny)]

    def up_block(step, right):
        blocks = grads(a2_all, [right], up_at, dprows, range(step * nx, step * nx + nx))
        up_own[step] = blocks[0]
        up_got[step] = [shift(blocks[far], "x", nx - far) for far in range(1, nx)]

    right = dm
    for step in early:
        down_block(step, right, right)
        right = after(dm, down_own[step])
    blocks = [down_own[early[-1]]]
    dm = after(dm, blocks[0])
    da_keep, da_send, dz = call(
        functools.partial(mlp_back_kernel, nup, ndown),
        (
            shaped((rows_here, width), F32),
            shaped((rows_here, width), BF16),
            shaped((crow, ffh), BF16),
        ),
        [IN_SMEM, IN_SMEM, IN_VMEM, IN_VMEM, IN_VMEM] + [IN_HBM] * (nup + ndown),
        [pltpu.VMEM((width, ffh), BF16), pltpu.VMEM((ffh, width), BF16), sems(nup + ndown)],
        vmem=26,
    )(up_at, down_at, dm, dm_got, slope, *up_w, *down_w)
    da_got = shift(da_send, "c")
    a2_all = jnp.concatenate([a2, a2_got], 0)
    right = after(dz)
    for step in early + late:
        up_block(step, right)
        right = after(dz, up_own[step])
    blocks = [up_own[early[-1]]]
    da_keep = after(da_keep, blocks[0], *down_got[early[0]])
    dh, dr, dr_send, grads_21 = call(
        between_kernel,
        (
            shaped((rows_here, width), F32),
            shaped((rows_here, owh), BF16),
            shaped((rows_here, owh), BF16),
            shaped((4, width), F32),
        ),
        [IN_SMEM, IN_SMEM] + [IN_VMEM] * 7,
        [pltpu.VMEM((rows_here, width), F32), pltpu.VMEM((rows_here, width), BF16)],
    )(core, scale, da_keep, da_got, h, r_keep, r_got, cot, norms)
    dr_send = after(dr_send, *down_got[early[1]])
    dr_got = shift(dr_send, "c")
    do_keep, do_send = call(
        functools.partial(out_back_kernel, nqo, ny),
        (shaped((ny, crow, hw), F32), shaped((ny, crow, hw), BF16)),
        [IN_SMEM, IN_SMEM, IN_VMEM, IN_VMEM] + [ANYWHERE] * nqo,
        [pltpu.VMEM((width, owh), BF16), sems(nqo)],
    )(up_at, core, dr, dr_got, *o_back)
    do_got = shift(do_send, "c")
    do_got = jnp.concatenate([do_got[:, rows_here:], do_got[:, :rows_here]], 1)
    do = (do_keep + do_got.astype(F32)).astype(BF16)
    parts = []
    for sy in range(ny):
        item = take(do, lax.rem(iy + sy, ny))
        parts.append(item if sy == 0 else shift(item, "y", sy))
    do_all = jnp.concatenate(parts, 0)
    down_y, up_x = [None] * nz, [None] * nz
    right = after(dm, do)
    down_block(late[0], right, do_all)
    for step in late[1:]:
        down_block(step, after(dm, do), do_all)
    for step in early:
        down_y[step] = add_parts(down_own[step], down_got[step], do)
        up_x[step] = add_parts(up_own[step], up_got[step], do_all)
    out_own, out_send = stacked_grads(o_chip, [dr, dr_got], up_at, dprows)
    out_got = shift(out_send, "x")

    down_first = ring_first(down_y, "z")
    sums = [None] * nz
    for step in early:
        own_y, got_y = send_parts(up_x[step].reshape(ny, nc * wrows, ffh), "y")
        sums[step] = add_parts(own_y, got_y, do_all)
    up_first = ring_first(sums, "z")
    do_all = after(do_all, *[t for t in down_y + up_x + down_own + up_own if t is not None])
    dqkv = call(
        functools.partial(attend_back_kernel, spans, lanes),
        shaped((length, 3 * hw), BF16),
        [IN_SMEM] + [IN_VMEM] * 6,
        [pltpu.VMEM((length, lanes), F32)] * 2,
        vmem=20,
    )(sorted_at, qkv, attn, do_all, lse, cos_lanes, sin_lanes)
    dqkv = after(dqkv, *([t for step in late for t in up_got[step]] + [sums[step] for step in early]))
    qkv_own, qkv_send = stacked_grads(a1, [dqkv], up_at, dprows)
    qkv_got = shift(qkv_send, "x")
    da1_keep, da1_send = call(
        functools.partial(input_back_kernel, nqo, q_off),
        (shaped((ny, rows_here, width), F32), shaped((ny, rows_here, width), BF16)),
        [IN_SMEM, IN_VMEM] + [ANYWHERE] * nqo,
        [pltpu.VMEM((width, 3 * hw), BF16), sems(nqo)],
    )(up_at, after(dqkv, qkv_own, *down_first), *q_back)
    da1_got = shift(da1_send, "c")
    sent_on = [(da1_keep[sy] + da1_got[sy].astype(F32)).astype(BF16) for sy in range(1, ny)]
    arrived = [shift(item, "y", ny - sy) for sy, item in enumerate(sent_on, 1)]
    da1_keep = after(da1_keep, *(up_first + down_first + [t for step in late for t in down_got[step]]))
    grad_tokens, grads_0 = call(
        bottom_kernel,
        (shaped((rows_here, width), BF16), shaped((2, width), F32)),
        [IN_VMEM] * (5 + len(arrived)),
    )(tok, dh, norms, da1_keep[0], da1_got[0], *arrived)
    grad_tokens = grad_tokens.reshape(tokens.shape)
    out_tokens = out_tokens.reshape(tokens.shape)

    for step in range(nz):
        if down_y[step] is None:
            down_y[step] = add_parts(down_own[step], down_got[step], sent_on[0])
    down = ring_rest(down_y, down_first, "z").astype(BF16)
    down = scatter_sum(down.reshape(nx, ffrows, width), "x")
    for step in late:
        part = add_parts(up_own[step], up_got[step], qkv_own)
        own_y, got_y = send_parts(part.reshape(ny, nc * wrows, ffh), "y")
        sums[step] = add_parts(own_y, got_y, arrived[0])
    up = ring_rest(sums, up_first, "z").reshape(nc, wrows, ffh)
    up_got = shift(take(up, 1 - ic), "c")
    if aligned:
        up = call(
            functools.partial(up_kernel, (nz, nx, ny, ffrows)),
            shaped((wrows, ff), F32),
            [IN_SMEM] + [IN_VMEM] * 2,
        )(core, take(up, ic), up_got)
    else:
        up = pair(take(up, ic), up_got, ic)
        up = up.reshape(nc, wrows, nz, ny, nx, ffrows).transpose(1, 2, 4, 3, 0, 5).reshape(wrows, ff)

    out_x = add_parts(out_own, [out_got], qkv_got)
    qkv_x = (qkv_own.astype(F32) + qkv_got.astype(F32)).astype(BF16)
    both = jnp.concatenate([out_x, qkv_x], -1)
    both = ring_scatter([both[step] for step in range(nz)], "z").astype(BF16)
    out, qkv_g = both[:, :owh], both[:, owh:]
    out = scatter_sum(out.reshape(ny, nc * wrows, owh), "y").reshape(nc, wrows, owh)
    out_got = shift(take(out, 1 - ic), "c")
    qkv_g = exchange(qkv_g.reshape(ny, nc * wrows, 3 * hw), "y")
    qkv_g = qkv_g.reshape(ny, nc, wrows, 3 * hw)
    qkv_got = shift(take(qkv_g, 1 - ic, 1), "c")
    if aligned:
        qkv_g, out = call(
            qkv_out_kernel,
            (shaped((wrows, 3 * width), F32), shaped((wrows, width), F32)),
            [IN_SMEM] + [IN_VMEM] * 4,
        )(core, take(qkv_g, ic, 1), qkv_got, take(out, ic), out_got)
    else:
        out = pair(take(out, ic), out_got, ic).transpose(1, 0, 2).reshape(wrows, width)
        qkv_g = pair(take(qkv_g, ic, 1), qkv_got, ic)
        qkv_g = qkv_g.reshape(nc, ny, wrows, 3, hw).transpose(2, 3, 1, 0, 4)
        qkv_g = qkv_g.reshape(wrows, 3 * width).astype(F32)

    norm_sums = jnp.concatenate(
        [
            grads_0[0:1],
            grads_21[2:3],
            grads_21[0:1],
            grads_3[0:1],
            grads_0[1:2],
            grads_21[3:4],
            grads_21[1:2],
            grads_3[1:2],
        ],
        0,
    )
    norm_sums = after(norm_sums)
    for axis in "cyxz":
        norm_sums = all_sum(norm_sums, axis)
    place = ((iz * nx + ix) * ny + iy) * nc + ic
    norm_sums = lax.dynamic_slice(norm_sums, (0, place * wrows), (8, wrows))
    return (out_tokens, grad_tokens, qkv_g, out, up, down, norm_sums[:4], norm_sums[4:])


def solution(mesh):
    fine = Mesh(
        mesh.devices.reshape(mesh.shape["dp"] // 2, 2, mesh.shape["blk"] // 2, 2),
        ("z", "x", "y", "c"),
    )
    dp, blk, every = ("z", "x"), ("y", "c"), ("z", "x", "y", "c")
    return jax.shard_map(
        on_device,
        mesh=fine,
        in_specs=(
            P(blk, dp, None),
            P(blk, dp, None),
            P(dp),
            P(),
            P(dp, None),
            P(every, None),
            P(every, None),
            P(every, None),
            P(every, None),
            P(None, every),
            P(None, every),
        ),
        out_specs=(
            P(blk, dp, None),
            P(blk, dp, None),
            P(every, None),
            P(every, None),
            P(every, None),
            P(every, None),
            P(None, every),
            P(None, every),
        ),
        check_vma=False,
    )
```

```python
import functools
import math

import jax
import jax.numpy as jnp
from jax import lax
from jax.experimental import pallas as pl
from jax.experimental.pallas import tpu as pltpu
from jax.sharding import Mesh
from jax.sharding import PartitionSpec as P

HD = 64
F32 = jnp.float32
BF16 = jnp.bfloat16


def shift(value, axis, step=1):
    size = lax.axis_size(axis)
    return lax.ppermute(value, axis, [(i, (i + step) % size) for i in range(size)])


def after(value, *others):
    return lax.optimization_barrier((value,) + others)[0]


def back(axis, step):
    size = lax.axis_size(axis)
    return lax.rem(lax.axis_index(axis) + size - step, size)


def take(array, at, axis=0):
    return lax.dynamic_index_in_dim(array, at, axis, keepdims=False)


def direct_gather(piece, axis):
    size = lax.axis_size(axis)
    return [piece] + [shift(piece, axis, step) for step in range(1, size)]


def ring_gather(piece, axis, gate=()):
    size = lax.axis_size(axis)
    pieces = [piece] * size
    for step in range(1, size // 2 + 1):
        last = pieces[step - 1]
        pieces[step] = shift(after(last, *gate) if gate and step > 1 else last, axis)
    for step in range(size - 1, size // 2, -1):
        last = pieces[(step + 1) % size]
        pieces[step] = shift(after(last, *gate) if gate and step < size - 1 else last, axis, -1)
    return pieces


def in_order(pieces, axis):
    if len(pieces) == 2:
        return pair(pieces[0], pieces[1], lax.axis_index(axis))
    buffer = jnp.zeros((len(pieces),) + pieces[0].shape, pieces[0].dtype)
    for step, piece in enumerate(pieces):
        at = (back(axis, step),) + (0,) * piece.ndim
        buffer = lax.dynamic_update_slice(buffer, piece[None], at)
    return buffer


def pair(own, other, index):
    first = jnp.where(index == 0, own, other)
    second = jnp.where(index == 0, other, own)
    return jnp.stack([first, second])


def ring_first(parts, axis):
    size = len(parts)
    half = size // 2
    found = [shift(parts[half].astype(BF16), axis)]
    if size - 1 - half:
        found.append(shift(parts[size - 1 - half].astype(BF16), axis, -1))
    return found


def ring_rest(parts, arrived, axis):
    size = len(parts)
    half = size // 2
    total = parts[0].astype(F32)
    for carry, count, way in zip(arrived, (half, size - 1 - half), (1, -1)):
        for far in range(count - 1, 0, -1):
            part = parts[size - far if way == 1 else far]
            carry = shift((carry.astype(F32) + part.astype(F32)).astype(BF16), axis, way)
        total = total + carry.astype(F32)
    return total


def ring_scatter(parts, axis):
    return ring_rest(parts, ring_first(parts, axis), axis)


def scatter_sum(parts, axis):
    size = parts.shape[0]
    return ring_scatter([take(parts, back(axis, step)) for step in range(size)], axis)


def late_last(size):
    half = size // 2
    steps = list(range(half, 0, -1)) + list(range(half + 1, size)) + [0]
    return list(dict.fromkeys(steps))


def send_parts(parts, axis):
    size = parts.shape[0]
    got = [shift(take(parts, back(axis, step)), axis, size - step) for step in range(1, size)]
    return take(parts, lax.axis_index(axis)), got


def add_parts(own, got, when):
    total = own.astype(F32)
    for item in got:
        total = total + after(item, when).astype(F32)
    return total.astype(BF16)


def exchange(parts, axis):
    size = parts.shape[0]
    index = lax.axis_index(axis)
    pieces = [take(parts, index)]
    for step in range(1, size):
        pieces.append(shift(take(parts, lax.rem(index + step, size)), axis, step))
    return in_order(pieces, axis)


def all_sum(value, axis):
    pieces = direct_gather(value, axis)
    total = pieces[0]
    for piece in pieces[1:]:
        total = total + piece
    return total


IN_VMEM = pl.BlockSpec(memory_space=pltpu.VMEM)
IN_SMEM = pl.BlockSpec(memory_space=pltpu.SMEM)
ANYWHERE = pl.BlockSpec(memory_space=pl.ANY)
IN_HBM = pl.BlockSpec(memory_space=pltpu.HBM)


def call(kernel, out_shape, in_specs, scratch=(), vmem=16):
    several = isinstance(out_shape, (tuple, list))
    return pl.pallas_call(
        kernel,
        out_shape=out_shape,
        in_specs=in_specs,
        out_specs=[IN_VMEM] * len(out_shape) if several else IN_VMEM,
        scratch_shapes=list(scratch),
        compiler_params=pltpu.CompilerParams(vmem_limit_bytes=vmem * 1024 * 1024),
        cost_estimate=pl.CostEstimate(flops=1024, bytes_accessed=1024, transcendentals=0),
    )


def fetch(pieces, at_ref, target, sems, first, offset=0, columns=None):
    copies = []
    for number, piece in enumerate(pieces):
        rows = piece.shape[0]
        source = piece if columns is None else piece.at[:, pl.ds(offset, columns)]
        place = pl.ds(pl.multiple_of(at_ref[number] * rows, rows), rows)
        copies.append(pltpu.make_async_copy(source, target.at[place], sems.at[first + number]))
    for copy in copies:
        copy.start()
    return copies


def wait_all(copies):
    for copy in copies:
        copy.wait()


def partner(values):
    half = HD // 2
    if values.shape[-1] == HD:
        return jnp.concatenate([values[:, half:], values[:, :half]], -1)
    lanes = values.shape[-1]
    lane = lax.broadcasted_iota(jnp.int32, values.shape, 1)
    low = lax.rem(lane, HD) < half
    return jnp.where(low, pltpu.roll(values, lanes - half, 1), pltpu.roll(values, half, 1))


def attend_kernel(blocks, lanes, order_ref, qkv_ref, o_ref, lse_ref):
    length, third = o_ref.shape
    size = length // blocks
    per = lanes // HD
    lane = lax.broadcasted_iota(jnp.int32, (1, lanes), 1) // HD
    row = lax.broadcasted_iota(jnp.int32, (size, size), 0)
    col = lax.broadcasted_iota(jnp.int32, (size, size), 1)
    for group in range(third // lanes):
        left = group * lanes

        def one_row(i):
            at = pl.multiple_of(order_ref[i] * size, size)
            q = qkv_ref[pl.ds(at, size), left : left + lanes]
            outs, totals = [], []
            for head in range(per):
                qh = q * (lane == head).astype(BF16)

                def scores(start):
                    k = qkv_ref[pl.ds(start, size), third + left : third + left + lanes]
                    return lax.dot_general(qh, k, (((1,), (1,)), ((), ())), preferred_element_type=F32)

                def values(p, start):
                    v = qkv_ref[pl.ds(start, size), 2 * third + left : 2 * third + left + lanes]
                    return jnp.dot(p.astype(BF16), v, preferred_element_type=F32)

                s = jnp.where(col <= row, scores(at), -1e30)
                top = jnp.max(s, -1, keepdims=True)
                p = jnp.exp(s - top)
                state = (top, jnp.sum(p, -1, keepdims=True), values(p, at))

                def step(j, state):
                    top, total, acc = state
                    start = pl.multiple_of(order_ref[j] * size, size)
                    s = scores(start)
                    new = jnp.maximum(top, jnp.max(s, -1, keepdims=True))
                    factor = jnp.exp(top - new)
                    p = jnp.exp(s - new)
                    total = total * factor + jnp.sum(p, -1, keepdims=True)
                    return new, total, acc * factor + values(p, start)

                if blocks <= 4:
                    for j in range(i):
                        state = step(j, state)
                else:
                    state = lax.fori_loop(0, i, step, state)
                top, total, acc = state
                outs.append(acc / total)
                column = group * per + head
                lse_ref[pl.ds(at, size), column : column + 1] = top + jnp.log(total)
            out = outs[0]
            for head in range(1, per):
                out = jnp.where(lane == head, outs[head], out)
            o_ref[pl.ds(at, size), left : left + lanes] = out.astype(BF16)

        if blocks <= 4:
            for i in range(blocks):
                one_row(i)
        else:
            pl.loop(0, blocks)(one_row)


def attend_back_kernel(
    blocks, lanes, order_ref, qkv_ref, o_ref, do_ref, lse_ref, cos_ref, sin_ref, out_ref,
    dk_ref, dv_ref, delta_ref, rows_ref,
):
    length, third = o_ref.shape
    size = length // blocks
    per = lanes // HD
    lane = lax.broadcasted_iota(jnp.int32, (1, lanes), 1) // HD
    row = lax.broadcasted_iota(jnp.int32, (size, size), 0)
    col = lax.broadcasted_iota(jnp.int32, (size, size), 1)
    nt = (((1,), (1,)), ((), ()))
    tn = (((0,), (0,)), ((), ()))

    def unturn(values, rows):
        return values * cos_ref[rows, :] - partner(values) * sin_ref[rows, :]

    delta_ref[...] = jnp.zeros_like(delta_ref)
    for start in range(0, length, size):
        rows = pl.ds(start, size)
        for left in range(0, third, lanes):
            prod = do_ref[rows, left : left + lanes].astype(F32) * o_ref[rows, left : left + lanes].astype(F32)
            for head in range(per):
                column = left // HD + head
                total = jnp.sum(jnp.where(lane == head, prod, 0.0), -1, keepdims=True)
                delta_ref[rows, column : column + 1] = total
    rows_ref[0] = jnp.transpose(lse_ref[...])[: rows_ref.shape[1], :]
    rows_ref[1] = jnp.transpose(delta_ref[...])[: rows_ref.shape[1], :]

    for group in range(third // lanes):
        left = group * lanes
        dk_ref[...] = jnp.zeros_like(dk_ref)
        dv_ref[...] = jnp.zeros_like(dv_ref)

        def one_row(i):
            at = pl.multiple_of(order_ref[i] * size, size)
            rows = pl.ds(at, size)
            q = qkv_ref[rows, left : left + lanes]
            do = do_ref[rows, left : left + lanes]
            grads = []
            for head in range(per):
                own = (lane == head).astype(BF16)
                qh, doh = q * own, do * own
                number = group * per + head
                lse = rows_ref[0, number : number + 1, rows]
                delta = rows_ref[1, number : number + 1, rows]

                def step(start, diagonal):
                    where = pl.ds(start, size)
                    k = qkv_ref[where, third + left : third + left + lanes]
                    v = qkv_ref[where, 2 * third + left : 2 * third + left + lanes]
                    s = lax.dot_general(k, qh, nt, preferred_element_type=F32)
                    p = jnp.exp(s - lse)
                    if diagonal:
                        p = jnp.where(row <= col, p, 0.0)
                    dp = lax.dot_general(v, doh, nt, preferred_element_type=F32)
                    ds = (p * (dp - delta)).astype(BF16)
                    dv_ref[where, :] += jnp.dot(p.astype(BF16), doh, preferred_element_type=F32)
                    dk_ref[where, :] += jnp.dot(ds, qh, preferred_element_type=F32)
                    return lax.dot_general(ds, k, tn, preferred_element_type=F32)

                dq = step(at, True)
                if blocks <= 4:
                    for j in range(i):
                        dq = dq + step(pl.multiple_of(order_ref[j] * size, size), False)
                else:
                    dq = lax.fori_loop(
                        0, i, lambda j, c: c + step(pl.multiple_of(order_ref[j] * size, size), False), dq
                    )
                grads.append(dq)
            dq = grads[0]
            for head in range(1, per):
                dq = jnp.where(lane == head, grads[head], dq)
            out_ref[rows, left : left + lanes] = unturn(dq * 0.125, rows).astype(BF16)

        if blocks <= 4:
            for i in range(blocks):
                one_row(i)
        else:
            pl.loop(0, blocks)(one_row)
        for start in range(0, length, size):
            rows = pl.ds(start, size)
            out_ref[rows, third + left : third + left + lanes] = unturn(dk_ref[rows, :], rows).astype(BF16)
            out_ref[rows, 2 * third + left : 2 * third + left + lanes] = dv_ref[rows, :].astype(BF16)


GELU_A = math.sqrt(2.0 / math.pi)
GELU_B = 0.044715


NT = (((1,), (1,)), ((), ()))
TN = (((0,), (0,)), ((), ()))


def normed(values):
    centred = values - jnp.mean(values, -1, keepdims=True)
    scale = lax.rsqrt(jnp.mean(centred * centred, -1, keepdims=True) + 1e-05)
    return centred * scale, scale


def normed_back(grad, gain, vhat, scale):
    scaled = grad * gain
    return scale * (
        scaled - jnp.mean(scaled, -1, keepdims=True) - vhat * jnp.mean(scaled * vhat, -1, keepdims=True)
    )


def column_sum(values):
    return jnp.sum(values, 0, keepdims=True)


def halves(core_ref, width):
    own = pl.ds(pl.multiple_of(core_ref[0] * width, width), width)
    other = pl.ds(pl.multiple_of((1 - core_ref[0]) * width, width), width)
    return own, other


def cut_kernel(sizes, core_ref, qkv_in, out_in, up_in, norm_ref, keep_ref, send_ref, qkv_ref, out_ref, up_ref, sems):
    nz, nx, ny, hw, ffrows = sizes
    width, owh = out_ref.shape[1], out_ref.shape[1] // 2
    pairs = ((qkv_in, qkv_ref), (out_in, out_ref), (up_in, up_ref))
    copies = [pltpu.make_async_copy(a, b, sems.at[n]) for n, (a, b) in enumerate(pairs)]
    for copy in copies:
        copy.start()
    wait_all(copies)
    for target, core in ((keep_ref, core_ref[0]), (send_ref, 1 - core_ref[0])):
        at = 0
        for y in range(ny):
            for part in range(3):
                left = pl.multiple_of(part * width + (y * 2 + core) * hw, hw)
                target[:, at : at + hw] = qkv_ref[:, pl.ds(left, hw)]
                at += hw
        target[:, at : at + owh] = out_ref[:, pl.ds(pl.multiple_of(core * owh, owh), owh)]
        at += owh
        target[:, at : at + 128] = norm_ref[...]
        at += 128
        for z in range(nz):
            for y in range(ny):
                for x in range(nx):
                    left = pl.multiple_of((((z * nx + x) * ny + y) * 2 + core) * ffrows, ffrows)
                    target[:, at : at + ffrows] = up_ref[:, pl.ds(left, ffrows)]
                    at += ffrows


def up_kernel(sizes, core_ref, own_ref, got_ref, up_ref):
    nz, nx, ny, ffrows = sizes
    for source, core in ((own_ref, core_ref[0]), (got_ref, 1 - core_ref[0])):
        at = 0
        for z in range(nz):
            for y in range(ny):
                for x in range(nx):
                    left = pl.multiple_of((((z * nx + x) * ny + y) * 2 + core) * ffrows, ffrows)
                    up_ref[:, pl.ds(left, ffrows)] = source[:, at : at + ffrows]
                    at += ffrows


def qkv_out_kernel(core_ref, own_ref, got_ref, out_own_ref, out_got_ref, qkv_ref, out_ref):
    ny, hw = own_ref.shape[0], own_ref.shape[2] // 3
    width, owh = out_ref.shape[1], out_own_ref.shape[1]
    own, other = halves(core_ref, owh)
    out_ref[:, own] = out_own_ref[...]
    out_ref[:, other] = out_got_ref[...]
    for source, core in ((own_ref, core_ref[0]), (got_ref, 1 - core_ref[0])):
        for y in range(ny):
            for part in range(3):
                left = pl.multiple_of(part * width + (y * 2 + core) * hw, hw)
                qkv_ref[:, pl.ds(left, hw)] = source[y, :, part * hw : part * hw + hw].astype(F32)


def input_kernel(count, blocks, lanes, q_off, n_off, at_ref, cos_ref, sin_ref, *refs):
    toks, refs = refs[:blocks], refs[blocks:]
    q_pieces, n_pieces, refs = refs[:count], refs[count : 2 * count], refs[2 * count :]
    a_ref, out_ref, norm_ref, weight, columns, sems = refs
    wide = out_ref.shape[1]
    first = fetch(n_pieces, at_ref, columns, sems, 0, n_off, 128)
    later = fetch(q_pieces, at_ref, weight, sems, count, q_off, wide)
    wait_all(first)
    norm_ref[...] = jnp.transpose(columns[...].astype(F32))[:8, :]
    gain, bias = norm_ref[0:1, :], norm_ref[4:5, :]
    rows_here = toks[0].shape[0]
    for number, tok_ref in enumerate(toks):
        vhat, _ = normed(tok_ref[...].astype(F32))
        a_ref[pl.ds(number * rows_here, rows_here), :] = (vhat * gain + bias).astype(BF16)
    wait_all(later)
    third = wide // 3
    block = 256
    for start in range(0, out_ref.shape[0], block):
        rows = pl.ds(start, block)
        acc = jnp.dot(a_ref[rows, :], weight[...], preferred_element_type=F32)
        cos, sin = cos_ref[rows, :], sin_ref[rows, :]
        for part in range(3):
            for left in range(0, third, lanes):
                at = part * third + left
                values = acc[:, at : at + lanes]
                if part < 2:
                    values = values * cos + partner(values) * sin
                if part == 0:
                    values = values * 0.125
                out_ref[rows, at : at + lanes] = values.astype(BF16)


def out_kernel(count, ny, at_ref, core_ref, *refs):
    near, far, refs = refs[:ny], refs[ny : 2 * ny], refs[2 * ny :]
    y_ref, pieces, refs = refs[0], refs[1 : 1 + count], refs[1 + count :]
    keep_ref, send_ref, chip_ref, weight, sems = refs
    copies = fetch(pieces, at_ref, weight, sems, 0, 0, weight.shape[1])
    core = core_ref[0]
    rows, hw = near[0].shape[1], near[0].shape[2]
    for parts, is_far in ((near, False), (far, True)):
        other = 1 - core if is_far else core
        for ahead in range(ny):
            yh = lax.rem(y_ref[0] + ahead, ny)
            for sc in range(2):
                token = pl.ds(((1 - sc) if is_far else sc) * rows, rows)
                value = parts[ahead][sc]
                if hw % 128 == 0:
                    left = pl.multiple_of((yh * 2 + other) * hw, hw)
                    chip_ref[token, pl.ds(left, hw)] = value
                else:
                    for place in range(2 * ny):

                        @pl.when(yh * 2 + other == place)
                        def _(place=place, value=value, token=token):
                            chip_ref[token, place * hw : place * hw + hw] = value

    wait_all(copies)
    send_ref[...] = jnp.dot(chip_ref[rows:, :], weight[...], preferred_element_type=F32)
    keep_ref[...] = jnp.dot(chip_ref[:rows, :], weight[...], preferred_element_type=F32)


def middle_kernel(core_ref, keep_ref, got_ref, tok_ref, norm_ref, h_ref, a_ref, r_ref):
    own, other = halves(core_ref, keep_ref.shape[1])
    r_ref[:, own] = keep_ref[...]
    r_ref[:, other] = got_ref[...]
    vhat, _ = normed(r_ref[...])
    h = tok_ref[...].astype(F32) + vhat * norm_ref[1:2, :] + norm_ref[5:6, :]
    h_ref[...] = h
    vhat, _ = normed(h)
    a_ref[...] = (vhat * norm_ref[2:3, :] + norm_ref[6:7, :]).astype(BF16)


def mlp_kernel(ups, downs, up_at, down_at, own_ref, got_ref, *refs):
    up_pieces, down_pieces = refs[:ups], refs[ups : ups + downs]
    keep_ref, send_ref, u_ref, slope_ref, up, down, sems = refs[ups + downs :]
    copies = fetch(up_pieces, up_at, up, sems, 0)
    later = fetch(down_pieces, down_at, down, sems, ups)
    wait_all(copies)
    count, wide = own_ref.shape[0], u_ref.shape[1]
    step = min(512, wide)
    for start, a_ref in ((count, got_ref), (0, own_ref)):
        rows = pl.ds(start, count)
        for left in range(0, wide, step):
            z = jnp.dot(a_ref[...], up[:, left : left + step], preferred_element_type=F32)
            square = z * z
            t = jnp.tanh(GELU_A * z * (1.0 + GELU_B * square))
            half = 0.5 * (1.0 + t)
            u_ref[rows, left : left + step] = (z * half).astype(BF16)
            slope = half + 0.5 * z * (1.0 - t * t) * (GELU_A * (1.0 + 3.0 * GELU_B * square))
            slope_ref[rows, left : left + step] = slope.astype(BF16)
    wait_all(later)
    send_ref[...] = jnp.dot(u_ref[count:, :], down[...], preferred_element_type=F32).astype(BF16)
    keep_ref[...] = jnp.dot(u_ref[:count, :], down[...], preferred_element_type=F32)


def top_kernel(scale_ref, keep_ref, got_ref, h_ref, cot_ref, norm_ref, out_ref, dm_ref, grad_ref):
    vhat, scale = normed(keep_ref[...] + got_ref[...].astype(F32))
    gain = norm_ref[3:4, :]
    out_ref[...] = (h_ref[...] + vhat * gain + norm_ref[7:8, :]).astype(BF16)
    g = cot_ref[...].astype(F32) * scale_ref[0]
    dm_ref[...] = normed_back(g, gain, vhat, scale).astype(BF16)
    grad_ref[0:1, :] = column_sum(g * vhat)
    grad_ref[1:2, :] = column_sum(g)


def mlp_back_kernel(ups, downs, up_at, down_at, own_ref, got_ref, slope_ref, *refs):
    up_pieces, down_pieces = refs[:ups], refs[ups : ups + downs]
    keep_ref, send_ref, dz_ref, up, down, sems = refs[ups + downs :]
    copies = fetch(down_pieces, down_at, down, sems, ups)
    later = fetch(up_pieces, up_at, up, sems, 0)
    wait_all(copies)
    count, wide = own_ref.shape[0], dz_ref.shape[1]
    step = min(512, wide)
    for start, dm_ref in ((count, got_ref), (0, own_ref)):
        rows = pl.ds(start, count)
        for left in range(0, wide, step):
            du = lax.dot_general(dm_ref[...], down[left : left + step, :], NT, preferred_element_type=F32)
            slope = slope_ref[rows, left : left + step].astype(F32)
            dz_ref[rows, left : left + step] = (du * slope).astype(BF16)
    wait_all(later)
    send = lax.dot_general(dz_ref[count:, :], up[...], NT, preferred_element_type=F32)
    send_ref[...] = send.astype(BF16)
    keep_ref[...] = lax.dot_general(dz_ref[:count, :], up[...], NT, preferred_element_type=F32)


def between_kernel(
    core_ref, scale_ref, da_ref, da_got_ref, h_ref, keep_ref, got_ref, cot_ref, norm_ref,
    dh_ref, own_ref, send_ref, grad_ref, r_ref, dr_ref,
):
    own, other = halves(core_ref, keep_ref.shape[1])
    r_ref[:, own] = keep_ref[...]
    r_ref[:, other] = got_ref[...]
    e = da_ref[...] + da_got_ref[...].astype(F32)
    vhat, scale = normed(h_ref[...])
    grad_ref[0:1, :] = column_sum(e * vhat)
    grad_ref[1:2, :] = column_sum(e)
    g = cot_ref[...].astype(F32) * scale_ref[0]
    dh = g + normed_back(e, norm_ref[2:3, :], vhat, scale)
    dh_ref[...] = dh
    vhat, scale = normed(r_ref[...])
    grad_ref[2:3, :] = column_sum(dh * vhat)
    grad_ref[3:4, :] = column_sum(dh)
    dr_ref[...] = normed_back(dh, norm_ref[1:2, :], vhat, scale).astype(BF16)
    own_ref[...] = dr_ref[:, own]
    send_ref[...] = dr_ref[:, other]


def out_back_kernel(count, ny, at_ref, core_ref, own_ref, got_ref, *refs):
    pieces = refs[:count]
    keep_ref, send_ref, weight, sems = refs[count:]
    wait_all(fetch(pieces, at_ref, weight, sems, 0, 0, weight.shape[1]))
    core = core_ref[0]
    hw = keep_ref.shape[2]
    size = own_ref.shape[0]
    for own in (False, True):
        head = core if own else 1 - core
        for yh in range(ny):
            rows = pl.ds(pl.multiple_of((yh * 2 + head) * hw, hw), hw)
            for start, dr_ref in ((0, own_ref), (size, got_ref)):
                value = lax.dot_general(dr_ref[...], weight[rows, :], NT, preferred_element_type=F32)
                if own:
                    keep_ref[yh, pl.ds(start, size), :] = value
                else:
                    send_ref[yh, pl.ds(start, size), :] = value.astype(BF16)


def input_back_kernel(count, offset, at_ref, a_ref, *refs):
    pieces = refs[:count]
    keep_ref, send_ref, weight, sems = refs[count:]
    wait_all(fetch(pieces, at_ref, weight, sems, 0, offset, weight.shape[1]))
    block = keep_ref.shape[1]
    for number in range(a_ref.shape[0] // block):
        rows = pl.ds(number * block, block)
        value = lax.dot_general(a_ref[rows, :], weight[...], NT, preferred_element_type=F32)
        if number % 2 == 0:
            keep_ref[number // 2] = value
        else:
            send_ref[number // 2] = value.astype(BF16)


def bottom_kernel(*refs):
    tok_ref, dh_ref, norm_ref = refs[:3]
    pieces, (out_ref, grad_ref) = refs[3:-2], refs[-2:]
    e = pieces[0][...].astype(F32)
    for piece in pieces[1:]:
        e = e + piece[...].astype(F32)
    vhat, scale = normed(tok_ref[...].astype(F32))
    out_ref[...] = (dh_ref[...] + normed_back(e, norm_ref[0:1, :], vhat, scale)).astype(BF16)
    grad_ref[0:1, :] = column_sum(e * vhat)
    grad_ref[1:2, :] = column_sum(e)


def stacked_kernel(parts, cols, at_ref, left_ref, *refs):
    rights, (own_ref, send_ref) = refs[:parts], refs[parts:]
    size = rights[0].shape[0]
    for number in range(2 * own_ref.shape[0]):
        columns = pl.ds(pl.multiple_of(at_ref[number] * cols, cols), cols)
        total = None
        for place, right in enumerate(rights):
            left = left_ref[place * size : place * size + size, columns]
            value = lax.dot_general(left, right[...], TN, preferred_element_type=F32)
            total = value if total is None else total + value
        target = send_ref if number % 2 else own_ref
        target[number // 2] = total.astype(BF16)


def stacked_grads(left, rights, at, cols):
    wide, count = rights[0].shape[1], left.shape[1] // cols // 2
    if cols % 128:
        blocks = grads(left, rights, at, cols, range(2 * count))
        return jnp.stack(blocks[0::2]), jnp.stack(blocks[1::2])
    return call(
        functools.partial(stacked_kernel, len(rights), cols),
        [jax.ShapeDtypeStruct((count, cols, wide), BF16)] * 2,
        [IN_SMEM] + [IN_VMEM] * (1 + len(rights)),
    )(at, left, *rights)


def blocks_kernel(parts, cols, numbers, at_ref, left_ref, *refs):
    rights, outs = refs[:parts], refs[parts:]
    size = rights[0].shape[0]
    for number, out_ref in zip(numbers, outs):
        columns = pl.ds(pl.multiple_of(at_ref[number] * cols, cols), cols)
        total = None
        for place, right in enumerate(rights):
            left = left_ref[place * size : place * size + size, columns]
            value = lax.dot_general(left, right[...], TN, preferred_element_type=F32)
            total = value if total is None else total + value
        out_ref[...] = total.astype(BF16)


def grads(left, rights, at, cols, numbers):
    if cols % 128 == 0:
        return call(
            functools.partial(blocks_kernel, len(rights), cols, tuple(numbers)),
            [jax.ShapeDtypeStruct((cols, rights[0].shape[1]), BF16)] * len(numbers),
            [IN_SMEM] + [IN_VMEM] * (1 + len(rights)),
        )(at, left, *rights)
    right = jnp.concatenate(rights, 0)
    found = []
    for number in numbers:
        block = lax.dynamic_slice(left, (0, at[number] * cols), (left.shape[0], cols))
        found.append(lax.dot_general(block, right, TN, preferred_element_type=F32).astype(BF16))
    return found


def on_device(
    tokens,
    cotangent,
    group_ids,
    group_weight,
    block_order,
    w_qkv,
    w_out,
    w_up,
    w_down,
    norm_gain,
    norm_bias,
):
    nz, nx, ny, nc = (lax.axis_size(a) for a in "zxyc")
    iz, ix, iy, ic = (lax.axis_index(a) for a in "zxyc")
    rows_here, _, width = tokens.shape
    heads = width // HD
    spans = ny * nc
    mine = heads // spans
    hw = mine * HD
    lanes = min(128, hw)
    wrows = w_qkv.shape[0]
    ffrows = w_down.shape[0]
    ff = w_up.shape[1]
    ffh = ff // nc
    owh = width // nc
    dprows = spans * wrows
    length = spans * rows_here
    crow = nc * rows_here
    half = nz // 2
    shaped = jax.ShapeDtypeStruct

    def middle(pieces):
        return pieces[1:2] + pieces[-1:]

    def sems(count):
        return pltpu.SemaphoreType.DMA((count,))

    tok = tokens.reshape(rows_here, width)
    cot = cotangent.reshape(rows_here, width)
    norm_rows = jnp.concatenate([norm_gain, norm_bias], 0).T
    norm_rows = jnp.pad(norm_rows, ((0, 0), (0, 120)))
    core = ic.astype(jnp.int32).reshape(1)
    aligned = hw % 128 == 0 and ffrows % 128 == 0
    if aligned:
        keep, send = call(
            functools.partial(cut_kernel, (nz, nx, ny, hw, ffrows)),
            [shaped((wrows, ny * 3 * hw + owh + 128 + ffh), BF16)] * 2,
            [IN_SMEM] + [ANYWHERE] * 3 + [IN_VMEM],
            [pltpu.VMEM(item.shape, BF16) for item in (w_qkv, w_out, w_up)] + [sems(3)],
        )(core, *(pltpu.with_memory_space_constraint(w, pltpu.HBM) for w in (w_qkv, w_out, w_up)), norm_rows)
    else:
        norm_rows = jnp.broadcast_to(norm_rows[None], (nc, wrows, 128))
        cut = jnp.concatenate(
            [
                w_qkv.reshape(wrows, 3, ny, nc, hw).transpose(3, 0, 2, 1, 4).reshape(nc, wrows, -1),
                w_out.reshape(wrows, nc, owh).transpose(1, 0, 2),
                norm_rows,
                w_up.reshape(wrows, nz, nx, ny, nc, ffrows)
                .transpose(4, 0, 1, 3, 2, 5)
                .reshape(nc, wrows, ffh),
            ],
            -1,
        )
        keep, send = take(cut, ic), take(cut, 1 - ic)
    cut = pair(keep, shift(send, "c"), ic).reshape(nc * wrows, -1)
    q_cut = cut[:, : ny * 3 * hw].reshape(nc * wrows, ny, 3 * hw)
    left = ny * 3 * hw
    o_cut = jnp.broadcast_to(cut[:, None, left : left + owh + 128], (nc * wrows, ny, owh + 128))
    up_cut = cut[:, left + owh + 128 :]
    qo = exchange(jnp.concatenate([o_cut, q_cut], -1).transpose(1, 0, 2), "y")
    qo = qo.reshape(dprows, owh + 128 + 3 * hw)
    down_pieces = ring_gather(w_down, "x")
    span_y = iy.astype(jnp.int32).reshape(1)

    qo_z = ring_gather(qo, "z")
    up_z = ring_gather(up_cut, "z")
    tok_y = ring_gather(after(tok, *[qo]), "y")
    tok_all = []
    for item in tok_y:
        item = item if not tok_all else after(item, *qo_z)
        tok_all.append(item)
        tok_all.append(shift(item, "c"))
    qo_w, up_w, down_w = [], [], []
    up_at, down_at = [], []
    for step, item in enumerate(qo_z):
        for far, piece in enumerate(ring_gather(item, "x")):
            qo_w.append(piece)
            up_at.append(back("z", step) * nx + back("x", far))
    up_use = [after(up_z[0], *[qo])] + [after(item, *middle(qo_z)) for item in up_z[1:]]
    up_use[half] = after(up_use[half], *[qo_z[half]])
    up_y = []
    for item in up_use:
        pieces = ring_gather(item, "y")
        pieces = pieces[:1] + [after(piece, *qo_w) for piece in pieces[1:]]
        up_y.append(in_order(pieces, "y").reshape(dprows, ffh))
        up_w += ring_gather(up_y[-1], "x")
    down_pieces = [down_pieces[0]] + [after(item, *qo_z) for item in down_pieces[1:]]
    down_z = ring_gather(in_order(down_pieces, "x").reshape(nx * ffrows, width), "z")
    for step, item in enumerate(down_z):
        for far, piece in enumerate(ring_gather(item, "y")):
            down_w.append(piece)
            down_at.append(back("z", step) * ny + back("y", far))
    up_at = jnp.stack(up_at).astype(jnp.int32)
    down_at = jnp.stack(down_at).astype(jnp.int32)
    q_w, o_w, q_off = qo_w, qo_w, owh + 128
    if hw % 128:
        q_w, o_w, q_off = [p[:, owh + 128 :] for p in qo_w], [p[:, : owh + 128] for p in qo_w], 0
    nqo, nup, ndown = len(qo_w), len(up_w), len(down_w)
    up_w, down_w, q_back, o_back = (
        [pltpu.with_memory_space_constraint(piece, pltpu.HBM) for piece in pieces]
        for pieces in (up_w, down_w, q_w, o_w)
    )

    order = after(block_order, *middle(qo_z))[0].reshape(ny, nc)
    places = []
    for sy in range(ny):
        for sc in range(nc):
            places.append(take(take(order, back("y", sy)), back("c", sc)))
    places = jnp.stack(places)
    ranks = jnp.arange(spans, dtype=jnp.int32)
    sorted_at = jnp.sum(jnp.where(places[None, :] == ranks[:, None], ranks[None, :], 0), -1)
    offsets = jnp.arange(rows_here, dtype=jnp.int32)
    positions = (places[:, None] * rows_here + offsets[None, :]).reshape(length)
    lane = jnp.arange(lanes, dtype=jnp.int32)
    frequency = jnp.exp((lane % (HD // 2)).astype(F32) * (-2.0 * math.log(10000.0) / HD))
    angles = positions.astype(F32)[:, None] * frequency[None, :]
    cos_lanes = after(jnp.cos(angles))
    sin_lanes = jnp.sin(angles) * jnp.where(lane % HD < HD // 2, -1.0, 1.0)

    a1, qkv, norms = call(
        functools.partial(input_kernel, nqo, spans, lanes, q_off, owh),
        (shaped((length, width), BF16), shaped((length, 3 * hw), BF16), shaped((8, width), F32)),
        [IN_SMEM] + [IN_VMEM] * (2 + spans) + [ANYWHERE] * (2 * nqo),
        [pltpu.VMEM((width, 3 * hw), BF16), pltpu.VMEM((width, 128), BF16), sems(2 * nqo)],
    )(up_at, cos_lanes, sin_lanes, *tok_all, *q_w, *o_w)
    qkv_now = after(qkv, *middle(down_z))
    attn, lse = call(
        functools.partial(attend_kernel, spans, lanes),
        (shaped((length, hw), BF16), shaped((length, 128), F32)),
        [IN_SMEM, IN_VMEM],
    )(sorted_at, qkv_now)

    attn_now = after(attn, *(up_y[half : half + 1] + down_w[:ny]))
    sent = attn_now.reshape(ny, nc, rows_here, hw)
    o_near = [sent[0]] + [shift(sent[sy], "y", ny - sy) for sy in range(1, ny)]
    o_far = [shift(item, "c") for item in o_near]
    o_near[0] = after(o_near[0], *([down_z[half]] + up_w[: 2 * nx] + up_w[-nx:] + down_w[ny : 2 * ny]))
    r_keep, r_send, o_chip = call(
        functools.partial(out_kernel, nqo, ny),
        (shaped((rows_here, owh), F32), shaped((rows_here, owh), F32), shaped((crow, width), BF16)),
        [IN_SMEM, IN_SMEM] + [IN_VMEM] * (2 * ny) + [IN_SMEM] + [ANYWHERE] * nqo,
        [pltpu.VMEM((width, owh), BF16), sems(nqo)],
    )(up_at, core, *o_near, *o_far, span_y, *o_w)
    r_send = after(r_send, *(down_w[ny : 2 * ny] + down_w[-ny:] + up_w[half * nx : half * nx + nx]))
    r_got = shift(r_send, "c")
    h, a2 = call(
        middle_kernel,
        (shaped((rows_here, width), F32), shaped((rows_here, width), BF16)),
        [IN_SMEM] + [IN_VMEM] * 4,
        [pltpu.VMEM((rows_here, width), F32)],
    )(core, r_keep, r_got, tok, norms)
    a2 = after(a2)
    a2_got = shift(a2, "c")
    m_keep, m_send, u, slope = call(
        functools.partial(mlp_kernel, nup, ndown),
        (
            shaped((rows_here, width), F32),
            shaped((rows_here, width), BF16),
            shaped((crow, ffh), BF16),
            shaped((crow, ffh), BF16),
        ),
        [IN_SMEM, IN_SMEM, IN_VMEM, IN_VMEM] + [IN_HBM] * (nup + ndown),
        [pltpu.VMEM((width, ffh), BF16), pltpu.VMEM((ffh, width), BF16), sems(nup + ndown)],
        vmem=26,
    )(up_at, down_at, a2, a2_got, *up_w, *down_w)
    m_got = shift(m_send, "c")
    match = group_ids[:, None] == jnp.arange(group_weight.shape[0], dtype=jnp.int32)[None, :]
    scale = jnp.sum(jnp.where(match, group_weight[None, :], 0.0)).reshape(1)
    out_tokens, dm, grads_3 = call(
        top_kernel,
        (shaped((rows_here, width), BF16), shaped((rows_here, width), BF16), shaped((2, width), F32)),
        [IN_SMEM] + [IN_VMEM] * 5,
    )(scale, m_keep, m_got, h, cot, norms)

    dm_got = shift(dm, "c")
    down_own, down_got = [None] * nz, [None] * nz
    up_own, up_got = [None] * nz, [None] * nz
    early, late = late_last(nz)[:2], late_last(nz)[2:]

    def down_block(step, right, *when):
        blocks = grads(u, [right, dm_got], down_at, nx * ffrows, range(step * ny, step * ny + ny))
        down_own[step] = blocks[0]
        down_got[step] = [shift(after(blocks[far], *when), "y", ny - far) for far in range(1, ny)]

    def up_block(step, right):
        blocks = grads(a2_all, [right], up_at, dprows, range(step * nx, step * nx + nx))
        up_own[step] = blocks[0]
        up_got[step] = [shift(blocks[far], "x", nx - far) for far in range(1, nx)]

    right = dm
    for step in early:
        down_block(step, right, right)
        right = after(dm, down_own[step])
    blocks = [down_own[early[-1]]]
    dm = after(dm, blocks[0])
    da_keep, da_send, dz = call(
        functools.partial(mlp_back_kernel, nup, ndown),
        (
            shaped((rows_here, width), F32),
            shaped((rows_here, width), BF16),
            shaped((crow, ffh), BF16),
        ),
        [IN_SMEM, IN_SMEM, IN_VMEM, IN_VMEM, IN_VMEM] + [IN_HBM] * (nup + ndown),
        [pltpu.VMEM((width, ffh), BF16), pltpu.VMEM((ffh, width), BF16), sems(nup + ndown)],
        vmem=26,
    )(up_at, down_at, dm, dm_got, slope, *up_w, *down_w)
    da_got = shift(da_send, "c")
    a2_all = jnp.concatenate([a2, a2_got], 0)
    right = after(dz)
    for step in early + late:
        up_block(step, right)
        right = after(dz, up_own[step])
    blocks = [up_own[early[-1]]]
    da_keep = after(da_keep, blocks[0], *down_got[early[0]])
    dh, dr, dr_send, grads_21 = call(
        between_kernel,
        (
            shaped((rows_here, width), F32),
            shaped((rows_here, owh), BF16),
            shaped((rows_here, owh), BF16),
            shaped((4, width), F32),
        ),
        [IN_SMEM, IN_SMEM] + [IN_VMEM] * 7,
        [pltpu.VMEM((rows_here, width), F32), pltpu.VMEM((rows_here, width), BF16)],
    )(core, scale, da_keep, da_got, h, r_keep, r_got, cot, norms)
    dr_send = after(dr_send, *down_got[early[1]])
    dr_got = shift(dr_send, "c")
    do_keep, do_send = call(
        functools.partial(out_back_kernel, nqo, ny),
        (shaped((ny, crow, hw), F32), shaped((ny, crow, hw), BF16)),
        [IN_SMEM, IN_SMEM, IN_VMEM, IN_VMEM] + [ANYWHERE] * nqo,
        [pltpu.VMEM((width, owh), BF16), sems(nqo)],
    )(up_at, core, dr, dr_got, *o_back)
    do_got = shift(do_send, "c")
    do_got = jnp.concatenate([do_got[:, rows_here:], do_got[:, :rows_here]], 1)
    do = (do_keep + do_got.astype(F32)).astype(BF16)
    parts = []
    for sy in range(ny):
        item = take(do, lax.rem(iy + sy, ny))
        parts.append(item if sy == 0 else shift(item, "y", sy))
    do_all = jnp.concatenate(parts, 0)
    down_y, up_x = [None] * nz, [None] * nz
    right = after(dm, do)
    down_block(late[0], right, do_all)
    for step in late[1:]:
        down_block(step, after(dm, do), do_all)
    for step in early:
        down_y[step] = add_parts(down_own[step], down_got[step], do)
        up_x[step] = add_parts(up_own[step], up_got[step], do_all)
    out_own, out_send = stacked_grads(o_chip, [dr, dr_got], up_at, dprows)
    out_got = shift(out_send, "x")

    down_first = ring_first(down_y, "z")
    sums = [None] * nz
    for step in early:
        own_y, got_y = send_parts(up_x[step].reshape(ny, nc * wrows, ffh), "y")
        sums[step] = add_parts(own_y, got_y, do_all)
    up_first = ring_first(sums, "z")
    do_all = after(do_all, *[t for t in down_y + up_x + down_own + up_own if t is not None])
    dqkv = call(
        functools.partial(attend_back_kernel, spans, lanes),
        shaped((length, 3 * hw), BF16),
        [IN_SMEM] + [IN_VMEM] * 6,
        [pltpu.VMEM((length, lanes), F32)] * 2
        + [pltpu.VMEM((length, 128), F32), pltpu.VMEM((2, 8, length), F32)],
        vmem=20,
    )(sorted_at, qkv, attn, do_all, lse, cos_lanes, sin_lanes)
    dqkv = after(dqkv, *([t for step in late for t in up_got[step]] + [sums[step] for step in early]))
    qkv_own, qkv_send = stacked_grads(a1, [dqkv], up_at, dprows)
    qkv_got = shift(qkv_send, "x")
    da1_keep, da1_send = call(
        functools.partial(input_back_kernel, nqo, q_off),
        (shaped((ny, rows_here, width), F32), shaped((ny, rows_here, width), BF16)),
        [IN_SMEM, IN_VMEM] + [ANYWHERE] * nqo,
        [pltpu.VMEM((width, 3 * hw), BF16), sems(nqo)],
    )(up_at, after(dqkv, qkv_own, *down_first), *q_back)
    da1_got = shift(da1_send, "c")
    sent_on = [(da1_keep[sy] + da1_got[sy].astype(F32)).astype(BF16) for sy in range(1, ny)]
    arrived = [shift(item, "y", ny - sy) for sy, item in enumerate(sent_on, 1)]
    da1_keep = after(da1_keep, *(up_first + down_first + [t for step in late for t in down_got[step]]))
    grad_tokens, grads_0 = call(
        bottom_kernel,
        (shaped((rows_here, width), BF16), shaped((2, width), F32)),
        [IN_VMEM] * (5 + len(arrived)),
    )(tok, dh, norms, da1_keep[0], da1_got[0], *arrived)
    grad_tokens = grad_tokens.reshape(tokens.shape)
    out_tokens = out_tokens.reshape(tokens.shape)

    for step in range(nz):
        if down_y[step] is None:
            down_y[step] = add_parts(down_own[step], down_got[step], sent_on[0])
    down = ring_rest(down_y, down_first, "z").astype(BF16)
    down = scatter_sum(down.reshape(nx, ffrows, width), "x")
    for step in late:
        part = add_parts(up_own[step], up_got[step], qkv_own)
        own_y, got_y = send_parts(part.reshape(ny, nc * wrows, ffh), "y")
        sums[step] = add_parts(own_y, got_y, arrived[0])
    up = ring_rest(sums, up_first, "z").reshape(nc, wrows, ffh)
    up_got = shift(take(up, 1 - ic), "c")
    if aligned:
        up = call(
            functools.partial(up_kernel, (nz, nx, ny, ffrows)),
            shaped((wrows, ff), F32),
            [IN_SMEM] + [IN_VMEM] * 2,
        )(core, take(up, ic), up_got)
    else:
        up = pair(take(up, ic), up_got, ic)
        up = up.reshape(nc, wrows, nz, ny, nx, ffrows).transpose(1, 2, 4, 3, 0, 5).reshape(wrows, ff)

    out_x = add_parts(out_own, [out_got], qkv_got)
    qkv_x = (qkv_own.astype(F32) + qkv_got.astype(F32)).astype(BF16)
    both = jnp.concatenate([out_x, qkv_x], -1)
    both = ring_scatter([both[step] for step in range(nz)], "z").astype(BF16)
    out, qkv_g = both[:, :owh], both[:, owh:]
    out = scatter_sum(out.reshape(ny, nc * wrows, owh), "y").reshape(nc, wrows, owh)
    out_got = shift(take(out, 1 - ic), "c")
    qkv_g = exchange(qkv_g.reshape(ny, nc * wrows, 3 * hw), "y")
    qkv_g = qkv_g.reshape(ny, nc, wrows, 3 * hw)
    qkv_got = shift(take(qkv_g, 1 - ic, 1), "c")
    if aligned:
        qkv_g, out = call(
            qkv_out_kernel,
            (shaped((wrows, 3 * width), F32), shaped((wrows, width), F32)),
            [IN_SMEM] + [IN_VMEM] * 4,
        )(core, take(qkv_g, ic, 1), qkv_got, take(out, ic), out_got)
    else:
        out = pair(take(out, ic), out_got, ic).transpose(1, 0, 2).reshape(wrows, width)
        qkv_g = pair(take(qkv_g, ic, 1), qkv_got, ic)
        qkv_g = qkv_g.reshape(nc, ny, wrows, 3, hw).transpose(2, 3, 1, 0, 4)
        qkv_g = qkv_g.reshape(wrows, 3 * width).astype(F32)

    norm_sums = jnp.concatenate(
        [
            grads_0[0:1],
            grads_21[2:3],
            grads_21[0:1],
            grads_3[0:1],
            grads_0[1:2],
            grads_21[3:4],
            grads_21[1:2],
            grads_3[1:2],
        ],
        0,
    )
    norm_sums = after(norm_sums)
    for axis in "cyxz":
        norm_sums = all_sum(norm_sums, axis)
    place = ((iz * nx + ix) * ny + iy) * nc + ic
    norm_sums = lax.dynamic_slice(norm_sums, (0, place * wrows), (8, wrows))
    return (out_tokens, grad_tokens, qkv_g, out, up, down, norm_sums[:4], norm_sums[4:])


def solution(mesh):
    fine = Mesh(
        mesh.devices.reshape(mesh.shape["dp"] // 2, 2, mesh.shape["blk"] // 2, 2),
        ("z", "x", "y", "c"),
    )
    dp, blk, every = ("z", "x"), ("y", "c"), ("z", "x", "y", "c")
    return jax.shard_map(
        on_device,
        mesh=fine,
        in_specs=(
            P(blk, dp, None),
            P(blk, dp, None),
            P(dp),
            P(),
            P(dp, None),
            P(every, None),
            P(every, None),
            P(every, None),
            P(every, None),
            P(None, every),
            P(None, every),
        ),
        out_specs=(
            P(blk, dp, None),
            P(blk, dp, None),
            P(every, None),
            P(every, None),
            P(every, None),
            P(every, None),
            P(None, every),
            P(None, every),
        ),
        check_vma=False,
    )
```

```python
import functools
import math

import jax
import jax.numpy as jnp
from jax import lax
from jax.experimental import pallas as pl
from jax.experimental.pallas import tpu as pltpu
from jax.sharding import Mesh
from jax.sharding import PartitionSpec as P

HD = 64
F32 = jnp.float32
BF16 = jnp.bfloat16


def shift(value, axis, step=1):
    size = lax.axis_size(axis)
    return lax.ppermute(value, axis, [(i, (i + step) % size) for i in range(size)])


def after(value, *others):
    return lax.optimization_barrier((value,) + others)[0]


def back(axis, step):
    size = lax.axis_size(axis)
    return lax.rem(lax.axis_index(axis) + size - step, size)


def take(array, at, axis=0):
    return lax.dynamic_index_in_dim(array, at, axis, keepdims=False)


def direct_gather(piece, axis):
    size = lax.axis_size(axis)
    return [piece] + [shift(piece, axis, step) for step in range(1, size)]


def ring_gather(piece, axis, gate=()):
    size = lax.axis_size(axis)
    pieces = [piece] * size
    for step in range(1, size // 2 + 1):
        last = pieces[step - 1]
        pieces[step] = shift(after(last, *gate) if gate and step > 1 else last, axis)
    for step in range(size - 1, size // 2, -1):
        last = pieces[(step + 1) % size]
        pieces[step] = shift(after(last, *gate) if gate and step < size - 1 else last, axis, -1)
    return pieces


def in_order(pieces, axis):
    if len(pieces) == 2:
        return pair(pieces[0], pieces[1], lax.axis_index(axis))
    buffer = jnp.zeros((len(pieces),) + pieces[0].shape, pieces[0].dtype)
    for step, piece in enumerate(pieces):
        at = (back(axis, step),) + (0,) * piece.ndim
        buffer = lax.dynamic_update_slice(buffer, piece[None], at)
    return buffer


def pair(own, other, index):
    first = jnp.where(index == 0, own, other)
    second = jnp.where(index == 0, other, own)
    return jnp.stack([first, second])


def ring_first(parts, axis):
    size = len(parts)
    half = size // 2
    found = [shift(parts[half].astype(BF16), axis)]
    if size - 1 - half:
        found.append(shift(parts[size - 1 - half].astype(BF16), axis, -1))
    return found


def ring_rest(parts, arrived, axis):
    size = len(parts)
    half = size // 2
    total = parts[0].astype(F32)
    for carry, count, way in zip(arrived, (half, size - 1 - half), (1, -1)):
        for far in range(count - 1, 0, -1):
            part = parts[size - far if way == 1 else far]
            carry = shift((carry.astype(F32) + part.astype(F32)).astype(BF16), axis, way)
        total = total + carry.astype(F32)
    return total


def ring_scatter(parts, axis):
    return ring_rest(parts, ring_first(parts, axis), axis)


def scatter_sum(parts, axis):
    size = parts.shape[0]
    return ring_scatter([take(parts, back(axis, step)) for step in range(size)], axis)


def late_last(size):
    half = size // 2
    steps = list(range(half, 0, -1)) + list(range(half + 1, size)) + [0]
    return list(dict.fromkeys(steps))


def send_parts(parts, axis):
    size = parts.shape[0]
    got = [shift(take(parts, back(axis, step)), axis, size - step) for step in range(1, size)]
    return take(parts, lax.axis_index(axis)), got


def add_parts(own, got, when):
    total = own.astype(F32)
    for item in got:
        total = total + after(item, when).astype(F32)
    return total.astype(BF16)


def exchange(parts, axis):
    size = parts.shape[0]
    index = lax.axis_index(axis)
    pieces = [take(parts, index)]
    for step in range(1, size):
        pieces.append(shift(take(parts, lax.rem(index + step, size)), axis, step))
    return in_order(pieces, axis)


def all_sum(value, axis):
    pieces = direct_gather(value, axis)
    total = pieces[0]
    for piece in pieces[1:]:
        total = total + piece
    return total


IN_VMEM = pl.BlockSpec(memory_space=pltpu.VMEM)
IN_SMEM = pl.BlockSpec(memory_space=pltpu.SMEM)
ANYWHERE = pl.BlockSpec(memory_space=pl.ANY)
IN_HBM = pl.BlockSpec(memory_space=pltpu.HBM)


def call(kernel, out_shape, in_specs, scratch=(), vmem=16):
    several = isinstance(out_shape, (tuple, list))
    return pl.pallas_call(
        kernel,
        out_shape=out_shape,
        in_specs=in_specs,
        out_specs=[IN_VMEM] * len(out_shape) if several else IN_VMEM,
        scratch_shapes=list(scratch),
        compiler_params=pltpu.CompilerParams(vmem_limit_bytes=vmem * 1024 * 1024),
        cost_estimate=pl.CostEstimate(flops=1024, bytes_accessed=1024, transcendentals=0),
    )


def fetch(pieces, at_ref, target, sems, first, offset=0, columns=None):
    copies = []
    for number, piece in enumerate(pieces):
        rows = piece.shape[0]
        source = piece if columns is None else piece.at[:, pl.ds(offset, columns)]
        place = pl.ds(pl.multiple_of(at_ref[number] * rows, rows), rows)
        copies.append(pltpu.make_async_copy(source, target.at[place], sems.at[first + number]))
    for copy in copies:
        copy.start()
    return copies


def wait_all(copies):
    for copy in copies:
        copy.wait()


def partner(values):
    half = HD // 2
    if values.shape[-1] == HD:
        return jnp.concatenate([values[:, half:], values[:, :half]], -1)
    lanes = values.shape[-1]
    lane = lax.broadcasted_iota(jnp.int32, values.shape, 1)
    low = lax.rem(lane, HD) < half
    return jnp.where(low, pltpu.roll(values, lanes - half, 1), pltpu.roll(values, half, 1))


def attend_kernel(blocks, lanes, order_ref, qkv_ref, o_ref, lse_ref):
    length, third = o_ref.shape
    size = length // blocks
    per = lanes // HD
    lane = lax.broadcasted_iota(jnp.int32, (1, lanes), 1) // HD
    row = lax.broadcasted_iota(jnp.int32, (size, size), 0)
    col = lax.broadcasted_iota(jnp.int32, (size, size), 1)
    for group in range(third // lanes):
        left = group * lanes

        def one_row(i):
            at = pl.multiple_of(order_ref[i] * size, size)
            q = qkv_ref[pl.ds(at, size), left : left + lanes]
            outs, totals = [], []
            for head in range(per):
                qh = q * (lane == head).astype(BF16)

                def scores(start):
                    k = qkv_ref[pl.ds(start, size), third + left : third + left + lanes]
                    return lax.dot_general(qh, k, (((1,), (1,)), ((), ())), preferred_element_type=F32)

                def values(p, start):
                    v = qkv_ref[pl.ds(start, size), 2 * third + left : 2 * third + left + lanes]
                    return jnp.dot(p.astype(BF16), v, preferred_element_type=F32)

                s = jnp.where(col <= row, scores(at), -1e30)
                top = jnp.max(s, -1, keepdims=True)
                p = jnp.exp(s - top)
                state = (top, jnp.sum(p, -1, keepdims=True), values(p, at))

                def step(j, state):
                    top, total, acc = state
                    start = pl.multiple_of(order_ref[j] * size, size)
                    s = scores(start)
                    new = jnp.maximum(top, jnp.max(s, -1, keepdims=True))
                    factor = jnp.exp(top - new)
                    p = jnp.exp(s - new)
                    total = total * factor + jnp.sum(p, -1, keepdims=True)
                    return new, total, acc * factor + values(p, start)

                if blocks <= 4:
                    for j in range(i):
                        state = step(j, state)
                else:
                    state = lax.fori_loop(0, i, step, state)
                top, total, acc = state
                outs.append(acc / total)
                column = group * per + head
                lse_ref[pl.ds(at, size), column : column + 1] = top + jnp.log(total)
            out = outs[0]
            for head in range(1, per):
                out = jnp.where(lane == head, outs[head], out)
            o_ref[pl.ds(at, size), left : left + lanes] = out.astype(BF16)

        if blocks <= 4:
            for i in range(blocks):
                one_row(i)
        else:
            pl.loop(0, blocks)(one_row)


def attend_back_kernel(
    blocks, lanes, order_ref, qkv_ref, o_ref, do_ref, lse_ref, cos_ref, sin_ref, out_ref,
    dk_ref, dv_ref, delta_ref, rows_ref,
):
    length, third = o_ref.shape
    size = length // blocks
    per = lanes // HD
    lane = lax.broadcasted_iota(jnp.int32, (1, lanes), 1) // HD
    row = lax.broadcasted_iota(jnp.int32, (size, size), 0)
    col = lax.broadcasted_iota(jnp.int32, (size, size), 1)
    nt = (((1,), (1,)), ((), ()))
    tn = (((0,), (0,)), ((), ()))

    def unturn(values, rows):
        return values * cos_ref[rows, :] - partner(values) * sin_ref[rows, :]

    delta_ref[...] = jnp.zeros_like(delta_ref)
    for start in range(0, length, size):
        rows = pl.ds(start, size)
        for left in range(0, third, lanes):
            prod = do_ref[rows, left : left + lanes].astype(F32) * o_ref[rows, left : left + lanes].astype(F32)
            for head in range(per):
                column = left // HD + head
                total = jnp.sum(jnp.where(lane == head, prod, 0.0), -1, keepdims=True)
                delta_ref[rows, column : column + 1] = total
    rows_ref[0] = jnp.transpose(lse_ref[...])[: rows_ref.shape[1], :]
    rows_ref[1] = jnp.transpose(delta_ref[...])[: rows_ref.shape[1], :]

    for group in range(third // lanes):
        left = group * lanes
        dk_ref[...] = jnp.zeros_like(dk_ref)
        dv_ref[...] = jnp.zeros_like(dv_ref)

        def one_row(i):
            at = pl.multiple_of(order_ref[i] * size, size)
            rows = pl.ds(at, size)
            q = qkv_ref[rows, left : left + lanes]
            do = do_ref[rows, left : left + lanes]
            grads = []
            for head in range(per):
                own = (lane == head).astype(BF16)
                qh, doh = q * own, do * own
                number = group * per + head
                lse = rows_ref[0, number : number + 1, rows]
                delta = rows_ref[1, number : number + 1, rows]

                def step(start, diagonal):
                    where = pl.ds(start, size)
                    k = qkv_ref[where, third + left : third + left + lanes]
                    v = qkv_ref[where, 2 * third + left : 2 * third + left + lanes]
                    s = lax.dot_general(k, qh, nt, preferred_element_type=F32)
                    p = jnp.exp(s - lse)
                    if diagonal:
                        p = jnp.where(row <= col, p, 0.0)
                    dp = lax.dot_general(v, doh, nt, preferred_element_type=F32)
                    ds = (p * (dp - delta)).astype(BF16)
                    dv_ref[where, :] += jnp.dot(p.astype(BF16), doh, preferred_element_type=F32)
                    dk_ref[where, :] += jnp.dot(ds, qh, preferred_element_type=F32)
                    return lax.dot_general(ds, k, tn, preferred_element_type=F32)

                dq = step(at, True)
                if blocks <= 4:
                    for j in range(i):
                        dq = dq + step(pl.multiple_of(order_ref[j] * size, size), False)
                else:
                    dq = lax.fori_loop(
                        0, i, lambda j, c: c + step(pl.multiple_of(order_ref[j] * size, size), False), dq
                    )
                grads.append(dq)
            dq = grads[0]
            for head in range(1, per):
                dq = jnp.where(lane == head, grads[head], dq)
            out_ref[rows, left : left + lanes] = unturn(dq * 0.125, rows).astype(BF16)

        if blocks <= 4:
            for i in range(blocks):
                one_row(i)
        else:
            pl.loop(0, blocks)(one_row)
        for start in range(0, length, size):
            rows = pl.ds(start, size)
            out_ref[rows, third + left : third + left + lanes] = unturn(dk_ref[rows, :], rows).astype(BF16)
            out_ref[rows, 2 * third + left : 2 * third + left + lanes] = dv_ref[rows, :].astype(BF16)


GELU_A = math.sqrt(2.0 / math.pi)
GELU_B = 0.044715


NT = (((1,), (1,)), ((), ()))
TN = (((0,), (0,)), ((), ()))


def normed(values):
    centred = values - jnp.mean(values, -1, keepdims=True)
    scale = lax.rsqrt(jnp.mean(centred * centred, -1, keepdims=True) + 1e-05)
    return centred * scale, scale


def normed_back(grad, gain, vhat, scale):
    scaled = grad * gain
    return scale * (
        scaled - jnp.mean(scaled, -1, keepdims=True) - vhat * jnp.mean(scaled * vhat, -1, keepdims=True)
    )


def column_sum(values):
    return jnp.sum(values, 0, keepdims=True)


def halves(core_ref, width):
    own = pl.ds(pl.multiple_of(core_ref[0] * width, width), width)
    other = pl.ds(pl.multiple_of((1 - core_ref[0]) * width, width), width)
    return own, other


def cut_kernel(sizes, core_ref, qkv_in, out_in, up_in, norm_ref, keep_ref, send_ref, qkv_ref, out_ref, up_ref, sems):
    nz, nx, ny, hw, ffrows = sizes
    width, owh = out_ref.shape[1], out_ref.shape[1] // 2
    pairs = ((qkv_in, qkv_ref), (out_in, out_ref), (up_in, up_ref))
    copies = [pltpu.make_async_copy(a, b, sems.at[n]) for n, (a, b) in enumerate(pairs)]
    for copy in copies:
        copy.start()
    wait_all(copies)
    for target, core in ((keep_ref, core_ref[0]), (send_ref, 1 - core_ref[0])):
        at = 0
        for y in range(ny):
            for part in range(3):
                left = pl.multiple_of(part * width + (y * 2 + core) * hw, hw)
                target[:, at : at + hw] = qkv_ref[:, pl.ds(left, hw)]
                at += hw
        target[:, at : at + owh] = out_ref[:, pl.ds(pl.multiple_of(core * owh, owh), owh)]
        at += owh
        target[:, at : at + 128] = norm_ref[...]
        at += 128
        for z in range(nz):
            for y in range(ny):
                for x in range(nx):
                    left = pl.multiple_of((((z * nx + x) * ny + y) * 2 + core) * ffrows, ffrows)
                    target[:, at : at + ffrows] = up_ref[:, pl.ds(left, ffrows)]
                    at += ffrows


def up_kernel(sizes, core_ref, own_ref, got_ref, up_ref):
    nz, nx, ny, ffrows = sizes
    for source, core in ((own_ref, core_ref[0]), (got_ref, 1 - core_ref[0])):
        at = 0
        for z in range(nz):
            for y in range(ny):
                for x in range(nx):
                    left = pl.multiple_of((((z * nx + x) * ny + y) * 2 + core) * ffrows, ffrows)
                    up_ref[:, pl.ds(left, ffrows)] = source[:, at : at + ffrows]
                    at += ffrows


def qkv_out_kernel(core_ref, own_ref, got_ref, out_own_ref, out_got_ref, qkv_ref, out_ref):
    ny, hw = own_ref.shape[0], own_ref.shape[2] // 3
    width, owh = out_ref.shape[1], out_own_ref.shape[1]
    own, other = halves(core_ref, owh)
    out_ref[:, own] = out_own_ref[...]
    out_ref[:, other] = out_got_ref[...]
    for source, core in ((own_ref, core_ref[0]), (got_ref, 1 - core_ref[0])):
        for y in range(ny):
            for part in range(3):
                left = pl.multiple_of(part * width + (y * 2 + core) * hw, hw)
                qkv_ref[:, pl.ds(left, hw)] = source[y, :, part * hw : part * hw + hw].astype(F32)


def input_kernel(count, blocks, lanes, q_off, n_off, at_ref, cos_ref, sin_ref, *refs):
    toks, refs = refs[:blocks], refs[blocks:]
    q_pieces, n_pieces, refs = refs[:count], refs[count : 2 * count], refs[2 * count :]
    a_ref, out_ref, norm_ref, weight, columns, sems = refs
    wide = out_ref.shape[1]
    first = fetch(n_pieces, at_ref, columns, sems, 0, n_off, 128)
    later = fetch(q_pieces, at_ref, weight, sems, count, q_off, wide)
    wait_all(first)
    norm_ref[...] = jnp.transpose(columns[...].astype(F32))[:8, :]
    gain, bias = norm_ref[0:1, :], norm_ref[4:5, :]
    rows_here = toks[0].shape[0]
    for number, tok_ref in enumerate(toks):
        vhat, _ = normed(tok_ref[...].astype(F32))
        a_ref[pl.ds(number * rows_here, rows_here), :] = (vhat * gain + bias).astype(BF16)
    wait_all(later)
    third = wide // 3
    block = 256
    for start in range(0, out_ref.shape[0], block):
        rows = pl.ds(start, block)
        acc = jnp.dot(a_ref[rows, :], weight[...], preferred_element_type=F32)
        cos, sin = cos_ref[rows, :], sin_ref[rows, :]
        for part in range(3):
            for left in range(0, third, lanes):
                at = part * third + left
                values = acc[:, at : at + lanes]
                if part < 2:
                    values = values * cos + partner(values) * sin
                if part == 0:
                    values = values * 0.125
                out_ref[rows, at : at + lanes] = values.astype(BF16)


def out_kernel(count, ny, at_ref, core_ref, *refs):
    near, far, refs = refs[:ny], refs[ny : 2 * ny], refs[2 * ny :]
    y_ref, pieces, refs = refs[0], refs[1 : 1 + count], refs[1 + count :]
    keep_ref, send_ref, chip_ref, weight, sems = refs
    copies = fetch(pieces, at_ref, weight, sems, 0, 0, weight.shape[1])
    core = core_ref[0]
    rows, hw = near[0].shape[1], near[0].shape[2]
    for parts, is_far in ((near, False), (far, True)):
        other = 1 - core if is_far else core
        for ahead in range(ny):
            yh = lax.rem(y_ref[0] + ahead, ny)
            for sc in range(2):
                token = pl.ds(((1 - sc) if is_far else sc) * rows, rows)
                value = parts[ahead][sc]
                if hw % 128 == 0:
                    left = pl.multiple_of((yh * 2 + other) * hw, hw)
                    chip_ref[token, pl.ds(left, hw)] = value
                else:
                    for place in range(2 * ny):

                        @pl.when(yh * 2 + other == place)
                        def _(place=place, value=value, token=token):
                            chip_ref[token, place * hw : place * hw + hw] = value

    wait_all(copies)
    send_ref[...] = jnp.dot(chip_ref[rows:, :], weight[...], preferred_element_type=F32)
    keep_ref[...] = jnp.dot(chip_ref[:rows, :], weight[...], preferred_element_type=F32)


def middle_kernel(core_ref, keep_ref, got_ref, tok_ref, norm_ref, h_ref, a_ref, r_ref):
    own, other = halves(core_ref, keep_ref.shape[1])
    r_ref[:, own] = keep_ref[...]
    r_ref[:, other] = got_ref[...]
    vhat, _ = normed(r_ref[...])
    h = tok_ref[...].astype(F32) + vhat * norm_ref[1:2, :] + norm_ref[5:6, :]
    h_ref[...] = h
    vhat, _ = normed(h)
    a_ref[...] = (vhat * norm_ref[2:3, :] + norm_ref[6:7, :]).astype(BF16)


def mlp_kernel(ups, downs, up_at, down_at, own_ref, got_ref, *refs):
    up_pieces, down_pieces = refs[:ups], refs[ups : ups + downs]
    keep_ref, send_ref, u_ref, slope_ref, up, down, sems = refs[ups + downs :]
    copies = fetch(up_pieces, up_at, up, sems, 0)
    later = fetch(down_pieces, down_at, down, sems, ups)
    wait_all(copies)
    count, wide = own_ref.shape[0], u_ref.shape[1]
    step = min(512, wide)
    for start, a_ref in ((count, got_ref), (0, own_ref)):
        rows = pl.ds(start, count)
        for left in range(0, wide, step):
            z = jnp.dot(a_ref[...], up[:, left : left + step], preferred_element_type=F32)
            square = z * z
            t = jnp.tanh(GELU_A * z * (1.0 + GELU_B * square))
            half = 0.5 * (1.0 + t)
            u_ref[rows, left : left + step] = (z * half).astype(BF16)
            slope = half + 0.5 * z * (1.0 - t * t) * (GELU_A * (1.0 + 3.0 * GELU_B * square))
            slope_ref[rows, left : left + step] = slope.astype(BF16)
    wait_all(later)
    send_ref[...] = jnp.dot(u_ref[count:, :], down[...], preferred_element_type=F32).astype(BF16)
    keep_ref[...] = jnp.dot(u_ref[:count, :], down[...], preferred_element_type=F32)


def top_kernel(scale_ref, keep_ref, got_ref, h_ref, cot_ref, norm_ref, out_ref, dm_ref, grad_ref):
    vhat, scale = normed(keep_ref[...] + got_ref[...].astype(F32))
    gain = norm_ref[3:4, :]
    out_ref[...] = (h_ref[...] + vhat * gain + norm_ref[7:8, :]).astype(BF16)
    g = cot_ref[...].astype(F32) * scale_ref[0]
    dm_ref[...] = normed_back(g, gain, vhat, scale).astype(BF16)
    grad_ref[0:1, :] = column_sum(g * vhat)
    grad_ref[1:2, :] = column_sum(g)


def mlp_back_kernel(ups, downs, up_at, down_at, own_ref, got_ref, slope_ref, *refs):
    up_pieces, down_pieces = refs[:ups], refs[ups : ups + downs]
    keep_ref, send_ref, dz_ref, up, down, sems = refs[ups + downs :]
    copies = fetch(down_pieces, down_at, down, sems, ups)
    later = fetch(up_pieces, up_at, up, sems, 0)
    wait_all(copies)
    count, wide = own_ref.shape[0], dz_ref.shape[1]
    step = min(512, wide)
    for start, dm_ref in ((count, got_ref), (0, own_ref)):
        rows = pl.ds(start, count)
        for left in range(0, wide, step):
            du = lax.dot_general(dm_ref[...], down[left : left + step, :], NT, preferred_element_type=F32)
            slope = slope_ref[rows, left : left + step].astype(F32)
            dz_ref[rows, left : left + step] = (du * slope).astype(BF16)
    wait_all(later)
    send = lax.dot_general(dz_ref[count:, :], up[...], NT, preferred_element_type=F32)
    send_ref[...] = send.astype(BF16)
    keep_ref[...] = lax.dot_general(dz_ref[:count, :], up[...], NT, preferred_element_type=F32)


def between_kernel(
    core_ref, scale_ref, da_ref, da_got_ref, h_ref, keep_ref, got_ref, cot_ref, norm_ref,
    dh_ref, own_ref, send_ref, grad_ref, r_ref, dr_ref,
):
    own, other = halves(core_ref, keep_ref.shape[1])
    r_ref[:, own] = keep_ref[...]
    r_ref[:, other] = got_ref[...]
    e = da_ref[...] + da_got_ref[...].astype(F32)
    vhat, scale = normed(h_ref[...])
    grad_ref[0:1, :] = column_sum(e * vhat)
    grad_ref[1:2, :] = column_sum(e)
    g = cot_ref[...].astype(F32) * scale_ref[0]
    dh = g + normed_back(e, norm_ref[2:3, :], vhat, scale)
    dh_ref[...] = dh
    vhat, scale = normed(r_ref[...])
    grad_ref[2:3, :] = column_sum(dh * vhat)
    grad_ref[3:4, :] = column_sum(dh)
    dr_ref[...] = normed_back(dh, norm_ref[1:2, :], vhat, scale).astype(BF16)
    own_ref[...] = dr_ref[:, own]
    send_ref[...] = dr_ref[:, other]


def out_back_kernel(count, ny, at_ref, core_ref, own_ref, got_ref, *refs):
    pieces = refs[:count]
    keep_ref, send_ref, weight, sems = refs[count:]
    wait_all(fetch(pieces, at_ref, weight, sems, 0, 0, weight.shape[1]))
    core = core_ref[0]
    hw = keep_ref.shape[2]
    size = own_ref.shape[0]
    for own in (False, True):
        head = core if own else 1 - core
        for yh in range(ny):
            rows = pl.ds(pl.multiple_of((yh * 2 + head) * hw, hw), hw)
            for start, dr_ref in ((0, own_ref), (size, got_ref)):
                value = lax.dot_general(dr_ref[...], weight[rows, :], NT, preferred_element_type=F32)
                if own:
                    keep_ref[yh, pl.ds(start, size), :] = value
                else:
                    send_ref[yh, pl.ds(start, size), :] = value.astype(BF16)


def input_back_kernel(count, offset, at_ref, a_ref, *refs):
    pieces = refs[:count]
    keep_ref, send_ref, weight, sems = refs[count:]
    wait_all(fetch(pieces, at_ref, weight, sems, 0, offset, weight.shape[1]))
    block = keep_ref.shape[1]
    for number in range(a_ref.shape[0] // block):
        rows = pl.ds(number * block, block)
        value = lax.dot_general(a_ref[rows, :], weight[...], NT, preferred_element_type=F32)
        if number % 2 == 0:
            keep_ref[number // 2] = value
        else:
            send_ref[number // 2] = value.astype(BF16)


def bottom_kernel(*refs):
    tok_ref, dh_ref, norm_ref = refs[:3]
    pieces, (out_ref, grad_ref) = refs[3:-2], refs[-2:]
    e = pieces[0][...].astype(F32)
    for piece in pieces[1:]:
        e = e + piece[...].astype(F32)
    vhat, scale = normed(tok_ref[...].astype(F32))
    out_ref[...] = (dh_ref[...] + normed_back(e, norm_ref[0:1, :], vhat, scale)).astype(BF16)
    grad_ref[0:1, :] = column_sum(e * vhat)
    grad_ref[1:2, :] = column_sum(e)


def stacked_kernel(parts, cols, at_ref, left_ref, *refs):
    rights, (own_ref, send_ref) = refs[:parts], refs[parts:]
    size = rights[0].shape[0]
    for number in range(2 * own_ref.shape[0]):
        columns = pl.ds(pl.multiple_of(at_ref[number] * cols, cols), cols)
        total = None
        for place, right in enumerate(rights):
            left = left_ref[place * size : place * size + size, columns]
            value = lax.dot_general(left, right[...], TN, preferred_element_type=F32)
            total = value if total is None else total + value
        target = send_ref if number % 2 else own_ref
        target[number // 2] = total.astype(BF16)


def stacked_grads(left, rights, at, cols):
    wide, count = rights[0].shape[1], left.shape[1] // cols // 2
    if cols % 128:
        blocks = grads(left, rights, at, cols, range(2 * count))
        return jnp.stack(blocks[0::2]), jnp.stack(blocks[1::2])
    return call(
        functools.partial(stacked_kernel, len(rights), cols),
        [jax.ShapeDtypeStruct((count, cols, wide), BF16)] * 2,
        [IN_SMEM] + [IN_VMEM] * (1 + len(rights)),
    )(at, left, *rights)


def blocks_kernel(parts, cols, numbers, at_ref, left_ref, *refs):
    rights, outs = refs[:parts], refs[parts:]
    size = rights[0].shape[0]
    for number, out_ref in zip(numbers, outs):
        columns = pl.ds(pl.multiple_of(at_ref[number] * cols, cols), cols)
        total = None
        for place, right in enumerate(rights):
            left = left_ref[place * size : place * size + size, columns]
            value = lax.dot_general(left, right[...], TN, preferred_element_type=F32)
            total = value if total is None else total + value
        out_ref[...] = total.astype(BF16)


def grads(left, rights, at, cols, numbers):
    if cols % 128 == 0:
        return call(
            functools.partial(blocks_kernel, len(rights), cols, tuple(numbers)),
            [jax.ShapeDtypeStruct((cols, rights[0].shape[1]), BF16)] * len(numbers),
            [IN_SMEM] + [IN_VMEM] * (1 + len(rights)),
        )(at, left, *rights)
    right = jnp.concatenate(rights, 0)
    found = []
    for number in numbers:
        block = lax.dynamic_slice(left, (0, at[number] * cols), (left.shape[0], cols))
        found.append(lax.dot_general(block, right, TN, preferred_element_type=F32).astype(BF16))
    return found


def on_device(
    tokens,
    cotangent,
    group_ids,
    group_weight,
    block_order,
    w_qkv,
    w_out,
    w_up,
    w_down,
    norm_gain,
    norm_bias,
):
    nz, nx, ny, nc = (lax.axis_size(a) for a in "zxyc")
    iz, ix, iy, ic = (lax.axis_index(a) for a in "zxyc")
    rows_here, _, width = tokens.shape
    heads = width // HD
    spans = ny * nc
    mine = heads // spans
    hw = mine * HD
    lanes = min(128, hw)
    wrows = w_qkv.shape[0]
    ffrows = w_down.shape[0]
    ff = w_up.shape[1]
    ffh = ff // nc
    owh = width // nc
    dprows = spans * wrows
    length = spans * rows_here
    crow = nc * rows_here
    half = nz // 2
    shaped = jax.ShapeDtypeStruct

    def middle(pieces):
        return pieces[1:2] + pieces[-1:]

    def sems(count):
        return pltpu.SemaphoreType.DMA((count,))

    tok = tokens.reshape(rows_here, width)
    cot = cotangent.reshape(rows_here, width)
    norm_rows = jnp.concatenate([norm_gain, norm_bias], 0).T
    norm_rows = jnp.pad(norm_rows, ((0, 0), (0, 120)))
    core = ic.astype(jnp.int32).reshape(1)
    aligned = hw % 128 == 0 and ffrows % 128 == 0
    if aligned:
        keep, send = call(
            functools.partial(cut_kernel, (nz, nx, ny, hw, ffrows)),
            [shaped((wrows, ny * 3 * hw + owh + 128 + ffh), BF16)] * 2,
            [IN_SMEM] + [ANYWHERE] * 3 + [IN_VMEM],
            [pltpu.VMEM(item.shape, BF16) for item in (w_qkv, w_out, w_up)] + [sems(3)],
        )(core, *(pltpu.with_memory_space_constraint(w, pltpu.HBM) for w in (w_qkv, w_out, w_up)), norm_rows)
    else:
        norm_rows = jnp.broadcast_to(norm_rows[None], (nc, wrows, 128))
        cut = jnp.concatenate(
            [
                w_qkv.reshape(wrows, 3, ny, nc, hw).transpose(3, 0, 2, 1, 4).reshape(nc, wrows, -1),
                w_out.reshape(wrows, nc, owh).transpose(1, 0, 2),
                norm_rows,
                w_up.reshape(wrows, nz, nx, ny, nc, ffrows)
                .transpose(4, 0, 1, 3, 2, 5)
                .reshape(nc, wrows, ffh),
            ],
            -1,
        )
        keep, send = take(cut, ic), take(cut, 1 - ic)
    cut = pair(keep, shift(send, "c"), ic).reshape(nc * wrows, -1)
    q_cut = cut[:, : ny * 3 * hw].reshape(nc * wrows, ny, 3 * hw)
    left = ny * 3 * hw
    o_cut = jnp.broadcast_to(cut[:, None, left : left + owh + 128], (nc * wrows, ny, owh + 128))
    up_cut = cut[:, left + owh + 128 :]
    qo = exchange(jnp.concatenate([o_cut, q_cut], -1).transpose(1, 0, 2), "y")
    qo = qo.reshape(dprows, owh + 128 + 3 * hw)
    down_pieces = ring_gather(w_down, "x")
    span_y = iy.astype(jnp.int32).reshape(1)

    qo_z = ring_gather(qo, "z")
    up_z = ring_gather(up_cut, "z")
    tok_y = ring_gather(after(tok, *[qo]), "y")
    tok_all = []
    for item in tok_y:
        item = item if not tok_all else after(item, *qo_z)
        tok_all.append(item)
        tok_all.append(shift(item, "c"))
    qo_w, up_w, down_w = [], [], []
    up_at, down_at = [], []
    for step, item in enumerate(qo_z):
        for far, piece in enumerate(ring_gather(item, "x")):
            qo_w.append(piece)
            up_at.append(back("z", step) * nx + back("x", far))
    up_use = [after(up_z[0], *[qo])] + [after(item, *middle(qo_z)) for item in up_z[1:]]
    up_use[half] = after(up_use[half], *[qo_z[half]])
    up_y = []
    for item in up_use:
        pieces = ring_gather(item, "y")
        pieces = pieces[:1] + [after(piece, *qo_w) for piece in pieces[1:]]
        up_y.append(in_order(pieces, "y").reshape(dprows, ffh))
        up_w += ring_gather(up_y[-1], "x")
    down_pieces = [down_pieces[0]] + [after(item, *qo_z) for item in down_pieces[1:]]
    down_z = ring_gather(in_order(down_pieces, "x").reshape(nx * ffrows, width), "z")
    for step, item in enumerate(down_z):
        for far, piece in enumerate(ring_gather(item, "y")):
            down_w.append(piece)
            down_at.append(back("z", step) * ny + back("y", far))
    up_at = jnp.stack(up_at).astype(jnp.int32)
    down_at = jnp.stack(down_at).astype(jnp.int32)
    q_w, o_w, q_off = qo_w, qo_w, owh + 128
    if hw % 128:
        q_w, o_w, q_off = [p[:, owh + 128 :] for p in qo_w], [p[:, : owh + 128] for p in qo_w], 0
    nqo, nup, ndown = len(qo_w), len(up_w), len(down_w)
    up_w, down_w, q_back, o_back = (
        [pltpu.with_memory_space_constraint(piece, pltpu.HBM) for piece in pieces]
        for pieces in (up_w, down_w, q_w, o_w)
    )

    order = after(block_order, *middle(qo_z))[0].reshape(ny, nc)
    places = []
    for sy in range(ny):
        for sc in range(nc):
            places.append(take(take(order, back("y", sy)), back("c", sc)))
    places = jnp.stack(places)
    ranks = jnp.arange(spans, dtype=jnp.int32)
    sorted_at = jnp.sum(jnp.where(places[None, :] == ranks[:, None], ranks[None, :], 0), -1)
    offsets = jnp.arange(rows_here, dtype=jnp.int32)
    positions = (places[:, None] * rows_here + offsets[None, :]).reshape(length)
    lane = jnp.arange(lanes, dtype=jnp.int32)
    frequency = jnp.exp((lane % (HD // 2)).astype(F32) * (-2.0 * math.log(10000.0) / HD))
    angles = positions.astype(F32)[:, None] * frequency[None, :]
    cos_lanes = after(jnp.cos(angles))
    sin_lanes = jnp.sin(angles) * jnp.where(lane % HD < HD // 2, -1.0, 1.0)

    a1, qkv, norms = call(
        functools.partial(input_kernel, nqo, spans, lanes, q_off, owh),
        (shaped((length, width), BF16), shaped((length, 3 * hw), BF16), shaped((8, width), F32)),
        [IN_SMEM] + [IN_VMEM] * (2 + spans) + [ANYWHERE] * (2 * nqo),
        [pltpu.VMEM((width, 3 * hw), BF16), pltpu.VMEM((width, 128), BF16), sems(2 * nqo)],
    )(up_at, cos_lanes, sin_lanes, *tok_all, *q_w, *o_w)
    qkv_now = after(qkv, *middle(down_z))
    attn, lse = call(
        functools.partial(attend_kernel, spans, lanes),
        (shaped((length, hw), BF16), shaped((length, 128), F32)),
        [IN_SMEM, IN_VMEM],
    )(sorted_at, qkv_now)

    attn_now = after(attn, *(up_y[half : half + 1] + down_w[:ny]))
    sent = attn_now.reshape(ny, nc, rows_here, hw)
    o_near = [sent[0]] + [shift(sent[sy], "y", ny - sy) for sy in range(1, ny)]
    o_far = [shift(item, "c") for item in o_near]
    o_near[0] = after(o_near[0], *([down_z[half]] + up_w[: 2 * nx] + up_w[-nx:] + down_w[ny : 2 * ny]))
    r_keep, r_send, o_chip = call(
        functools.partial(out_kernel, nqo, ny),
        (shaped((rows_here, owh), F32), shaped((rows_here, owh), F32), shaped((crow, width), BF16)),
        [IN_SMEM, IN_SMEM] + [IN_VMEM] * (2 * ny) + [IN_SMEM] + [ANYWHERE] * nqo,
        [pltpu.VMEM((width, owh), BF16), sems(nqo)],
    )(up_at, core, *o_near, *o_far, span_y, *o_w)
    r_send = after(r_send, *(down_w[ny : 2 * ny] + down_w[-ny:] + up_w[half * nx : half * nx + nx]))
    r_got = shift(r_send, "c")
    h, a2 = call(
        middle_kernel,
        (shaped((rows_here, width), F32), shaped((rows_here, width), BF16)),
        [IN_SMEM] + [IN_VMEM] * 4,
        [pltpu.VMEM((rows_here, width), F32)],
    )(core, r_keep, r_got, tok, norms)
    a2 = after(a2)
    a2_got = shift(a2, "c")
    m_keep, m_send, u, slope = call(
        functools.partial(mlp_kernel, nup, ndown),
        (
            shaped((rows_here, width), F32),
            shaped((rows_here, width), BF16),
            shaped((crow, ffh), BF16),
            shaped((crow, ffh), BF16),
        ),
        [IN_SMEM, IN_SMEM, IN_VMEM, IN_VMEM] + [IN_HBM] * (nup + ndown),
        [pltpu.VMEM((width, ffh), BF16), pltpu.VMEM((ffh, width), BF16), sems(nup + ndown)],
        vmem=26,
    )(up_at, down_at, a2, a2_got, *up_w, *down_w)
    m_got = shift(m_send, "c")
    match = group_ids[:, None] == jnp.arange(group_weight.shape[0], dtype=jnp.int32)[None, :]
    scale = jnp.sum(jnp.where(match, group_weight[None, :], 0.0)).reshape(1)
    out_tokens, dm, grads_3 = call(
        top_kernel,
        (shaped((rows_here, width), BF16), shaped((rows_here, width), BF16), shaped((2, width), F32)),
        [IN_SMEM] + [IN_VMEM] * 5,
    )(scale, m_keep, m_got, h, cot, norms)

    dm_got = shift(dm, "c")
    down_own, down_got = [None] * nz, [None] * nz
    up_own, up_got = [None] * nz, [None] * nz
    early, late = late_last(nz)[:2], late_last(nz)[2:]

    def down_block(step, right, *when):
        blocks = grads(u, [right, dm_got], down_at, nx * ffrows, range(step * ny, step * ny + ny))
        down_own[step] = blocks[0]
        down_got[step] = [shift(after(blocks[far], *when), "y", ny - far) for far in range(1, ny)]

    def up_block(step, right):
        blocks = grads(a2_all, [right], up_at, dprows, range(step * nx, step * nx + nx))
        up_own[step] = blocks[0]
        up_got[step] = [shift(blocks[far], "x", nx - far) for far in range(1, nx)]

    right = dm
    for step in early:
        down_block(step, right, right)
        right = after(dm, down_own[step])
    blocks = [down_own[early[-1]]]
    dm = after(dm, blocks[0])
    da_keep, da_send, dz = call(
        functools.partial(mlp_back_kernel, nup, ndown),
        (
            shaped((rows_here, width), F32),
            shaped((rows_here, width), BF16),
            shaped((crow, ffh), BF16),
        ),
        [IN_SMEM, IN_SMEM, IN_VMEM, IN_VMEM, IN_VMEM] + [IN_HBM] * (nup + ndown),
        [pltpu.VMEM((width, ffh), BF16), pltpu.VMEM((ffh, width), BF16), sems(nup + ndown)],
        vmem=26,
    )(up_at, down_at, dm, dm_got, slope, *up_w, *down_w)
    da_got = shift(da_send, "c")
    a2_all = jnp.concatenate([a2, a2_got], 0)
    right = after(dz)
    for step in early + late:
        up_block(step, right)
        right = after(dz, up_own[step])
    blocks = [up_own[early[-1]]]
    da_keep = after(da_keep, blocks[0], *down_got[early[0]])
    dh, dr, dr_send, grads_21 = call(
        between_kernel,
        (
            shaped((rows_here, width), F32),
            shaped((rows_here, owh), BF16),
            shaped((rows_here, owh), BF16),
            shaped((4, width), F32),
        ),
        [IN_SMEM, IN_SMEM] + [IN_VMEM] * 7,
        [pltpu.VMEM((rows_here, width), F32), pltpu.VMEM((rows_here, width), BF16)],
    )(core, scale, da_keep, da_got, h, r_keep, r_got, cot, norms)
    dr_send = after(dr_send, *down_got[early[1]])
    dr_got = shift(dr_send, "c")
    do_keep, do_send = call(
        functools.partial(out_back_kernel, nqo, ny),
        (shaped((ny, crow, hw), F32), shaped((ny, crow, hw), BF16)),
        [IN_SMEM, IN_SMEM, IN_VMEM, IN_VMEM] + [ANYWHERE] * nqo,
        [pltpu.VMEM((width, owh), BF16), sems(nqo)],
    )(up_at, core, dr, dr_got, *o_back)
    do_got = shift(do_send, "c")
    do_got = jnp.concatenate([do_got[:, rows_here:], do_got[:, :rows_here]], 1)
    do = (do_keep + do_got.astype(F32)).astype(BF16)
    parts = []
    for sy in range(ny):
        item = take(do, lax.rem(iy + sy, ny))
        parts.append(item if sy == 0 else shift(item, "y", sy))
    do_all = jnp.concatenate(parts, 0)
    down_y, up_x = [None] * nz, [None] * nz
    right = after(dm, do)
    down_block(late[0], right, do_all)
    for step in late[1:]:
        down_block(step, after(dm, do), do_all)
    for step in early:
        down_y[step] = add_parts(down_own[step], down_got[step], do)
        up_x[step] = add_parts(up_own[step], up_got[step], do_all)
    out_own, out_send = stacked_grads(o_chip, [dr, dr_got], up_at, dprows)
    out_got = shift(out_send, "x")

    down_first = ring_first(down_y, "z")
    sums = [None] * nz
    for step in early:
        own_y, got_y = send_parts(up_x[step].reshape(ny, nc * wrows, ffh), "y")
        sums[step] = add_parts(own_y, got_y, do_all)
    up_first = ring_first(sums, "z")
    do_all = after(do_all, *[t for t in down_y + up_x + down_own + up_own if t is not None])
    dqkv = call(
        functools.partial(attend_back_kernel, spans, lanes),
        shaped((length, 3 * hw), BF16),
        [IN_SMEM] + [IN_VMEM] * 6,
        [pltpu.VMEM((length, lanes), F32)] * 2
        + [pltpu.VMEM((length, 128), F32), pltpu.VMEM((2, 8, length), F32)],
        vmem=20,
    )(sorted_at, qkv, attn, do_all, lse, cos_lanes, sin_lanes)
    dqkv = after(dqkv, *([t for step in late for t in up_got[step]] + [sums[step] for step in early]))
    qkv_own, qkv_send = stacked_grads(a1, [dqkv], up_at, dprows)
    qkv_got = shift(qkv_send, "x")
    da1_keep, da1_send = call(
        functools.partial(input_back_kernel, nqo, q_off),
        (shaped((ny, rows_here, width), F32), shaped((ny, rows_here, width), BF16)),
        [IN_SMEM, IN_VMEM] + [ANYWHERE] * nqo,
        [pltpu.VMEM((width, 3 * hw), BF16), sems(nqo)],
    )(up_at, after(dqkv, qkv_own, *down_first), *q_back)
    da1_got = shift(da1_send, "c")
    sent_on = [(da1_keep[sy] + da1_got[sy].astype(F32)).astype(BF16) for sy in range(1, ny)]
    arrived = [shift(item, "y", ny - sy) for sy, item in enumerate(sent_on, 1)]
    da1_keep = after(da1_keep, *(up_first + down_first + [t for step in late for t in down_got[step]]))
    grad_tokens, grads_0 = call(
        bottom_kernel,
        (shaped((rows_here, width), BF16), shaped((2, width), F32)),
        [IN_VMEM] * (5 + len(arrived)),
    )(tok, dh, norms, da1_keep[0], da1_got[0], *arrived)
    grad_tokens = grad_tokens.reshape(tokens.shape)
    out_tokens = out_tokens.reshape(tokens.shape)

    for step in range(nz):
        if down_y[step] is None:
            down_y[step] = add_parts(down_own[step], down_got[step], sent_on[0])
    down = ring_rest(down_y, down_first, "z").astype(BF16)
    down = scatter_sum(down.reshape(nx, ffrows, width), "x")
    for step in late:
        part = add_parts(up_own[step], up_got[step], qkv_own)
        own_y, got_y = send_parts(part.reshape(ny, nc * wrows, ffh), "y")
        sums[step] = add_parts(own_y, got_y, qkv_got)
    up = ring_rest(sums, up_first, "z").reshape(nc, wrows, ffh)
    up_got = shift(take(up, 1 - ic), "c")
    if aligned:
        up = call(
            functools.partial(up_kernel, (nz, nx, ny, ffrows)),
            shaped((wrows, ff), F32),
            [IN_SMEM] + [IN_VMEM] * 2,
        )(core, take(up, ic), up_got)
    else:
        up = pair(take(up, ic), up_got, ic)
        up = up.reshape(nc, wrows, nz, ny, nx, ffrows).transpose(1, 2, 4, 3, 0, 5).reshape(wrows, ff)

    out_x = add_parts(out_own, [out_got], qkv_got)
    qkv_x = (qkv_own.astype(F32) + qkv_got.astype(F32)).astype(BF16)
    both = jnp.concatenate([out_x, qkv_x], -1)
    both = ring_scatter([both[step] for step in range(nz)], "z").astype(BF16)
    both = after(both)
    out, qkv_g = both[:, :owh], both[:, owh:]
    out = scatter_sum(out.reshape(ny, nc * wrows, owh), "y").reshape(nc, wrows, owh)
    out_got = shift(take(out, 1 - ic), "c")
    qkv_g = exchange(qkv_g.reshape(ny, nc * wrows, 3 * hw), "y")
    qkv_g = qkv_g.reshape(ny, nc, wrows, 3 * hw)
    qkv_got = shift(take(qkv_g, 1 - ic, 1), "c")
    if aligned:
        qkv_g, out = call(
            qkv_out_kernel,
            (shaped((wrows, 3 * width), F32), shaped((wrows, width), F32)),
            [IN_SMEM] + [IN_VMEM] * 4,
        )(core, take(qkv_g, ic, 1), qkv_got, take(out, ic), out_got)
    else:
        out = pair(take(out, ic), out_got, ic).transpose(1, 0, 2).reshape(wrows, width)
        qkv_g = pair(take(qkv_g, ic, 1), qkv_got, ic)
        qkv_g = qkv_g.reshape(nc, ny, wrows, 3, hw).transpose(2, 3, 1, 0, 4)
        qkv_g = qkv_g.reshape(wrows, 3 * width).astype(F32)

    norm_sums = jnp.concatenate(
        [
            grads_0[0:1],
            grads_21[2:3],
            grads_21[0:1],
            grads_3[0:1],
            grads_0[1:2],
            grads_21[3:4],
            grads_21[1:2],
            grads_3[1:2],
        ],
        0,
    )
    norm_sums = after(norm_sums)
    for axis in "cyxz":
        norm_sums = all_sum(norm_sums, axis)
    place = ((iz * nx + ix) * ny + iy) * nc + ic
    norm_sums = lax.dynamic_slice(norm_sums, (0, place * wrows), (8, wrows))
    return (out_tokens, grad_tokens, qkv_g, out, up, down, norm_sums[:4], norm_sums[4:])


def solution(mesh):
    fine = Mesh(
        mesh.devices.reshape(mesh.shape["dp"] // 2, 2, mesh.shape["blk"] // 2, 2),
        ("z", "x", "y", "c"),
    )
    dp, blk, every = ("z", "x"), ("y", "c"), ("z", "x", "y", "c")
    return jax.shard_map(
        on_device,
        mesh=fine,
        in_specs=(
            P(blk, dp, None),
            P(blk, dp, None),
            P(dp),
            P(),
            P(dp, None),
            P(every, None),
            P(every, None),
            P(every, None),
            P(every, None),
            P(None, every),
            P(None, every),
        ),
        out_specs=(
            P(blk, dp, None),
            P(blk, dp, None),
            P(every, None),
            P(every, None),
            P(every, None),
            P(every, None),
            P(None, every),
            P(None, every),
        ),
        check_vma=False,
    )
```
